32 devices in a mesh: row: 4 (over y, x), col: 8 (over z, core).
Axes of the slice: x: 2, y: 2, z: 4, core: 2. Of those that a mesh axis runs over, the one named last changes fastest.
Arguments:
- block_input: float32 [2, 8192, 640], P(None, ('row', 'col')), may hold values from -6 to 6
- output_grad: float32 [2, 8192, 640], P(None, ('row', 'col')), may hold values from -6 to 6
- sequence_ids: int32 [2, 8192], P(None, ('row', 'col')), may hold values from 0 to 7, as said below
- attn_weights: float32 [640, 2560], P(None, ('row', 'col')), may hold values from -0.29646353 to 0.29646353
- attn_momentum: float32 [640, 2560], P(None, ('row', 'col')), may hold values from -422.4 to 422.4
- attn_average: float32 [640, 2560], P(None, ('row', 'col')), may hold values from -0.29646353 to 0.29646353
- norm_params: float32 [2560], P(('row', 'col')), may hold values from -0.6 to 1.3
- norm_momentum: float32 [2560], P(('row', 'col')), may hold values from -806.4 to 806.4
- norm_average: float32 [2560], P(('row', 'col')), may hold values from -0.6 to 1.3
- ffn_weights: float32 [2, 640, 5120], P(None, 'row', 'col'), may hold values from -0.118585412 to 0.118585412
- ffn_momentum: float32 [2, 640, 5120], P(None, 'row', 'col'), may hold values from -249.6 to 249.6
- ffn_average: float32 [2, 640, 5120], P(None, 'row', 'col'), may hold values from -0.118585412 to 0.118585412
Outputs:
- block_output: float32 [2, 8192, 640], P(None, ('row', 'col'))
- input_grad: float32 [2, 8192, 640], P(None, ('row', 'col'))
- attn_grad: float32 [640, 2560], P(None, ('row', 'col'))
- attn_momentum_new: float32 [640, 2560], P(None, ('row', 'col'))
- attn_weights_new: float32 [640, 2560], P(None, ('row', 'col'))
- attn_average_new: float32 [640, 2560], P(None, ('row', 'col'))
- attn_copy: bfloat16 [640, 2560], P(None, ('row', 'col'))
- norm_grad: float32 [2560], P(('row', 'col'))
- norm_momentum_new: float32 [2560], P(('row', 'col'))
- norm_params_new: float32 [2560], P(('row', 'col'))
- norm_average_new: float32 [2560], P(('row', 'col'))
- norm_copy: bfloat16 [2560], P(('row', 'col'))
- ffn_grad: float32 [2, 640, 5120], P(None, 'row', 'col')
- ffn_momentum_new: float32 [2, 640, 5120], P(None, 'row', 'col')
- ffn_weights_new: float32 [2, 640, 5120], P(None, 'row', 'col')
- ffn_average_new: float32 [2, 640, 5120], P(None, 'row', 'col')
- ffn_copy: bfloat16 [2, 640, 5120], P(None, 'row', 'col')
The draws below stay inside these ranges and needn't reach their ends.
Inputs may be any that keep to these rules, and one draw needn't show every extreme that they name: `sequence_ids`: within each aligned block of 256 tokens the numbers start at 0, never fall and step by one; a sequence (a run of equal numbers) holds 20 to 256 tokens; in each micro-batch one block holds a single sequence and another holds 8 sequences.
All inputs are finite; a program needn't handle non-finite values.
Results may differ from the reference program's by a relative error of at most 0.014.
The reference program's roundings to bfloat16 on the way count: a program that leaves them out, or rounds other values in their place, can miss the bound.
Values may be sent and summed in bfloat16 or wider, within the bound.
A program may use at most 128 MiB of HBM per device.

```python
import math
import jax
import jax.numpy as jnp
from jax import lax

D = 640
H = 20
HD = 32
FF = 5120
PACK = 256
MB = 2
TOKENS = 8192


def rough_values(key, shape):
    return jax.random.truncated_normal(key, -3.0, 3.0, shape, jnp.float32)


def block_scales(block_count, block_width, factors):
    block_index = jnp.arange(block_count * block_width) // block_width
    scales = jnp.zeros((block_count * block_width,), jnp.float32)
    for number, factor in enumerate(factors):
        scales = jnp.where(block_index == number, factor, scales)
    return scales


def attn_law(key, salt_value):
    scales = block_scales(4, D, (1.3, 1.3, 2.5, 2.5)) / math.sqrt(D)
    return rough_values(jax.random.fold_in(key, salt_value), (D, 4 * D)) * scales[None, :]


def norm_law(key, salt_value):
    raw_values = rough_values(jax.random.fold_in(key, salt_value), (4 * D,))
    gain_mask = block_scales(4, D, (1.0, 0.0, 1.0, 0.0))
    return gain_mask * (1.0 + 0.1 * raw_values) + (1.0 - gain_mask) * 0.2 * raw_values


def ffn_law(key, salt_value):
    scales = jnp.array([1.0 / math.sqrt(D), 1.0 / math.sqrt(FF)], jnp.float32)
    return rough_values(jax.random.fold_in(key, salt_value), (2, D, FF)) * scales[:, None, None]


def draw_sequence_ids(key, part):
    base_key = jax.random.fold_in(key, 3)
    key_cut, key_lone, key_full, key_jitter = jax.random.split(base_key, 4)
    blocks = TOKENS // PACK
    unit_count = PACK // 32
    cut_flag = jax.random.randint(key_cut, (MB, blocks, unit_count), 0, 2)
    lone_block = jax.random.randint(key_lone, (MB, 1, 1), 0, blocks)
    full_block = (lone_block + 1 + jax.random.randint(key_full, (MB, 1, 1), 0, blocks - 1)) % blocks
    unit_ids = jnp.arange(unit_count)[None, None, :]
    block_ids = jnp.arange(blocks)[None, :, None]
    cut_flag = jnp.where(block_ids == full_block, 1, cut_flag)
    cut_flag = jnp.where(unit_ids == 0, 1, jnp.where(block_ids == lone_block, 0, cut_flag))
    jitter = jax.random.randint(key_jitter, (MB, blocks, unit_count), -6, 7)
    start_at = jnp.where(unit_ids == 0, 0, unit_ids * 32 + jitter)
    positions = jnp.arange(PACK)[None, None, :, None]
    hits = (positions == start_at[:, :, None, :]) & (cut_flag[:, :, None, :] == 1)
    starts = jnp.sum(jnp.where(hits, 1, 0), axis=-1)
    local_ids = jnp.cumsum(starts, axis=-1) - 1
    return local_ids.reshape(MB, TOKENS).astype(jnp.int32)


def draw_attn_weights(key, part):
    return attn_law(key, 11)


def draw_attn_average(key, part):
    return attn_law(key, 12)


def draw_attn_momentum(key, part):
    token_root = math.sqrt(MB * TOKENS)
    scales = block_scales(4, D, (1.1, 1.1, 0.45, 0.45)) * token_root
    return rough_values(jax.random.fold_in(key, 13), (D, 4 * D)) * scales[None, :]


def draw_norm_params(key, part):
    return norm_law(key, 21)


def draw_norm_average(key, part):
    return norm_law(key, 22)


def draw_norm_momentum(key, part):
    token_root = math.sqrt(MB * TOKENS)
    scales = block_scales(4, D, (2.1, 2.1, 0.6, 0.6)) * token_root
    return rough_values(jax.random.fold_in(key, 23), (4 * D,)) * scales


def draw_ffn_weights(key, part):
    return ffn_law(key, 31)


def draw_ffn_average(key, part):
    return ffn_law(key, 32)


def draw_ffn_momentum(key, part):
    token_root = math.sqrt(MB * TOKENS)
    scales = jnp.array([0.2, 0.65], jnp.float32) * token_root
    return rough_values(jax.random.fold_in(key, 33), (2, D, FF)) * scales[:, None, None]


def block_scale(key, dims, cuts, low, largest):
    level = 1.0
    for axis_at, blocks in cuts:
        draws = jax.random.uniform(jax.random.fold_in(jax.random.fold_in(key, 6), axis_at), (blocks,), jnp.float32, low / len(cuts), largest / len(cuts))
        level = level * jnp.repeat(jnp.exp(draws), dims[axis_at] // blocks).reshape((-1,) + (1,) * (len(dims) - 1 - axis_at))
    return level


def bell_draw(own_key, extent, scale, most, cuts=(), dtype=jnp.bfloat16):
    entries = jax.random.normal(own_key, extent, jnp.float32) * scale
    if len(cuts) > 0:
        entries = block_scale(own_key, extent, cuts, -0.22, 0.18) * entries
    return jnp.clip(entries, min=-most, max=most).astype(dtype)


def setup_inputs(seed: int = 0) -> dict:
    arg_keys = jax.random.split(jax.random.key(seed), 13)
    return {
        "block_input": bell_draw(arg_keys[0], (MB, TOKENS, D), 1.0, 6.0, ((1, 32),), jnp.float32),
        "output_grad": bell_draw(arg_keys[1], (MB, TOKENS, D), 1.0, 6.0, ((1, 32),), jnp.float32),
        "sequence_ids": draw_sequence_ids(jax.random.fold_in(arg_keys[12], 71), 0),
        "attn_weights": draw_attn_weights(jax.random.fold_in(arg_keys[12], 71), 0),
        "attn_momentum": draw_attn_momentum(jax.random.fold_in(arg_keys[12], 71), 0),
        "attn_average": draw_attn_average(jax.random.fold_in(arg_keys[12], 71), 0),
        "norm_params": draw_norm_params(jax.random.fold_in(arg_keys[12], 71), 0),
        "norm_momentum": draw_norm_momentum(jax.random.fold_in(arg_keys[12], 71), 0),
        "norm_average": draw_norm_average(jax.random.fold_in(arg_keys[12], 71), 0),
        "ffn_weights": draw_ffn_weights(jax.random.fold_in(arg_keys[12], 71), 0),
        "ffn_momentum": draw_ffn_momentum(jax.random.fold_in(arg_keys[12], 71), 0),
        "ffn_average": draw_ffn_average(jax.random.fold_in(arg_keys[12], 71), 0),
    }


@jax.custom_vjp
def low(v):
    return lax.optimization_barrier(v.astype(jnp.bfloat16)).astype(jnp.float32)

@jax.custom_vjp
def low_back(v):
    return v

def low_keep(v):
    return (low(v), None)

def low_pass(kept, grad):
    return (grad,)

def back_keep(v):
    return (v, None)

def back_low(kept, grad):
    return (low(grad),)
low.defvjp(low_keep, low_pass)
low_back.defvjp(back_keep, back_low)
HIGHEST = lax.Precision.HIGHEST
EPSILON = 1e-05
MOMENT_DECAY = 0.9
AVERAGE_DECAY = 0.85
RATE_SCALE = 0.06
MASKED = -1e+30

def layer_norm(values, gain, shift):
    center = values - lax.optimization_barrier(jnp.mean(values, axis=-1, keepdims=True))
    spread = lax.optimization_barrier(jnp.mean(center * center, axis=-1, keepdims=True))
    return center * lax.rsqrt(spread + EPSILON) * gain + shift

def pack_attention(qkv_pack, ids_pack):
    length = qkv_pack.shape[0]
    split_heads = qkv_pack.reshape(length, 3, H, HD)
    queries = split_heads[:, 0]
    keys_part = split_heads[:, 1]
    values = split_heads[:, 2]
    scores = jnp.einsum('qhe,khe->hqk', queries, keys_part, precision=HIGHEST) * HD ** (-0.5)
    scores = low_back(scores)
    same_seq = ids_pack[:, None] == ids_pack[None, :]
    scores = jnp.where(same_seq[None], scores, MASKED)
    row_max = lax.optimization_barrier(jnp.max(scores, axis=-1, keepdims=True))
    exponent = jnp.exp(scores - row_max)
    attn_probs = low(exponent / lax.optimization_barrier(jnp.sum(exponent, axis=-1, keepdims=True)))
    mixed_rows = jnp.einsum('hqk,khe->qhe', attn_probs, values, precision=HIGHEST)
    return mixed_rows.reshape(length, H * HD)

def ffn_block(rows_low, ffn_low):
    up_proj = low_back(jnp.dot(rows_low, ffn_low[0], precision=HIGHEST))
    activation = low(jax.nn.gelu(up_proj, approximate=False))
    return low_back(lax.dot_general(activation, ffn_low[1], (((1,), (1,)), ((), ())), precision=HIGHEST))

def forward(inputs, attn_full, norm_full, ffn_full, ids_row):
    attn_low = low(attn_full)
    norm_low = low(norm_full)
    ffn_low = low(ffn_full)
    normed = low(layer_norm(inputs, norm_low[:D], norm_low[D:2 * D]))
    qkv_rows = low(low_back(jnp.dot(normed, attn_low[:, :3 * D], precision=HIGHEST)))
    pack_count = TOKENS // PACK
    attended = lax.map(lambda pack_pair: jax.checkpoint(pack_attention)(pack_pair[0], pack_pair[1]), (qkv_rows.reshape(pack_count, PACK, 3 * D), ids_row.reshape(pack_count, PACK)))
    attended = low(low_back(attended.reshape(TOKENS, D)))
    hidden_in = inputs + low_back(jnp.dot(attended, attn_low[:, 3 * D:], precision=HIGHEST))
    normed_two = low(layer_norm(hidden_in, norm_low[2 * D:3 * D], norm_low[3 * D:]))
    block_rows = math.gcd(TOKENS, 4096)
    ffn_out = lax.map(lambda rows_low: jax.checkpoint(ffn_block)(rows_low, ffn_low), normed_two.reshape(TOKENS // block_rows, block_rows, D))
    return hidden_in + ffn_out.reshape(TOKENS, D)

def sgd_update(weights_old, moment, average, grad_sum, step_rate):
    moment_new = MOMENT_DECAY * moment + grad_sum
    weights_new = weights_old - step_rate * (grad_sum + MOMENT_DECAY * moment_new)
    average_new = AVERAGE_DECAY * average + (1.0 - AVERAGE_DECAY) * weights_new
    return (moment_new, weights_new, average_new, weights_new.astype(jnp.bfloat16))

def reference(block_input, output_grad, sequence_ids, attn_weights, attn_momentum, attn_average, norm_params, norm_momentum, norm_average, ffn_weights, ffn_momentum, ffn_average):
    attn_sum = jnp.zeros(attn_weights.shape, jnp.float32)
    norm_sum = jnp.zeros(norm_params.shape, jnp.float32)
    ffn_sum = jnp.zeros(ffn_weights.shape, jnp.float32)
    outputs_all = []
    grads_all = []
    for micro_step in range(MB):
        ids_row = sequence_ids[micro_step]

        def micro_forward(inputs, attn_full, norm_full, ffn_full):
            return forward(inputs, attn_full, norm_full, ffn_full, ids_row)
        result, pullback = jax.vjp(micro_forward, block_input[micro_step], attn_weights, norm_params, ffn_weights)
        grad_in, attn_part, norm_part, ffn_part = pullback(output_grad[micro_step])
        outputs_all.append(result)
        grads_all.append(grad_in)
        attn_sum = attn_sum + attn_part
        norm_sum = norm_sum + norm_part
        ffn_sum = ffn_sum + ffn_part
    step_rate = RATE_SCALE * (MB * TOKENS) ** (-0.5)
    attn_moment_new, attn_new, attn_avg_new, attn_copy = sgd_update(attn_weights, attn_momentum, attn_average, attn_sum, step_rate)
    norm_moment_new, norm_new, norm_avg_new, norm_copy = sgd_update(norm_params, norm_momentum, norm_average, norm_sum, step_rate)
    ffn_moment_new, ffn_new, ffn_avg_new, ffn_copy = sgd_update(ffn_weights, ffn_momentum, ffn_average, ffn_sum, step_rate)
    return (jnp.stack(outputs_all), jnp.stack(grads_all), attn_sum, attn_moment_new, attn_new, attn_avg_new, attn_copy, norm_sum, norm_moment_new, norm_new, norm_avg_new, norm_copy, ffn_sum, ffn_moment_new, ffn_new, ffn_avg_new, ffn_copy)
```

```python
import functools
import math

import jax
import jax.numpy as jnp
from jax import lax
from jax.experimental import pallas as pl
from jax.experimental.pallas import tpu as pltpu
from jax.sharding import PartitionSpec as P

D = 640
H = 20
HD = 32
MB = 2


EPSILON = 1e-05
MOMENT_DECAY = 0.9
AVERAGE_DECAY = 0.85
RATE_SCALE = 0.06
MASKED = -1e30


def layer_norm(values, gain, shift):
    center = values - jnp.mean(values, axis=-1, keepdims=True)
    spread = jnp.mean(center * center, axis=-1, keepdims=True)
    return center * lax.rsqrt(spread + EPSILON) * gain + shift


def gelu_exact(values):
    return jax.nn.gelu(values, approximate=False)


def matmul(left_side, right_side):
    return jnp.dot(left_side, right_side, preferred_element_type=jnp.float32)


def contract_rows(left_side, right_side):
    return lax.dot_general(
        left_side, right_side, (((0,), (0,)), ((), ())), preferred_element_type=jnp.float32
    )


def contract_cols(left_side, right_side):
    return lax.dot_general(
        left_side, right_side, (((1,), (1,)), ((), ())), preferred_element_type=jnp.float32
    )


def head_slices(qkv_low, first_col, head_group):
    length = qkv_low.shape[0]
    group_width = head_group * HD
    queries = lax.dynamic_slice_in_dim(qkv_low, first_col, group_width, 1).reshape(
        length, head_group, HD
    )
    keys_part = lax.dynamic_slice_in_dim(qkv_low, D + first_col, group_width, 1).reshape(
        length, head_group, HD
    )
    values = lax.dynamic_slice_in_dim(qkv_low, 2 * D + first_col, group_width, 1).reshape(
        length, head_group, HD
    )
    return (queries, keys_part, values)


def masked_scores(queries, keys_part, same_seq):
    scores = jnp.einsum(
        "qhe,khe->hqk", queries, keys_part, preferred_element_type=jnp.float32
    ) * HD ** (-0.5)
    return jnp.where(same_seq[None], scores, MASKED)


def attend_forward(qkv_low, same_seq):
    length = qkv_low.shape[0]
    head_group = math.gcd(H, 4)
    group_width = head_group * HD

    def one_group(group_index, state_all):
        mixed_all, maxima, totals = state_all
        first_col = group_index * group_width
        queries, keys_part, values = head_slices(qkv_low, first_col, head_group)
        scores = masked_scores(queries, keys_part, same_seq)
        row_max = jnp.max(scores, axis=-1, keepdims=True)
        exponent = jnp.exp(scores - row_max)
        row_total = jnp.sum(exponent, axis=-1, keepdims=True)
        attn_probs = (exponent / row_total).astype(jnp.bfloat16)
        mixed_rows = jnp.einsum(
            "hqk,khe->qhe", attn_probs, values, preferred_element_type=jnp.float32
        )
        mixed_all = lax.dynamic_update_slice_in_dim(
            mixed_all, mixed_rows.reshape(length, group_width), first_col, 1
        )
        maxima = lax.dynamic_update_slice_in_dim(
            maxima, row_max[:, :, 0], group_index * head_group, 0
        )
        totals = lax.dynamic_update_slice_in_dim(
            totals, row_total[:, :, 0], group_index * head_group, 0
        )
        return (mixed_all, maxima, totals)

    initial = (
        jnp.zeros((length, D), jnp.float32),
        jnp.zeros((H, length), jnp.float32),
        jnp.zeros((H, length), jnp.float32),
    )
    return lax.fori_loop(0, H // head_group, one_group, initial)


def attend_backward(qkv_low, same_seq, maxima, totals, grad_mixed):
    length = qkv_low.shape[0]
    head_group = math.gcd(H, 4)
    group_width = head_group * HD

    def one_group(group_index, grad_qkv):
        first_col = group_index * group_width
        queries, keys_part, values = head_slices(qkv_low, first_col, head_group)
        grad_part = lax.dynamic_slice_in_dim(grad_mixed, first_col, group_width, 1).reshape(
            length, head_group, HD
        )
        scores = masked_scores(queries, keys_part, same_seq)
        row_max = lax.dynamic_slice_in_dim(maxima, group_index * head_group, head_group, 0)[
            :, :, None
        ]
        row_total = lax.dynamic_slice_in_dim(totals, group_index * head_group, head_group, 0)[
            :, :, None
        ]
        attn_probs = jnp.exp(scores - row_max) / row_total
        grad_probs = jnp.einsum(
            "qhe,khe->hqk", grad_part, values, preferred_element_type=jnp.float32
        )
        grad_values = jnp.einsum(
            "hqk,qhe->khe",
            attn_probs.astype(jnp.bfloat16),
            grad_part,
            preferred_element_type=jnp.float32,
        )
        grad_scores = attn_probs * (
            grad_probs - jnp.sum(grad_probs * attn_probs, axis=-1, keepdims=True)
        )
        grad_scores = grad_scores.astype(jnp.bfloat16)
        grad_queries = jnp.einsum(
            "hqk,khe->qhe", grad_scores, keys_part, preferred_element_type=jnp.float32
        ) * HD ** (-0.5)
        grad_keys = jnp.einsum(
            "hqk,qhe->khe", grad_scores, queries, preferred_element_type=jnp.float32
        ) * HD ** (-0.5)
        for offset, grad_piece in ((0, grad_queries), (D, grad_keys), (2 * D, grad_values)):
            grad_qkv = lax.dynamic_update_slice_in_dim(
                grad_qkv, grad_piece.reshape(length, group_width), offset + first_col, 1
            )
        return grad_qkv

    return lax.fori_loop(0, H // head_group, one_group, jnp.zeros((length, 3 * D), jnp.float32))


def sgd_update(weights_old, moment, average, grad_sum, step_rate):
    moment_new = MOMENT_DECAY * moment + grad_sum
    weights_new = weights_old - step_rate * (grad_sum + MOMENT_DECAY * moment_new)
    average_new = AVERAGE_DECAY * average + (1.0 - AVERAGE_DECAY) * weights_new
    return (moment_new, weights_new, average_new, weights_new.astype(jnp.bfloat16))


def local_general(
    block_input,
    output_grad,
    sequence_ids,
    attn_weights,
    attn_momentum,
    attn_average,
    norm_params,
    norm_momentum,
    norm_average,
    ffn_weights,
    ffn_momentum,
    ffn_average,
):
    attn_full, norm_full = (
        lax.all_gather(attn_weights.astype(jnp.bfloat16), ("row", "col"), axis=1, tiled=True),
        lax.all_gather(norm_params.astype(jnp.bfloat16), ("row", "col"), axis=0, tiled=True),
    )
    norm_values = norm_full.astype(jnp.float32)
    gain_one = norm_values[:D]
    shift_one = norm_values[D : 2 * D]
    gain_two = norm_values[2 * D : 3 * D]
    shift_two = norm_values[3 * D :]
    qkv_weights = attn_full[:, : 3 * D]
    out_weights = attn_full[:, 3 * D :]
    ffn_rows = lax.all_gather(ffn_weights.astype(jnp.bfloat16), "row", axis=1, tiled=True)
    col_width = ffn_weights.shape[2]
    length = block_input.shape[1]
    attn_acc = jnp.zeros((D, 4 * D), jnp.float32)
    norm_acc = jnp.zeros((4 * D,), jnp.float32)
    ffn_acc = jnp.zeros((2, D, col_width), jnp.float32)
    outputs_all = []
    grads_all = []
    for micro_step in range(MB):
        inputs = block_input[micro_step]
        ids_row = sequence_ids[micro_step]
        same_seq = ids_row[:, None] == ids_row[None, :]
        normed, pull_one = jax.vjp(layer_norm, inputs, gain_one, shift_one)
        normed_low = normed.astype(jnp.bfloat16)
        qkv_low = matmul(normed_low, qkv_weights).astype(jnp.bfloat16)
        mixed_all, maxima, totals = attend_forward(qkv_low, same_seq)
        mixed_low = mixed_all.astype(jnp.bfloat16)
        hidden_in = inputs + matmul(mixed_low, out_weights)
        normed_two, pull_two = jax.vjp(layer_norm, hidden_in, gain_two, shift_two)
        normed_two_low = normed_two.astype(jnp.bfloat16)
        grad_out = output_grad[micro_step]
        grad_out_low = grad_out.astype(jnp.bfloat16)
        normed_all = lax.all_gather(normed_two_low, "col", axis=0, tiled=True)
        up_proj = matmul(normed_all, ffn_rows[0])
        activation, pull_gelu = jax.vjp(gelu_exact, up_proj)
        activ_low = activation.astype(jnp.bfloat16)
        ffn_out = lax.psum_scatter(
            contract_cols(activ_low, ffn_rows[1]).astype(jnp.bfloat16),
            "col",
            scatter_dimension=0,
            tiled=True,
        ).astype(jnp.float32)
        grad_all = lax.all_gather(grad_out_low, "col", axis=0, tiled=True)
        grad_act = matmul(grad_all, ffn_rows[1])
        grad_up = pull_gelu(grad_act)[0].astype(jnp.bfloat16)
        grad_normed_two = lax.psum_scatter(
            contract_cols(grad_up, ffn_rows[0]).astype(jnp.bfloat16),
            "col",
            scatter_dimension=0,
            tiled=True,
        ).astype(jnp.float32)
        ffn_acc = ffn_acc + jnp.stack(
            [contract_rows(normed_all, grad_up), contract_rows(grad_all, activ_low)]
        )
        outputs_all.append(hidden_in + ffn_out)
        grad_ln_two, gain_two_grad, shift_two_grad = pull_two(grad_normed_two)
        grad_hidden = grad_out + grad_ln_two
        grad_branch_low = grad_hidden.astype(jnp.bfloat16)
        out_proj_grad = contract_rows(mixed_low, grad_branch_low)
        grad_mixed_low = contract_cols(grad_branch_low, out_weights).astype(jnp.bfloat16)
        grad_qkv_low = attend_backward(qkv_low, same_seq, maxima, totals, grad_mixed_low).astype(
            jnp.bfloat16
        )
        qkv_grad = contract_rows(normed_low, grad_qkv_low)
        grad_normed = contract_cols(grad_qkv_low, qkv_weights)
        grad_ln_one, gain_one_grad, shift_one_grad = pull_one(grad_normed)
        grads_all.append(grad_hidden + grad_ln_one)
        attn_acc = attn_acc + jnp.concatenate([qkv_grad, out_proj_grad], axis=1)
        norm_acc = norm_acc + jnp.concatenate(
            [gain_one_grad, shift_one_grad, gain_two_grad, shift_two_grad]
        )
    ffn_grad = lax.psum_scatter(
        ffn_acc.astype(jnp.bfloat16), "row", scatter_dimension=1, tiled=True
    ).astype(jnp.float32)
    attn_grad, norm_grad = (
        lax.psum_scatter(attn_acc, ("row", "col"), scatter_dimension=1, tiled=True),
        lax.psum_scatter(norm_acc, ("row", "col"), scatter_dimension=0, tiled=True),
    )
    total_tokens = MB * length * lax.axis_size("row") * lax.axis_size("col")
    step_rate = RATE_SCALE * total_tokens ** (-0.5)
    attn_moment_new, attn_new, attn_avg_new, attn_copy = sgd_update(
        attn_weights, attn_momentum, attn_average, attn_grad, step_rate
    )
    norm_moment_new, norm_new, norm_avg_new, norm_copy = sgd_update(
        norm_params, norm_momentum, norm_average, norm_grad, step_rate
    )
    ffn_moment_new, ffn_new, ffn_avg_new, ffn_copy = sgd_update(
        ffn_weights, ffn_momentum, ffn_average, ffn_grad, step_rate
    )
    return (
        jnp.stack(outputs_all),
        jnp.stack(grads_all),
        attn_grad,
        attn_moment_new,
        attn_new,
        attn_avg_new,
        attn_copy,
        norm_grad,
        norm_moment_new,
        norm_new,
        norm_avg_new,
        norm_copy,
        ffn_grad,
        ffn_moment_new,
        ffn_new,
        ffn_avg_new,
        ffn_copy,
    )


MESH_ID = pl.DeviceIdType.MESH
BF = jnp.bfloat16
F32 = jnp.float32
LANES = 128
HEADS_TILE = LANES // HD
PAD_ROWS = 96
HALF_ROWS = PAD_ROWS // 2
Z_SIZE = 4
ROWS = 4


def dot_nn(a, b):
    return lax.dot_general(a, b, (((1,), (0,)), ((), ())), preferred_element_type=F32)


def dot_nt(a, b):
    return lax.dot_general(a, b, (((1,), (1,)), ((), ())), preferred_element_type=F32)


def dot_tn(a, b):
    return lax.dot_general(a, b, (((0,), (0,)), ((), ())), preferred_element_type=F32)


def ln_stats(values):
    center = values - jnp.mean(values, axis=-1, keepdims=True)
    spread = jnp.mean(center * center, axis=-1, keepdims=True)
    inv = lax.rsqrt(spread + EPSILON)
    return center * inv, inv


def ln_backward(normal, inv, gain, grad):
    scaled = grad * gain
    mean_one = jnp.mean(scaled, axis=-1, keepdims=True)
    mean_two = jnp.mean(scaled * normal, axis=-1, keepdims=True)
    return inv * (scaled - mean_one - normal * mean_two)


def erf_f32(v):
    v = jnp.clip(v, -3.832506856900711, 3.832506856900711)
    s = v * v
    num = jnp.full_like(s, 0.00022905065861350646)
    for coef in (
        0.0034082910107109506,
        0.050955695062380861,
        0.18520832239976145,
        1.128379143519084,
    ):
        num = num * s + coef
    den = jnp.full_like(s, -1.1791602954361697e-7)
    for coef in (
        0.000023547966471313185,
        0.0010179625278914885,
        0.014070470171167667,
        0.11098505178285362,
        0.49746925110067538,
        1.0,
    ):
        den = den * s + coef
    return v * num / den


def gelu_pair(u):
    phi_cap = 0.5 + 0.5 * erf_f32(u * (2.0 ** -0.5))
    density = jnp.exp(-0.5 * u * u) * (1.0 / math.sqrt(2.0 * math.pi))
    return u * phi_cap, phi_cap + u * density


def step_kernel(
    x_hbm, dy_hbm, idr, idc, wsh, fsh,
    yout, ig, fgrad, agrad,
    wslot, wall, fw, n1, qkv, abuf, obuf, tn2, tdy, n2t, dyt, gb, dub, yacc, dnacc, ry, rdn, dyv, dw,
    fr1, fr2, fr3, rc, ar1, ar2, ar3, bias, dob,
    ld_sem, ag_s, ag_r, fg_s, fg_r, sib_s, sib_r, tok_s, tok_r, part_s, part_r,
    frs_s, frs_r, ars_s, ars_r, rc_s, rc_r,
):
    r = lax.axis_index("row")
    c = lax.axis_index("col")
    y, x, z, k = r // 2, r % 2, c // 2, c % 2
    rx, ry_, rd = y * 2 + (1 - x), (1 - y) * 2 + x, (1 - y) * 2 + (1 - x)
    dev_x = (rx, c)
    dev_y = (ry_, c)
    dev_sib = (r, z * 2 + (1 - k))

    def zat(j):
        return ((z // 2 + j // 2) % 2) * 2 + (z % 2 + j % 2) % 2

    def dev_z(j):
        return (r, zat(j) * 2 + k)

    def remote(src, dst, ss, rs, dev):
        return pltpu.make_async_remote_copy(
            src_ref=src, dst_ref=dst, send_sem=ss, recv_sem=rs, device_id=dev, device_id_type=MESH_ID
        )

    ld_x = pltpu.make_async_copy(x_hbm, ig, ld_sem.at[0])
    ld_y = pltpu.make_async_copy(dy_hbm, dyv, ld_sem.at[1])
    ld_x.start()
    ld_y.start()

    barrier = pltpu.get_barrier_semaphore()
    for dev in (dev_sib, dev_x, dev_y, dev_z(1), dev_z(2), dev_z(3)):
        pl.semaphore_signal(barrier, inc=1, device_id=dev, device_id_type=MESH_ID)

    wslot[r, z, k] = wsh[...]
    fw[z, :, r] = fsh[...]
    pl.semaphore_wait(barrier, 6)

    def a_piece(rr, zz):
        return wslot.at[rr, zz, k]

    def a_part(rr, zz, p):
        return wslot.at[rr, zz, k, pl.ds(HALF_ROWS * p, HALF_ROWS)]

    def f_piece(rr, zz):
        return fw.at[zz, :, rr]

    def f_part(rr, zz, p):
        return fw.at[zz, p, rr]

    def gather_ops(piece, part, ss, rs):
        def cz(j):
            return remote(piece(r, z), piece(r, z), ss.at[0, j], rs.at[0, j], dev_z(j))

        def cx(j):
            return remote(piece(r, zat(j)), piece(r, zat(j)), ss.at[1, j], rs.at[1, j], dev_x)

        def cy(j):
            return remote(piece(r, zat(j)), piece(r, zat(j)), ss.at[2, j], rs.at[2, j], dev_y)

        def cd0(j):
            return remote(part(rx, zat(j), 0), part(rx, zat(j), 0), ss.at[3, j], rs.at[3, j], dev_y)

        def cd1(j):
            return remote(part(ry_, zat(j), 1), part(ry_, zat(j), 1), ss.at[4, j], rs.at[4, j], dev_x)

        return cz, cx, cy, cd0, cd1

    az, ax, ay, ad0, ad1 = gather_ops(a_piece, a_part, ag_s, ag_r)
    fz, fx, fy, fd0, fd1 = gather_ops(f_piece, f_part, fg_s, fg_r)

    def sib(j):
        return remote(
            wslot.at[:, zat(j), k], wslot.at[:, zat(j), k], sib_s.at[j], sib_r.at[j], dev_sib
        )

    for j in (1, 2, 3):
        az(j).start()
    ax(0).start()
    ay(0).start()

    ld_y.wait()

    def make_bias(m, _):
        bias[m] = jnp.where(idr[m] == idc[m], 0.0, MASKED).astype(F32)
        tdy[2 * k + m] = dyv[m].astype(BF)
        return 0

    lax.fori_loop(0, MB, make_bias, 0)

    def tok_dy():
        return remote(tdy.at[pl.ds(2 * k, 2)], tdy.at[pl.ds(2 * k, 2)], tok_s.at[0], tok_r.at[0], dev_sib)

    def tok_n2():
        return remote(tn2.at[pl.ds(2 * k, 2)], tn2.at[pl.ds(2 * k, 2)], tok_s.at[1], tok_r.at[1], dev_sib)

    tok_dy().start()

    ax(0).wait_recv()
    ad0(0).start()
    ay(0).wait_recv()
    ad1(0).start()
    for j in (1, 2, 3):
        az(j).wait_recv()
        ax(j).start()
        ay(j).start()
    for j in (1, 2, 3):
        fz(j).start()
    for j in (1, 2, 3):
        ax(j).wait_recv()
        ad0(j).start()
        ay(j).wait_recv()
        ad1(j).start()
    fx(0).start()
    fy(0).start()
    for j in range(Z_SIZE):
        ad0(j).wait_recv()
        ad1(j).wait_recv()
        sib(j).start()
    for j in range(Z_SIZE):
        sib(j).wait_recv()

    def compact(d, _):
        wall[d] = wslot[d // (2 * Z_SIZE), (d // 2) % Z_SIZE, d % 2, 0:80]
        return 0

    lax.fori_loop(0, 8 * ROWS, compact, 0)

    def norm_vector(row):
        total = jnp.zeros((1, D), F32)
        for zz in range(Z_SIZE):
            for kk in range(2):
                total = total + wslot[row, zz, kk, 80:96].astype(F32)[0:1]
        return total

    gain_one, shift_one, gain_two, shift_two = [norm_vector(row) for row in range(4)]

    ld_x.wait()

    def first_norm(m, _):
        normal, _inv = ln_stats(ig[m])
        n1[m] = (normal * gain_one + shift_one).astype(BF)
        return 0

    lax.fori_loop(0, MB, first_norm, 0)

    def project(i, _):
        m, p = i // 3, i % 3
        weights = wall[pl.ds(8 * p, 8)].reshape(D, D)
        qkv[m, p] = dot_nt(n1[m], weights).astype(BF)
        return 0

    lax.fori_loop(0, 3 * MB, project, 0)

    lane_head = lax.broadcasted_iota(jnp.int32, (1, LANES), 1) // HD
    head_mask = [jnp.where(lane_head == h, 1.0, 0.0).astype(BF) for h in range(HEADS_TILE)]
    groups = D // LANES
    scale = HD ** (-0.5)

    def at_step(it, i, fn):
        @pl.when(it == i)
        def _():
            fn()

    def gather_xy(j):
        fz(j).wait_recv()
        fx(j).start()
        fy(j).start()

    def gather_diag(j):
        fx(j).wait_recv()
        fd0(j).start()
        fy(j).wait_recv()
        fd1(j).start()

    def forward_group(it, _):
        m, g = it // groups, it % groups
        at_step(it, 1, lambda: gather_diag(0))
        at_step(it, 3, lambda: gather_xy(1))
        at_step(it, 5, lambda: gather_xy(2))
        at_step(it, 6, lambda: gather_diag(1))
        at_step(it, 8, lambda: gather_xy(3))
        lanes = pl.ds(pl.multiple_of(g * LANES, LANES), LANES)
        q = qkv[m, 0, :, lanes]
        kk = qkv[m, 1, :, lanes]
        v = qkv[m, 2, :, lanes]
        mask_bias = bias[m]
        mixed = None
        for h in range(HEADS_TILE):
            scores = dot_nt(q * head_mask[h], kk) * scale + mask_bias
            row_max = jnp.max(scores, axis=-1, keepdims=True)
            expo = jnp.exp(scores - row_max)
            total = jnp.sum(expo, axis=-1, keepdims=True)
            probs = (expo * (1.0 / total)).astype(BF)
            abuf[it * HEADS_TILE + h] = probs
            part = dot_nn(probs, v * head_mask[h])
            mixed = part if mixed is None else mixed + part
        obuf[m, :, lanes] = mixed.astype(BF)
        return 0

    lax.fori_loop(0, MB * groups, forward_group, 0)

    def second_norm(m, _):
        hidden = ig[m] + dot_nt(obuf[m], wall[24:32].reshape(D, D))
        yout[m] = hidden
        normal, _inv = ln_stats(hidden)
        tn2[2 * k + m] = (normal * gain_two + shift_two).astype(BF)
        return 0

    lax.fori_loop(0, MB, second_norm, 0)
    tok_n2().start()
    gather_diag(2)
    tok_dy().wait_recv()
    tok_n2().wait_recv()

    def turn(t, _):
        cols = pl.ds(pl.multiple_of(t * 256, 256), 256)
        n2t[:, :, cols] = tn2[t].T.reshape(ROWS, 160, 256)
        dyt[:, :, cols] = tdy[t].T.reshape(ROWS, 160, 256)
        return 0

    lax.fori_loop(0, 2 * MB, turn, 0)

    def scatter_ops(block, r1, r2, r3, ss, rs):
        def one(j, p, b):
            dev = dev_y if p == 0 else dev_x
            rr = rd if b == 1 else (ry_ if p == 0 else rx)
            return remote(block(rr, zat(j), p), r1(j, p, b), ss.at[2 * p + b, j], rs.at[2 * p + b, j], dev)

        def two(j, p):
            dev = dev_x if p == 0 else dev_y
            rr = rx if p == 0 else ry_
            return remote(block(rr, zat(j), p), r2(j, p), ss.at[4 + p, j], rs.at[4 + p, j], dev)

        def three(j, p):
            return remote(block(r, zat(j), p), r3(j, p), ss.at[6 + p, j], rs.at[6 + p, j], dev_z(j))

        def start_one(j):
            for p in range(2):
                for b in (1, 0):
                    one(j, p, b).start()

        def start_two(j):
            for p in range(2):
                one(j, p, 0).wait_recv()
                one(j, p, 1).wait_recv()
                rr = rx if p == 0 else ry_
                mine = block(rr, zat(j), p)
                mine[...] = (mine[...].astype(F32) + r1(j, p, 1)[...].astype(F32)).astype(BF)
                two(j, p).start()

        def own_sum(j, p):
            return (
                block(r, zat(j), p)[...].astype(F32)
                + r1(j, p, 0)[...].astype(F32)
                + r2(j, p)[...].astype(F32)
            )

        def start_three(j):
            for p in range(2):
                two(j, p).wait_recv()
                mine = block(r, zat(j), p)
                mine[...] = own_sum(j, p).astype(BF)
                three(j, p).start()

        def finish(out):
            for p in range(2):
                two(0, p).wait_recv()
                total = own_sum(0, p)
                for j in (1, 2, 3):
                    three(j, p).wait_recv()
                    total = total + r3(j, p)[...].astype(F32)
                out(p)[...] = total

        def drain(j):
            for p in range(2):
                one(j, p, 0).wait_send()
                one(j, p, 1).wait_send()
                two(j, p).wait_send()

        def drain_three(j):
            for p in range(2):
                three(j, p).wait_send()

        return start_one, start_two, start_three, finish, drain, drain_three

    f_one, f_two, f_three, f_finish, f_drain, f_drain3 = scatter_ops(
        lambda rr, zz, p: dw.at[zz, p, rr],
        lambda j, p, b: fr1.at[j, p, b],
        lambda j, p: fr2.at[j, p],
        lambda j, p: fr3.at[j - 1, p],
        frs_s, frs_r,
    )
    a_one, a_two, a_three, a_finish, a_drain, a_drain3 = scatter_ops(
        lambda rr, zz, p: wslot.at[rr, zz, k, pl.ds(HALF_ROWS * p, HALF_ROWS)],
        lambda j, p, b: ar1.at[j, p, b],
        lambda j, p: ar2.at[j, p],
        lambda j, p: ar3.at[j - 1, p],
        ars_s, ars_r,
    )

    def hidden_block(j, _):
        @pl.when(j == 0)
        def _():
            gather_diag(3)

        fd0(j).wait_recv()
        fd1(j).wait_recv()
        zz = zat(j)

        def token_tile(t, _):
            up = fw[zz, 0].reshape(D, D)
            down = fw[zz, 1].reshape(D, D)
            u = dot_nn(tn2[t], up)
            grad_act = dot_nn(tdy[t], down)
            act, slope = gelu_pair(u)
            act = act.astype(BF)
            grad_up = (grad_act * slope).astype(BF)
            gb[t] = act
            dub[t] = grad_up
            y_part = dot_nt(act, down)
            dn_part = dot_nt(grad_up, up)

            @pl.when(j == 0)
            def _():
                yacc[t] = y_part
                dnacc[t] = dn_part

            @pl.when(j > 0)
            def _():
                yacc[t] += y_part
                dnacc[t] += dn_part

            return 0

        lax.fori_loop(0, 2 * MB, token_tile, 0)

        @pl.when(j == Z_SIZE - 1)
        def _():
            part_dn().start()
            part_y().start()

        def weight_rows(rr, _):
            dw[zz, 0, rr] = dot_nn(n2t[rr], dub[...].reshape(4 * 256, D)).astype(BF)
            dw[zz, 1, rr] = dot_nn(dyt[rr], gb[...].reshape(4 * 256, D)).astype(BF)
            return 0

        lax.fori_loop(0, ROWS, weight_rows, 0)
        f_one(j)

        @pl.when(j >= 2)
        def _():
            f_two(j - 2)

        return 0

    def part_dn():
        return remote(dnacc.at[pl.ds(2 * (1 - k), 2)], rdn, part_s.at[0], part_r.at[0], dev_sib)

    def part_y():
        return remote(yacc.at[pl.ds(2 * (1 - k), 2)], ry, part_s.at[1], part_r.at[1], dev_sib)

    lax.fori_loop(0, Z_SIZE, hidden_block, 0)

    for j in (1, 2, 3):
        az(j).wait_send()
        fz(j).wait_send()
    for j in range(Z_SIZE):
        for op in (ax, ay, ad0, ad1, fx, fy, fd0, fd1, sib):
            op(j).wait_send()

    part_dn().wait_recv()
    part_y().wait_recv()

    zero = jnp.zeros((1, D), F32)

    def second_backward(m, sums):
        gain_sum, shift_sum = sums
        hidden = yout[m]
        normal, inv = ln_stats(hidden)
        grad = dnacc[2 * k + m] + rdn[m]
        yout[m] = hidden + (yacc[2 * k + m] + ry[m])
        grad_hidden = dyv[m] + ln_backward(normal, inv, gain_two, grad)
        dyv[m] = grad_hidden
        low = grad_hidden.astype(BF)
        n1_rows = wall[24:32].reshape(D, D)
        dob[m] = dot_nn(low, n1_rows).astype(BF)
        dhb = low
        tn2[2 * k + m] = dhb
        return (
            gain_sum + jnp.sum(grad * normal, axis=0, keepdims=True),
            shift_sum + jnp.sum(grad, axis=0, keepdims=True),
        )

    tok_n2().wait_send()
    gain_two_grad, shift_two_grad = lax.fori_loop(0, MB, second_backward, (zero, zero))

    out_grad = dot_tn(tn2[2 * k], obuf[0]) + dot_tn(tn2[2 * k + 1], obuf[1])
    wslot[3, :, :, 0:80] = out_grad.astype(BF).reshape(Z_SIZE, 2, 80, D)

    def backward_group(it, _):
        m, g = it // groups, it % groups
        at_step(it, 0, lambda: f_two(2))
        at_step(it, 2, lambda: f_two(3))
        at_step(it, 3, lambda: f_three(1))
        at_step(it, 6, lambda: f_three(2))
        at_step(it, 9, lambda: f_three(3))
        lanes = pl.ds(pl.multiple_of(g * LANES, LANES), LANES)
        q = qkv[m, 0, :, lanes]
        kk = qkv[m, 1, :, lanes]
        v = qkv[m, 2, :, lanes]
        do = dob[m, :, lanes]
        q_turned = q.T
        do_turned = do.T
        grad_q = None
        grad_k = []
        grad_v = []
        for h in range(HEADS_TILE):
            probs = abuf[it * HEADS_TILE + h]
            wide = probs.astype(F32)
            grad_probs = dot_nt(do * head_mask[h], v)
            product = grad_probs * wide
            row = jnp.sum(product, axis=-1, keepdims=True)
            grad_scores = (product - wide * row).astype(BF)
            part = dot_nn(grad_scores, kk * head_mask[h])
            grad_q = part if grad_q is None else grad_q + part
            grad_v.append(dot_nn(do_turned[h * HD : (h + 1) * HD], probs))
            grad_k.append(dot_nn(q_turned[h * HD : (h + 1) * HD], grad_scores))
        qkv[m, 0, :, lanes] = (grad_q * scale).astype(BF)
        qkv[m, 1, :, lanes] = (jnp.concatenate(grad_k, axis=0).T * scale).astype(BF)
        qkv[m, 2, :, lanes] = jnp.concatenate(grad_v, axis=0).T.astype(BF)
        return 0

    lax.fori_loop(0, MB * groups, backward_group, 0)

    def qkv_grad(p, _):
        total = dot_tn(qkv[0, p], n1[0]) + dot_tn(qkv[1, p], n1[1])
        wslot[p, :, :, 0:80] = total.astype(BF).reshape(Z_SIZE, 2, 80, D)
        return 0

    lax.fori_loop(0, 3, qkv_grad, 0)

    def first_backward(m, sums):
        gain_sum, shift_sum = sums
        grad = dot_nn(qkv[m, 0], wall[0:8].reshape(D, D))
        grad = grad + dot_nn(qkv[m, 1], wall[8:16].reshape(D, D))
        grad = grad + dot_nn(qkv[m, 2], wall[16:24].reshape(D, D))
        normal, inv = ln_stats(ig[m])
        ig[m] = dyv[m] + ln_backward(normal, inv, gain_one, grad)
        return (
            gain_sum + jnp.sum(grad * normal, axis=0, keepdims=True),
            shift_sum + jnp.sum(grad, axis=0, keepdims=True),
        )

    gain_one_grad, shift_one_grad = lax.fori_loop(0, MB, first_backward, (zero, zero))

    first_row = lax.broadcasted_iota(jnp.int32, (16, D), 0) == 0
    for row, vec in enumerate((gain_one_grad, shift_one_grad, gain_two_grad, shift_two_grad)):
        tile = jnp.where(first_row, jnp.broadcast_to(vec, (16, D)), 0.0).astype(BF)
        for zz in range(Z_SIZE):
            for kk in range(2):
                wslot[row, zz, kk, 80:96] = tile

    def cross(j):
        return remote(wslot.at[:, zat(j), 1 - k], rc.at[j], rc_s.at[j], rc_r.at[j], dev_sib)

    order = (3, 2, 1, 0)
    for j in order:
        cross(j).start()
    for j in order:
        cross(j).wait_recv()

        def add_pair(rr, _):
            mine = wslot[rr, zat(j), k].astype(F32) + rc[j, rr].astype(F32)
            wslot[rr, zat(j), k] = mine.astype(BF)
            return 0

        lax.fori_loop(0, ROWS, add_pair, 0)
        a_one(j)
    for j in order:
        a_two(j)
    for j in (3, 2, 1):
        a_three(j)
    f_finish(lambda p: fgrad.at[p])
    a_finish(lambda p: agrad.at[pl.ds(HALF_ROWS * p, HALF_ROWS)])

    tok_dy().wait_send()
    part_dn().wait_send()
    part_y().wait_send()
    for j in range(Z_SIZE):
        f_drain(j)
        a_drain(j)
        cross(j).wait_send()
    for j in (1, 2, 3):
        f_drain3(j)
        a_drain3(j)


def run_step(x, dy, ids, wsh, fsh):
    length = x.shape[1]
    vm = pltpu.VMEM
    dma = pltpu.SemaphoreType.DMA
    idr = ids[:, :, None]
    idc = ids[:, None, :]
    any_spec = pl.BlockSpec(memory_space=pl.ANY)
    vspec = pl.BlockSpec(memory_space=pltpu.VMEM)
    fr, fc = fsh.shape[1], fsh.shape[2]
    return pl.pallas_call(
        step_kernel,
        out_shape=(
            jax.ShapeDtypeStruct((MB, length, D), F32),
            jax.ShapeDtypeStruct((MB, length, D), F32),
            jax.ShapeDtypeStruct((2, fr, fc), F32),
            jax.ShapeDtypeStruct((PAD_ROWS, D), F32),
        ),
        in_specs=[any_spec, any_spec, vspec, vspec, vspec, vspec],
        out_specs=(vspec, vspec, vspec, vspec),
        scratch_shapes=[
            vm((ROWS, Z_SIZE, 2, PAD_ROWS, D), BF),
            vm((32, 80, D), BF),
            vm((Z_SIZE, 2, ROWS, fr, fc), BF),
            vm((MB, length, D), BF),
            vm((MB, 3, length, D), BF),
            vm((MB * H, length, length), BF),
            vm((MB, length, D), BF),
            vm((2 * MB, length, D), BF),
            vm((2 * MB, length, D), BF),
            vm((ROWS, fr, 2 * MB * length), BF),
            vm((ROWS, fr, 2 * MB * length), BF),
            vm((2 * MB, length, fc), BF),
            vm((2 * MB, length, fc), BF),
            vm((2 * MB, length, D), F32),
            vm((2 * MB, length, D), F32),
            vm((MB, length, D), F32),
            vm((MB, length, D), F32),
            vm((MB, length, D), F32),
            vm((Z_SIZE, 2, ROWS, fr, fc), BF),
            vm((Z_SIZE, 2, 2, fr, fc), BF),
            vm((Z_SIZE, 2, fr, fc), BF),
            vm((Z_SIZE - 1, 2, fr, fc), BF),
            vm((Z_SIZE, ROWS, PAD_ROWS, D), BF),
            vm((Z_SIZE, 2, 2, HALF_ROWS, D), BF),
            vm((Z_SIZE, 2, HALF_ROWS, D), BF),
            vm((Z_SIZE - 1, 2, HALF_ROWS, D), BF),
            vm((MB, length, length), F32),
            vm((MB, length, D), BF),
            dma((2,)),
            dma((5, Z_SIZE)), dma((5, Z_SIZE)),
            dma((5, Z_SIZE)), dma((5, Z_SIZE)),
            dma((Z_SIZE,)), dma((Z_SIZE,)),
            dma((2,)), dma((2,)),
            dma((2,)), dma((2,)),
            dma((8, Z_SIZE)), dma((8, Z_SIZE)),
            dma((8, Z_SIZE)), dma((8, Z_SIZE)),
            dma((Z_SIZE,)), dma((Z_SIZE,)),
        ],
        compiler_params=pltpu.CompilerParams(
            collective_id=0, has_side_effects=True, vmem_limit_bytes=64 * 1024 * 1024 - 4096
        ),
        name="encoder_step",
    )(x, dy, idr, idc, wsh, fsh)


def local_slice(
    block_input, output_grad, sequence_ids,
    attn_weights, attn_momentum, attn_average,
    norm_params, norm_momentum, norm_average,
    ffn_weights, ffn_momentum, ffn_average,
):
    width = attn_weights.shape[1]
    shift = lax.axis_index("col") * width
    norm_row = lax.dynamic_update_slice(
        jnp.zeros((D,), BF), norm_params.astype(BF), (shift,)
    )
    wsh = jnp.concatenate(
        [
            attn_weights.astype(BF).T,
            norm_row[None],
            jnp.zeros((PAD_ROWS - width - 1, D), BF),
        ],
        axis=0,
    )
    outputs, grads, ffn_grad, shard = run_step(
        block_input, output_grad, sequence_ids, wsh, ffn_weights.astype(BF)
    )
    attn_grad = shard[:width].T
    norm_grad = lax.dynamic_slice(shard[width], (shift,), (width,))
    total_tokens = MB * block_input.shape[1] * lax.axis_size("row") * lax.axis_size("col")
    step_rate = RATE_SCALE * total_tokens ** (-0.5)
    attn = sgd_update(attn_weights, attn_momentum, attn_average, attn_grad, step_rate)
    norm = sgd_update(norm_params, norm_momentum, norm_average, norm_grad, step_rate)
    ffn = sgd_update(ffn_weights, ffn_momentum, ffn_average, ffn_grad, step_rate)
    return (outputs, grads, attn_grad, *attn, norm_grad, *norm, ffn_grad, *ffn)


def local(*args):
    ffn_block = args[9].shape
    on_slice = (
        lax.axis_size("row") == ROWS
        and lax.axis_size("col") == 2 * Z_SIZE
        and ffn_block == (2, D // ROWS, D)
        and args[3].shape == (D, 80)
        and args[0].shape[1] == 256
    )
    return (local_slice if on_slice else local_general)(*args)


def solution(mesh):
    return jax.shard_map(
        local,
        mesh=mesh,
        in_specs=(
            P(None, ("row", "col"), None),
            P(None, ("row", "col"), None),
            P(None, ("row", "col")),
            P(None, ("row", "col")),
            P(None, ("row", "col")),
            P(None, ("row", "col")),
            P(("row", "col")),
            P(("row", "col")),
            P(("row", "col")),
            P(None, "row", "col"),
            P(None, "row", "col"),
            P(None, "row", "col"),
        ),
        out_specs=(
            P(None, ("row", "col"), None),
            P(None, ("row", "col"), None),
            P(None, ("row", "col")),
            P(None, ("row", "col")),
            P(None, ("row", "col")),
            P(None, ("row", "col")),
            P(None, ("row", "col")),
            P(("row", "col")),
            P(("row", "col")),
            P(("row", "col")),
            P(("row", "col")),
            P(("row", "col")),
            P(None, "row", "col"),
            P(None, "row", "col"),
            P(None, "row", "col"),
            P(None, "row", "col"),
            P(None, "row", "col"),
        ),
        check_vma=False,
    )
```

```python
import functools
import math

import jax
import jax.numpy as jnp
from jax import lax
from jax.experimental import pallas as pl
from jax.experimental.pallas import tpu as pltpu
from jax.sharding import PartitionSpec as P

D = 640
H = 20
HD = 32
MB = 2


EPSILON = 1e-05
MOMENT_DECAY = 0.9
AVERAGE_DECAY = 0.85
RATE_SCALE = 0.06
MASKED = -1e30


def layer_norm(values, gain, shift):
    center = values - jnp.mean(values, axis=-1, keepdims=True)
    spread = jnp.mean(center * center, axis=-1, keepdims=True)
    return center * lax.rsqrt(spread + EPSILON) * gain + shift


def gelu_exact(values):
    return jax.nn.gelu(values, approximate=False)


def matmul(left_side, right_side):
    return jnp.dot(left_side, right_side, preferred_element_type=jnp.float32)


def contract_rows(left_side, right_side):
    return lax.dot_general(
        left_side, right_side, (((0,), (0,)), ((), ())), preferred_element_type=jnp.float32
    )


def contract_cols(left_side, right_side):
    return lax.dot_general(
        left_side, right_side, (((1,), (1,)), ((), ())), preferred_element_type=jnp.float32
    )


def head_slices(qkv_low, first_col, head_group):
    length = qkv_low.shape[0]
    group_width = head_group * HD
    queries = lax.dynamic_slice_in_dim(qkv_low, first_col, group_width, 1).reshape(
        length, head_group, HD
    )
    keys_part = lax.dynamic_slice_in_dim(qkv_low, D + first_col, group_width, 1).reshape(
        length, head_group, HD
    )
    values = lax.dynamic_slice_in_dim(qkv_low, 2 * D + first_col, group_width, 1).reshape(
        length, head_group, HD
    )
    return (queries, keys_part, values)


def masked_scores(queries, keys_part, same_seq):
    scores = jnp.einsum(
        "qhe,khe->hqk", queries, keys_part, preferred_element_type=jnp.float32
    ) * HD ** (-0.5)
    return jnp.where(same_seq[None], scores, MASKED)


def attend_forward(qkv_low, same_seq):
    length = qkv_low.shape[0]
    head_group = math.gcd(H, 4)
    group_width = head_group * HD

    def one_group(group_index, state_all):
        mixed_all, maxima, totals = state_all
        first_col = group_index * group_width
        queries, keys_part, values = head_slices(qkv_low, first_col, head_group)
        scores = masked_scores(queries, keys_part, same_seq)
        row_max = jnp.max(scores, axis=-1, keepdims=True)
        exponent = jnp.exp(scores - row_max)
        row_total = jnp.sum(exponent, axis=-1, keepdims=True)
        attn_probs = (exponent / row_total).astype(jnp.bfloat16)
        mixed_rows = jnp.einsum(
            "hqk,khe->qhe", attn_probs, values, preferred_element_type=jnp.float32
        )
        mixed_all = lax.dynamic_update_slice_in_dim(
            mixed_all, mixed_rows.reshape(length, group_width), first_col, 1
        )
        maxima = lax.dynamic_update_slice_in_dim(
            maxima, row_max[:, :, 0], group_index * head_group, 0
        )
        totals = lax.dynamic_update_slice_in_dim(
            totals, row_total[:, :, 0], group_index * head_group, 0
        )
        return (mixed_all, maxima, totals)

    initial = (
        jnp.zeros((length, D), jnp.float32),
        jnp.zeros((H, length), jnp.float32),
        jnp.zeros((H, length), jnp.float32),
    )
    return lax.fori_loop(0, H // head_group, one_group, initial)


def attend_backward(qkv_low, same_seq, maxima, totals, grad_mixed):
    length = qkv_low.shape[0]
    head_group = math.gcd(H, 4)
    group_width = head_group * HD

    def one_group(group_index, grad_qkv):
        first_col = group_index * group_width
        queries, keys_part, values = head_slices(qkv_low, first_col, head_group)
        grad_part = lax.dynamic_slice_in_dim(grad_mixed, first_col, group_width, 1).reshape(
            length, head_group, HD
        )
        scores = masked_scores(queries, keys_part, same_seq)
        row_max = lax.dynamic_slice_in_dim(maxima, group_index * head_group, head_group, 0)[
            :, :, None
        ]
        row_total = lax.dynamic_slice_in_dim(totals, group_index * head_group, head_group, 0)[
            :, :, None
        ]
        attn_probs = jnp.exp(scores - row_max) / row_total
        grad_probs = jnp.einsum(
            "qhe,khe->hqk", grad_part, values, preferred_element_type=jnp.float32
        )
        grad_values = jnp.einsum(
            "hqk,qhe->khe",
            attn_probs.astype(jnp.bfloat16),
            grad_part,
            preferred_element_type=jnp.float32,
        )
        grad_scores = attn_probs * (
            grad_probs - jnp.sum(grad_probs * attn_probs, axis=-1, keepdims=True)
        )
        grad_scores = grad_scores.astype(jnp.bfloat16)
        grad_queries = jnp.einsum(
            "hqk,khe->qhe", grad_scores, keys_part, preferred_element_type=jnp.float32
        ) * HD ** (-0.5)
        grad_keys = jnp.einsum(
            "hqk,qhe->khe", grad_scores, queries, preferred_element_type=jnp.float32
        ) * HD ** (-0.5)
        for offset, grad_piece in ((0, grad_queries), (D, grad_keys), (2 * D, grad_values)):
            grad_qkv = lax.dynamic_update_slice_in_dim(
                grad_qkv, grad_piece.reshape(length, group_width), offset + first_col, 1
            )
        return grad_qkv

    return lax.fori_loop(0, H // head_group, one_group, jnp.zeros((length, 3 * D), jnp.float32))


def sgd_update(weights_old, moment, average, grad_sum, step_rate):
    moment_new = MOMENT_DECAY * moment + grad_sum
    weights_new = weights_old - step_rate * (grad_sum + MOMENT_DECAY * moment_new)
    average_new = AVERAGE_DECAY * average + (1.0 - AVERAGE_DECAY) * weights_new
    return (moment_new, weights_new, average_new, weights_new.astype(jnp.bfloat16))


def local_general(
    block_input,
    output_grad,
    sequence_ids,
    attn_weights,
    attn_momentum,
    attn_average,
    norm_params,
    norm_momentum,
    norm_average,
    ffn_weights,
    ffn_momentum,
    ffn_average,
):
    attn_full, norm_full = (
        lax.all_gather(attn_weights.astype(jnp.bfloat16), ("row", "col"), axis=1, tiled=True),
        lax.all_gather(norm_params.astype(jnp.bfloat16), ("row", "col"), axis=0, tiled=True),
    )
    norm_values = norm_full.astype(jnp.float32)
    gain_one = norm_values[:D]
    shift_one = norm_values[D : 2 * D]
    gain_two = norm_values[2 * D : 3 * D]
    shift_two = norm_values[3 * D :]
    qkv_weights = attn_full[:, : 3 * D]
    out_weights = attn_full[:, 3 * D :]
    ffn_rows = lax.all_gather(ffn_weights.astype(jnp.bfloat16), "row", axis=1, tiled=True)
    col_width = ffn_weights.shape[2]
    length = block_input.shape[1]
    attn_acc = jnp.zeros((D, 4 * D), jnp.float32)
    norm_acc = jnp.zeros((4 * D,), jnp.float32)
    ffn_acc = jnp.zeros((2, D, col_width), jnp.float32)
    outputs_all = []
    grads_all = []
    for micro_step in range(MB):
        inputs = block_input[micro_step]
        ids_row = sequence_ids[micro_step]
        same_seq = ids_row[:, None] == ids_row[None, :]
        normed, pull_one = jax.vjp(layer_norm, inputs, gain_one, shift_one)
        normed_low = normed.astype(jnp.bfloat16)
        qkv_low = matmul(normed_low, qkv_weights).astype(jnp.bfloat16)
        mixed_all, maxima, totals = attend_forward(qkv_low, same_seq)
        mixed_low = mixed_all.astype(jnp.bfloat16)
        hidden_in = inputs + matmul(mixed_low, out_weights)
        normed_two, pull_two = jax.vjp(layer_norm, hidden_in, gain_two, shift_two)
        normed_two_low = normed_two.astype(jnp.bfloat16)
        grad_out = output_grad[micro_step]
        grad_out_low = grad_out.astype(jnp.bfloat16)
        normed_all = lax.all_gather(normed_two_low, "col", axis=0, tiled=True)
        up_proj = matmul(normed_all, ffn_rows[0])
        activation, pull_gelu = jax.vjp(gelu_exact, up_proj)
        activ_low = activation.astype(jnp.bfloat16)
        ffn_out = lax.psum_scatter(
            contract_cols(activ_low, ffn_rows[1]).astype(jnp.bfloat16),
            "col",
            scatter_dimension=0,
            tiled=True,
        ).astype(jnp.float32)
        grad_all = lax.all_gather(grad_out_low, "col", axis=0, tiled=True)
        grad_act = matmul(grad_all, ffn_rows[1])
        grad_up = pull_gelu(grad_act)[0].astype(jnp.bfloat16)
        grad_normed_two = lax.psum_scatter(
            contract_cols(grad_up, ffn_rows[0]).astype(jnp.bfloat16),
            "col",
            scatter_dimension=0,
            tiled=True,
        ).astype(jnp.float32)
        ffn_acc = ffn_acc + jnp.stack(
            [contract_rows(normed_all, grad_up), contract_rows(grad_all, activ_low)]
        )
        outputs_all.append(hidden_in + ffn_out)
        grad_ln_two, gain_two_grad, shift_two_grad = pull_two(grad_normed_two)
        grad_hidden = grad_out + grad_ln_two
        grad_branch_low = grad_hidden.astype(jnp.bfloat16)
        out_proj_grad = contract_rows(mixed_low, grad_branch_low)
        grad_mixed_low = contract_cols(grad_branch_low, out_weights).astype(jnp.bfloat16)
        grad_qkv_low = attend_backward(qkv_low, same_seq, maxima, totals, grad_mixed_low).astype(
            jnp.bfloat16
        )
        qkv_grad = contract_rows(normed_low, grad_qkv_low)
        grad_normed = contract_cols(grad_qkv_low, qkv_weights)
        grad_ln_one, gain_one_grad, shift_one_grad = pull_one(grad_normed)
        grads_all.append(grad_hidden + grad_ln_one)
        attn_acc = attn_acc + jnp.concatenate([qkv_grad, out_proj_grad], axis=1)
        norm_acc = norm_acc + jnp.concatenate(
            [gain_one_grad, shift_one_grad, gain_two_grad, shift_two_grad]
        )
    ffn_grad = lax.psum_scatter(
        ffn_acc.astype(jnp.bfloat16), "row", scatter_dimension=1, tiled=True
    ).astype(jnp.float32)
    attn_grad, norm_grad = (
        lax.psum_scatter(attn_acc, ("row", "col"), scatter_dimension=1, tiled=True),
        lax.psum_scatter(norm_acc, ("row", "col"), scatter_dimension=0, tiled=True),
    )
    total_tokens = MB * length * lax.axis_size("row") * lax.axis_size("col")
    step_rate = RATE_SCALE * total_tokens ** (-0.5)
    attn_moment_new, attn_new, attn_avg_new, attn_copy = sgd_update(
        attn_weights, attn_momentum, attn_average, attn_grad, step_rate
    )
    norm_moment_new, norm_new, norm_avg_new, norm_copy = sgd_update(
        norm_params, norm_momentum, norm_average, norm_grad, step_rate
    )
    ffn_moment_new, ffn_new, ffn_avg_new, ffn_copy = sgd_update(
        ffn_weights, ffn_momentum, ffn_average, ffn_grad, step_rate
    )
    return (
        jnp.stack(outputs_all),
        jnp.stack(grads_all),
        attn_grad,
        attn_moment_new,
        attn_new,
        attn_avg_new,
        attn_copy,
        norm_grad,
        norm_moment_new,
        norm_new,
        norm_avg_new,
        norm_copy,
        ffn_grad,
        ffn_moment_new,
        ffn_new,
        ffn_avg_new,
        ffn_copy,
    )


MESH_ID = pl.DeviceIdType.MESH
BF = jnp.bfloat16
F32 = jnp.float32
LANES = 128
HEADS_TILE = LANES // HD
GROUPS = D // LANES
Z_SIZE = 4
COLS = 2 * Z_SIZE
ROWS = 4
WIDTH = D // COLS
LENGTH = 256
FEATURES = D // ROWS
PART_ROWS = (48, 32)
UNITS = ((0, 512), (512, 128), (640, 640))
CHUNKS = ((0, 512), (512, 768))


def dot_nn(a, b):
    return lax.dot_general(a, b, (((1,), (0,)), ((), ())), preferred_element_type=F32)


def dot_nt(a, b):
    return lax.dot_general(a, b, (((1,), (1,)), ((), ())), preferred_element_type=F32)


def dot_tn(a, b):
    return lax.dot_general(a, b, (((0,), (0,)), ((), ())), preferred_element_type=F32)


def ln_stats(values):
    center = values - jnp.mean(values, axis=-1, keepdims=True)
    spread = jnp.mean(center * center, axis=-1, keepdims=True)
    inv = lax.rsqrt(spread + EPSILON)
    return center * inv, inv


def ln_backward(normal, inv, gain, grad):
    scaled = grad * gain
    mean_one = jnp.mean(scaled, axis=-1, keepdims=True)
    mean_two = jnp.mean(scaled * normal, axis=-1, keepdims=True)
    return inv * (scaled - mean_one - normal * mean_two)


def gelu_pair(u):
    size = jnp.abs(u) * (2.0 ** -0.5)
    t = 1.0 / (1.0 + 0.3275911 * size)
    poly = 0.5 * 1.061405429
    for coef in (-1.453152027, 1.421413741, -0.284496736, 0.254829592):
        poly = poly * t + 0.5 * coef
    bell = jnp.exp2(u * u * (-0.5 * math.log2(math.e)))
    tail = poly * t * bell
    cap = jnp.where(u < 0.0, tail, 1.0 - tail)
    return u * cap, cap + u * (bell * (1.0 / math.sqrt(2.0 * math.pi)))


def step_kernel(
    x_hbm, dy_hbm, ffn_hbm, ids, attn_w, norm_w,
    yout, ig, fgrad, agrad, nout, probs_hbm,
    wall, wgrad, fw, n1, qkv, abuf, obuf, tn2, tdy, gb, dub, acc, near, stage, far, dyv,
    fr1, fr2, fr3, rc, ar1, ar2, ar3, bias, dob, nbuf, ngrad, nsum, nr1, nr2,
    ld_sem, pb_sem, ag_s, ag_r, fg_s, fg_r, sib_s, sib_r, tok_s, tok_r, part_s, part_r,
    frs_s, frs_r, ars_s, ars_r, rc_s, rc_r, na_s, na_r, nb_s, nb_r,
):
    r = lax.axis_index("row")
    c = lax.axis_index("col")
    y, x, z, k = r // 2, r % 2, c // 2, c % 2
    rx, ry, rd = y * 2 + (1 - x), (1 - y) * 2 + x, (1 - y) * 2 + (1 - x)
    dev_x = (rx, c)
    dev_y = (ry, c)
    dev_d = (rd, c)
    dev_sib = (r, z * 2 + (1 - k))

    def exclusive(a, b):
        return ((a // 2 + b // 2) % 2) * 2 + (a % 2 + b % 2) % 2

    def zat(j):
        return exclusive(z, j)

    def dev_z(j):
        return (r, zat(j) * 2 + k)

    def dev_row(j):
        return (r, zat(j // 2) * 2 + (k + j % 2) % 2)

    def owner(z_rel, k_rel):
        return ((z + z_rel) % 2) * 2 + (k + k_rel) % 2

    def rows16(start, size):
        return pl.ds(pl.multiple_of(start, 16), size)

    def remote(src, dst, ss, rs, dev):
        return pltpu.make_async_remote_copy(
            src_ref=src, dst_ref=dst, send_sem=ss, recv_sem=rs, device_id=dev, device_id_type=MESH_ID
        )

    barrier = pltpu.get_barrier_semaphore()
    for dev in (dev_x, dev_y, dev_d, *[dev_row(j) for j in range(1, COLS)]):
        pl.semaphore_signal(barrier, inc=1, device_id=dev, device_id_type=MESH_ID)

    ld_f = [pltpu.make_async_copy(ffn_hbm.at[s], acc.at[0, s, pl.ds(0, FEATURES)], ld_sem.at[2 + s]) for s in range(2)]
    ld_x = pltpu.make_async_copy(x_hbm, ig, ld_sem.at[0])
    ld_y = pltpu.make_async_copy(dy_hbm, dyv, ld_sem.at[1])
    for s in range(2):
        ld_f[s].start()
    ld_y.start()
    ld_x.start()

    wall[r, rows16(c * WIDTH, WIDTH)] = attn_w[...].T.astype(BF)
    nbuf[r, c] = jnp.zeros((1, LANES), F32)
    nbuf[r, c, :, 0:WIDTH] = norm_w[...].astype(BF).astype(F32)
    pl.semaphore_wait(barrier, COLS + 2)

    def norm_one(j):
        return remote(nbuf.at[r, c], nbuf.at[r, c], na_s.at[j], na_r.at[j], dev_row(j))

    def norm_two(i):
        return remote(nbuf.at[r], nbuf.at[r], na_s.at[COLS + i], na_r.at[COLS + i], (dev_x, dev_y, dev_d)[i])

    def a_rows(j, p):
        start = (zat(j) * 2 + k) * WIDTH
        if p is None:
            return rows16(start, WIDTH)
        return rows16(start + PART_ROWS[0] * p, PART_ROWS[p])

    def gather_ops(piece, part, far_piece, far_dev, ss, rs):
        def cz(j):
            return remote(piece(r, 0), far_piece(j), ss.at[0, j], rs.at[0, j], far_dev(j))

        def cx(j):
            return remote(piece(r, j), piece(r, j), ss.at[1, j], rs.at[1, j], dev_x)

        def cy(j):
            return remote(piece(r, j), piece(r, j), ss.at[2, j], rs.at[2, j], dev_y)

        def cd0(j):
            return remote(part(rx, j, 0), part(rx, j, 0), ss.at[3, j], rs.at[3, j], dev_y)

        def cd1(j):
            return remote(part(ry, j, 1), part(ry, j, 1), ss.at[4, j], rs.at[4, j], dev_x)

        return cz, cx, cy, cd0, cd1

    az, ax, ay, ad0, ad1 = gather_ops(
        lambda rr, j: wall.at[rr, a_rows(j, None)],
        lambda rr, j, p: wall.at[rr, a_rows(j, p)],
        lambda j: wall.at[r, a_rows(0, None)],
        dev_z, ag_s, ag_r,
    )
    fz, fx, fy, fd0, fd1 = gather_ops(
        lambda rr, i: fw.at[:, rr, :, pl.ds(i * D, D)],
        lambda rr, i, p: fw.at[p, rr, :, pl.ds(i * D, D)],
        lambda i: fw.at[:, r, :, pl.ds(D, D)],
        lambda i: dev_z(2), fg_s, fg_r,
    )

    def sib(j):
        ref = wall.at[:, a_rows(j, None)]
        return remote(ref, ref, sib_s.at[j], sib_r.at[j], dev_sib)

    for j in (1, 2, 3):
        az(j).start()
    ax(0).start()
    ay(0).start()
    for j in range(1, COLS):
        norm_one(j).start()

    for s in range(2):
        ld_f[s].wait()
        fw[s, r, :, 0:D] = acc[0, s, 0:FEATURES].astype(BF)
    ld_y.wait()

    def make_bias(m, _):
        across = jnp.broadcast_to(ids[pl.ds(m, 1)].astype(F32), (LENGTH, LENGTH))
        bias[m] = jnp.where(across == across.T, 0.0, MASKED)
        tdy[owner(0, 0), pl.ds(m * LENGTH, LENGTH)] = dyv[m].astype(BF)
        return 0

    lax.fori_loop(0, MB, make_bias, 0)

    def tok_copy(q, n, m, dev, whose):
        ref = (tdy, tn2)[q].at[whose, pl.ds(m * LENGTH, LENGTH)]
        return remote(ref, ref, tok_s.at[q, n, m], tok_r.at[q, n, m], dev)

    def tok_sib(q, m):
        return tok_copy(q, 0, m, dev_sib, owner(0, 0))

    def tok_far(q, m):
        return tok_copy(q, 1, m, dev_z(1), owner(0, 0))

    def tok_fwd(q, m):
        return tok_copy(q, 2, m, dev_sib, owner(1, 0))

    for m in range(MB):
        tok_sib(0, m).start()

    for j in range(1, COLS):
        norm_one(j).wait_recv()
    for i in range(3):
        norm_two(i).start()
    ax(0).wait_recv()
    ad0(0).start()
    ay(0).wait_recv()
    ad1(0).start()
    for j in (1, 2, 3):
        az(j).wait_recv()
        ax(j).start()
        ay(j).start()
    fz(1).start()
    for m in range(MB):
        tok_far(0, m).start()
    for j in (1, 2, 3):
        ax(j).wait_recv()
        ad0(j).start()
        ay(j).wait_recv()
        ad1(j).start()
    fx(0).start()
    fy(0).start()
    for i in range(3):
        norm_two(i).wait_recv()

    vectors = None
    for cc in range(COLS):
        shard = jnp.concatenate([nbuf[:, cc, 0, :], jnp.zeros((ROWS, D - LANES), F32)], axis=1)
        shard = pltpu.roll(shard, cc * WIDTH, 1) if cc else shard
        vectors = shard if vectors is None else vectors + shard
    gain_one, shift_one, gain_two, shift_two = [vectors[i : i + 1] for i in range(4)]

    ld_x.wait()

    def first_norm(m, _):
        normal, _inv = ln_stats(ig[m])
        n1[m] = (normal * gain_one + shift_one).astype(BF)
        return 0

    lax.fori_loop(0, MB, first_norm, 0)

    for j in range(Z_SIZE):
        ad0(j).wait_recv()
        ad1(j).wait_recv()
        sib(j).start()
    for j in range(Z_SIZE):
        sib(j).wait_recv()

    def project(i, _):
        m, p = i // 3, i % 3
        qkv[m, p] = dot_nt(n1[m], wall[p]).astype(BF)
        return 0

    lax.fori_loop(0, 3 * MB, project, 0)

    lane_head = lax.broadcasted_iota(jnp.int32, (1, LANES), 1) // HD
    head_mask = [jnp.where(lane_head == h, 1.0, 0.0).astype(BF) for h in range(HEADS_TILE)]
    scale = HD ** (-0.5)
    log2_scale = scale * math.log2(math.e)

    def at_step(it, i, fn):
        @pl.when(it == i)
        def _():
            fn()

    def gather_xy(j):
        fz(j).wait_recv()
        fx(j).start()
        fy(j).start()

    def gather_diag(j):
        fx(j).wait_recv()
        fd0(j).start()
        fy(j).wait_recv()
        fd1(j).start()

    def save_probs(it):
        return pltpu.make_async_copy(abuf.at[it % 2], probs_hbm.at[it], pb_sem.at[it % 2])

    def load_probs(it, where):
        return pltpu.make_async_copy(probs_hbm.at[where], abuf.at[it % 2], pb_sem.at[2 + it % 2])

    def second_norm(m):
        hidden = ig[m] + dot_nt(obuf[m], wall[3])
        yout[m] = hidden
        normal, _inv = ln_stats(hidden)
        tn2[owner(0, 0), pl.ds(m * LENGTH, LENGTH)] = (normal * gain_two + shift_two).astype(BF)
        tok_far(1, m).start()
        tok_sib(1, m).start()

    def forward_group(it, _):
        m, g = it // GROUPS, it % GROUPS
        at_step(it, 5, lambda: gather_diag(0))
        at_step(it, 9, lambda: gather_xy(1))
        slot = it % 2

        @pl.when(it >= 2)
        def _():
            save_probs(it - 2).wait()

        lanes = pl.ds(pl.multiple_of(g * LANES, LANES), LANES)
        q = qkv[m, 0, :, lanes]
        kk = qkv[m, 1, :, lanes]
        v = qkv[m, 2, :, lanes]
        mask_bias = bias[m]
        mixed = None
        for h in range(HEADS_TILE):
            scores = dot_nt(q * head_mask[h], kk) * log2_scale + mask_bias
            row_max = jnp.max(scores, axis=-1, keepdims=True)
            expo = jnp.exp2(scores - row_max)
            total = jnp.sum(expo, axis=-1, keepdims=True)
            probs = (expo * (1.0 / total)).astype(BF)
            abuf[slot, h] = probs
            part = dot_nn(probs, v * head_mask[h])
            mixed = part if mixed is None else mixed + part
        obuf[m, :, lanes] = mixed.astype(BF)
        save_probs(it).start()

        @pl.when(g == GROUPS - 1)
        def _():
            second_norm(m)

        return 0

    lax.fori_loop(0, MB * GROUPS, forward_group, 0)
    save_probs(MB * GROUPS - 2).wait()
    save_probs(MB * GROUPS - 1).wait()
    for m in range(MB):
        tok_far(0, m).wait_recv()
        tok_fwd(0, m).start()

    def scatter_ops(block, r1, r2, ss, rs):
        def one(u, p, b):
            dev = dev_y if p == 0 else dev_x
            rr = rd if b == 1 else (ry if p == 0 else rx)
            return remote(block(rr, u, p), r1(u, p, b), ss.at[2 * p + b, u], rs.at[2 * p + b, u], dev)

        def two(u, p):
            dev = dev_x if p == 0 else dev_y
            rr = rx if p == 0 else ry
            return remote(block(rr, u, p), r2(u, p), ss.at[4 + p, u], rs.at[4 + p, u], dev)

        def start_one(u):
            for p in range(2):
                for b in (1, 0):
                    one(u, p, b).start()

        def start_two(u):
            for p in range(2):
                one(u, p, 0).wait_recv()
                one(u, p, 1).wait_recv()
                mine = block(rx if p == 0 else ry, u, p)
                mine[...] = (mine[...].astype(F32) + r1(u, p, 1)[...].astype(F32)).astype(BF)
                two(u, p).start()

        def own_sum(u, p):
            two(u, p).wait_recv()
            return (
                block(r, u, p)[...].astype(F32)
                + r1(u, p, 0)[...].astype(F32)
                + r2(u, p)[...].astype(F32)
            )

        def drain(u):
            for p in range(2):
                one(u, p, 0).wait_send()
                one(u, p, 1).wait_send()
                two(u, p).wait_send()

        return start_one, start_two, own_sum, drain

    def unit_lanes(u):
        return pl.ds(UNITS[u][0], UNITS[u][1])

    f_one, f_two, f_sum, f_drain = scatter_ops(
        lambda rr, u, p: fw.at[p, rr, :, unit_lanes(u)],
        lambda u, p, b: fr1.at[p, b, :, unit_lanes(u)],
        lambda u, p: fr2.at[p, :, unit_lanes(u)],
        frs_s, frs_r,
    )

    def f_far(p):
        return remote(fw.at[p, r, :, unit_lanes(2)], fr3.at[p], frs_s.at[6 + p, 2], frs_r.at[6 + p, 2], dev_z(2))

    def f_three():
        for p in range(2):
            fw[p, r, :, unit_lanes(2)] = f_sum(2, p).astype(BF)
            f_far(p).start()

    def g_rows(zz, p, parity):
        start = (zz * 2 + parity) * WIDTH
        if p is None:
            return rows16(start, WIDTH)
        return rows16(start + PART_ROWS[0] * p, PART_ROWS[p])

    def part_rows(p):
        return pl.ds(PART_ROWS[0] * p, PART_ROWS[p])

    a_one, a_two, a_sum, a_drain = scatter_ops(
        lambda rr, zz, p: wgrad.at[rr, g_rows(zz, p, k)],
        lambda zz, p, b: ar1.at[zz, b, part_rows(p)],
        lambda zz, p: ar2.at[zz, part_rows(p)],
        ars_s, ars_r,
    )

    def a_far(zz, j):
        return remote(wgrad.at[r, g_rows(zz, None, k)], ar3.at[j - 1], ars_s.at[6, j], ars_r.at[6, j], (r, zz * 2 + k))

    def a_three(zz):
        total = [a_sum(zz, p) for p in range(2)]

        @pl.when(z == zz)
        def _():
            for p in range(2):
                agrad[part_rows(p)] = total[p]

        @pl.when(z != zz)
        def _():
            for p in range(2):
                wgrad[r, g_rows(zz, p, k)] = total[p].astype(BF)
            a_far(zz, exclusive(z, zz)).start()

    def cross(zz):
        return remote(wgrad.at[:, g_rows(zz, None, 1 - k)], rc.at[zz], rc_s.at[zz], rc_r.at[zz], dev_sib)

    def a_start(zz):
        cross(zz).wait_recv()
        for rr in range(ROWS):
            mine = wgrad.at[rr, g_rows(zz, None, k)]
            mine[...] = (mine[...].astype(F32) + rc[zz, rr].astype(F32)).astype(BF)
        a_one(zz)

    def ffn_tile(i, t):
        first, width = CHUNKS[i]
        up = fw[0, :, :, first : first + width].reshape(D, width)
        down = fw[1, :, :, first : first + width].reshape(D, width)
        act, slope = gelu_pair(dot_nn(tn2[t], up))
        grad_act = dot_nn(tdy[t], down)
        act = act.astype(BF)
        grad_up = (grad_act * slope).astype(BF)
        gb[t, :, 0:width] = act
        dub[t, :, 0:width] = grad_up
        dn_part = dot_nt(grad_up, up)
        y_part = dot_nt(act, down)
        if i == 0:
            acc[0, t] = dn_part
            acc[1, t] = y_part
        else:
            acc[0, t] += dn_part
            acc[1, t] += y_part

    def weight_grads(i):
        first, width = CHUNKS[i]
        for p, (left, right) in enumerate(((tn2, dub), (tdy, gb))):
            grad = dot_tn(left[...].reshape(4 * MB * LENGTH, D), right[:, :, 0:width].reshape(4 * MB * LENGTH, width))
            fw[p, :, :, first : first + width] = grad.astype(BF).reshape(ROWS, FEATURES, width)

    fd0(0).wait_recv()
    fd1(0).wait_recv()

    def first_block(s, _):
        def sib_tiles():
            for q in range(2):
                for m in range(MB):
                    tok_sib(q, m).wait_recv()

        def far_tiles():
            for m in range(MB):
                tok_far(1, m).wait_recv()
                tok_fwd(1, m).start()

        def fwd_tiles():
            for q in range(2):
                for m in range(MB):
                    tok_fwd(q, m).wait_recv()

        at_step(s, 1, sib_tiles)
        at_step(s, 2, far_tiles)
        at_step(s, 3, fwd_tiles)
        at_step(s, 3, lambda: gather_diag(1))
        ffn_tile(0, owner(s // 2, s % 2))
        return 0

    lax.fori_loop(0, 4, first_block, 0)
    fz(1).wait_send()
    for op in (fx, fy, fd0, fd1):
        op(0).wait_send()
    weight_grads(0)
    f_one(0)
    fd0(1).wait_recv()
    fd1(1).wait_recv()

    def part_sib(q, n):
        return remote(acc.at[q, owner(n, 1)], near.at[q, n], part_s.at[q, n], part_r.at[q, n], dev_sib)

    def part_far(q, m):
        return remote(stage.at[q, m], far.at[q, m], part_s.at[q, 2 + m], part_r.at[q, 2 + m], dev_z(1))

    def to_far(q):
        part_sib(q, 1).wait_recv()
        for m in range(MB):
            rows = pl.ds(m * LENGTH, LENGTH)
            stage[q, m] = (acc[q, owner(1, 0), rows] + near[q, 1, rows]).astype(BF)
            part_far(q, m).start()

    def second_block(s, _):
        ffn_tile(1, owner(1 - s // 2, 1 - s % 2))
        for n in range(2):

            def to_sib(n=n):
                part_sib(0, n).start()
                part_sib(1, n).start()

            at_step(s, 2 * (1 - n), to_sib)
        at_step(s, 1, lambda: to_far(0))
        at_step(s, 2, lambda: f_two(0))
        at_step(s, 3, lambda: to_far(1))
        return 0

    lax.fori_loop(0, 4, second_block, 0)
    for op in (fx, fy, fd0, fd1):
        op(1).wait_send()
    weight_grads(1)
    f_one(2)
    f_one(1)

    zero = jnp.zeros((1, D), F32)
    for m in range(MB):
        tok_far(1, m).wait_send()
        tok_sib(1, m).wait_send()
    part_sib(0, 0).wait_recv()

    def whole(q, m):
        rows = pl.ds(m * LENGTH, LENGTH)
        return acc[q, owner(0, 0), rows] + near[q, 0, rows] + far[q, m].astype(F32)

    def second_backward(m):
        part_far(0, m).wait_recv()
        normal, inv = ln_stats(yout[m])
        grad = whole(0, m)
        grad_hidden = dyv[m] + ln_backward(normal, inv, gain_two, grad)
        dyv[m] = grad_hidden
        low = grad_hidden.astype(BF)
        dob[m] = dot_nn(low, wall[3]).astype(BF)
        tn2[owner(0, 0), pl.ds(m * LENGTH, LENGTH)] = low
        nsum[pl.ds(2, 1)] += jnp.sum(grad * normal, axis=0, keepdims=True)
        nsum[pl.ds(3, 1)] += jnp.sum(grad, axis=0, keepdims=True)

    nsum[...] = jnp.zeros(nsum.shape, F32)
    load_probs(0, 0).start()
    second_backward(0)

    def backward_at(it):
        m = jnp.where(it < 6, it // 3, it % 2)
        g = jnp.where(it < 6, it % 3, it // 2)
        return m, g

    def group_grads(g):
        lanes = pl.ds(pl.multiple_of(g * LANES, LANES), LANES)
        for p in range(3):
            grad = dot_tn(qkv[0, p, :, lanes], n1[0]) + dot_tn(qkv[1, p, :, lanes], n1[1])
            wgrad[p, lanes] = grad.astype(BF)

    def backward_group(it, _):
        m, g = backward_at(it)

        @pl.when(it == 3)
        def _():
            second_backward(1)
            rows = [tn2[owner(0, 0), pl.ds(i * LENGTH, LENGTH)] for i in range(MB)]
            wgrad[3] = (dot_tn(rows[0], obuf[0]) + dot_tn(rows[1], obuf[1])).astype(BF)

        at_step(it, 5, lambda: f_two(2))
        at_step(it, 6, lambda: f_two(1))
        at_step(it, 6, lambda: a_start(0))
        at_step(it, 7, lambda: a_start(1))
        at_step(it, 8, lambda: a_two(0))
        at_step(it, 9, lambda: a_two(1))
        at_step(it, 9, lambda: a_start(2))
        at_step(it, 9, f_three)
        slot = it % 2

        @pl.when(it + 1 < MB * GROUPS)
        def _():
            m_next, g_next = backward_at(it + 1)
            load_probs(it + 1, m_next * GROUPS + g_next).start()

        load_probs(it, m * GROUPS + g).wait()
        lanes = pl.ds(pl.multiple_of(g * LANES, LANES), LANES)
        q = qkv[m, 0, :, lanes]
        kk = qkv[m, 1, :, lanes]
        v = qkv[m, 2, :, lanes]
        do = dob[m, :, lanes]
        q_turned = q.T
        do_turned = do.T
        grad_q = None
        grad_k = []
        grad_v = []
        for h in range(HEADS_TILE):
            probs = abuf[slot, h]
            wide = probs.astype(F32)
            grad_probs = dot_nt(do * head_mask[h], v)
            product = grad_probs * wide
            row = jnp.sum(product, axis=-1, keepdims=True)
            grad_scores = (product - wide * row).astype(BF)
            part = dot_nn(grad_scores, kk * head_mask[h])
            grad_q = part if grad_q is None else grad_q + part
            grad_v.append(dot_nn(do_turned[h * HD : (h + 1) * HD], probs))
            grad_k.append(dot_nn(q_turned[h * HD : (h + 1) * HD], grad_scores))
        qkv[m, 0, :, lanes] = (grad_q * scale).astype(BF)
        qkv[m, 1, :, lanes] = (jnp.concatenate(grad_k, axis=0).T * scale).astype(BF)
        qkv[m, 2, :, lanes] = jnp.concatenate(grad_v, axis=0).T.astype(BF)

        @pl.when(m == 1)
        def _():
            group_grads(g)

        at_step(it, 4, lambda: cross(0).start())
        at_step(it, 5, lambda: cross(1).start())
        at_step(it, 7, lambda: cross(2).start())
        at_step(it, 9, lambda: cross(3).start())
        return 0

    lax.fori_loop(0, MB * GROUPS, backward_group, 0)

    def first_backward(m):
        grad = dot_nn(qkv[m, 0], wall[0]) + dot_nn(qkv[m, 1], wall[1]) + dot_nn(qkv[m, 2], wall[2])
        normal, inv = ln_stats(ig[m])
        ig[m] = dyv[m] + ln_backward(normal, inv, gain_one, grad)
        nsum[pl.ds(0, 1)] += jnp.sum(grad * normal, axis=0, keepdims=True)
        nsum[pl.ds(1, 1)] += jnp.sum(grad, axis=0, keepdims=True)

    a_three(0)
    a_start(3)
    first_backward(0)
    a_two(2)
    first_backward(1)

    sums = nsum[...]
    lane_own = lax.broadcasted_iota(jnp.int32, (8, LANES), 1) < WIDTH
    for cc in range(COLS):
        shard = pltpu.roll(sums, D - cc * WIDTH, 1) if cc else sums
        shard = jnp.where(lane_own, shard[:, 0:LANES], 0.0)
        for rr in range(ROWS):
            ngrad[rr, cc] = shard[rr : rr + 1]

    def grad_rows(i):
        rr = (rx, ry, rd)[i]
        return remote(ngrad.at[rr], nr1.at[i], nb_s.at[i], nb_r.at[i], (dev_x, dev_y, dev_d)[i])

    def grad_cols(j):
        col = zat(j // 2) * 2 + (k + j % 2) % 2
        return remote(ngrad.at[r, col], nr2.at[j - 1], nb_s.at[2 + j], nb_r.at[2 + j], dev_row(j))

    for i in range(3):
        grad_rows(i).start()
    a_three(1)
    a_two(3)
    a_three(2)
    for i in range(3):
        grad_rows(i).wait_recv()
    ngrad[r] = ngrad[r] + nr1[0] + nr1[1] + nr1[2]
    for j in range(1, COLS):
        grad_cols(j).start()

    part_sib(1, 0).wait_recv()
    for m in range(MB):
        part_far(1, m).wait_recv()
        yout[m] = yout[m] + whole(1, m)

    a_three(3)
    for p in range(2):
        for u in range(2):
            total = f_sum(u, p)
            if u == 0:
                f_far(p).wait_recv()
            fgrad[p, :, unit_lanes(u)] = total + fr3[p, :, unit_lanes(u)].astype(F32)
    total = ngrad[r, c]
    for j in range(1, COLS):
        grad_cols(j).wait_recv()
        total = total + nr2[j - 1]
    nout[...] = total
    for j in (1, 2, 3):
        a_far(z, j).wait_recv()
    agrad[...] = agrad[...] + ar3[0].astype(F32) + ar3[1].astype(F32) + ar3[2].astype(F32)

    for j in (1, 2, 3):
        az(j).wait_send()
        a_far(z, j).wait_send()
    for j in range(Z_SIZE):
        for op in (ax, ay, ad0, ad1, sib, cross):
            op(j).wait_send()
        a_drain(j)
    for u in range(3):
        f_drain(u)
    for p in range(2):
        f_far(p).wait_send()
    for m in range(MB):
        tok_sib(0, m).wait_send()
        tok_far(0, m).wait_send()
        for q in range(2):
            tok_fwd(q, m).wait_send()
            part_far(q, m).wait_send()
            part_sib(q, m).wait_send()
    for j in range(1, COLS):
        norm_one(j).wait_send()
        grad_cols(j).wait_send()
    for i in range(3):
        norm_two(i).wait_send()
        grad_rows(i).wait_send()


def run_step(x, dy, ids, attn_w, norm_w, ffn_w):
    vm = pltpu.VMEM
    dma = pltpu.SemaphoreType.DMA
    any_spec = pl.BlockSpec(memory_space=pl.ANY)
    vspec = pl.BlockSpec(memory_space=pltpu.VMEM)
    tokens = MB * LENGTH
    return pl.pallas_call(
        step_kernel,
        out_shape=(
            jax.ShapeDtypeStruct((MB, LENGTH, D), F32),
            jax.ShapeDtypeStruct((MB, LENGTH, D), F32),
            jax.ShapeDtypeStruct((2, FEATURES, D), F32),
            jax.ShapeDtypeStruct((WIDTH, D), F32),
            jax.ShapeDtypeStruct((1, LANES), F32),
            jax.ShapeDtypeStruct((MB * GROUPS, HEADS_TILE, LENGTH, LENGTH), BF),
        ),
        in_specs=[any_spec, any_spec, any_spec, vspec, vspec, vspec],
        out_specs=(vspec, vspec, vspec, vspec, vspec, any_spec),
        scratch_shapes=[
            vm((ROWS, D, D), BF),
            vm((ROWS, D, D), BF),
            vm((2, ROWS, FEATURES, 2 * D), BF),
            vm((MB, LENGTH, D), BF),
            vm((MB, 3, LENGTH, D), BF),
            vm((2, HEADS_TILE, LENGTH, LENGTH), BF),
            vm((MB, LENGTH, D), BF),
            vm((4, tokens, D), BF),
            vm((4, tokens, D), BF),
            vm((4, tokens, CHUNKS[1][1]), BF),
            vm((4, tokens, CHUNKS[1][1]), BF),
            vm((2, 4, tokens, D), F32),
            vm((2, 2, tokens, D), F32),
            vm((2, MB, LENGTH, D), BF),
            vm((2, MB, LENGTH, D), BF),
            vm((MB, LENGTH, D), F32),
            vm((2, 2, FEATURES, 2 * D), BF),
            vm((2, FEATURES, 2 * D), BF),
            vm((2, FEATURES, D), BF),
            vm((Z_SIZE, ROWS, WIDTH, D), BF),
            vm((Z_SIZE, 2, WIDTH, D), BF),
            vm((Z_SIZE, WIDTH, D), BF),
            vm((Z_SIZE - 1, WIDTH, D), BF),
            vm((MB, LENGTH, LENGTH), F32),
            vm((MB, LENGTH, D), BF),
            vm((ROWS, COLS, 1, LANES), F32),
            vm((ROWS, COLS, 1, LANES), F32),
            vm((8, D), F32),
            vm((3, COLS, 1, LANES), F32),
            vm((COLS - 1, 1, LANES), F32),
            dma((4,)), dma((4,)),
            dma((5, Z_SIZE)), dma((5, Z_SIZE)),
            dma((5, 2)), dma((5, 2)),
            dma((Z_SIZE,)), dma((Z_SIZE,)),
            dma((2, 3, MB)), dma((2, 3, MB)),
            dma((2, 4)), dma((2, 4)),
            dma((8, 3)), dma((8, 3)),
            dma((7, Z_SIZE)), dma((7, Z_SIZE)),
            dma((Z_SIZE,)), dma((Z_SIZE,)),
            dma((COLS + 3,)), dma((COLS + 3,)),
            dma((COLS + 2,)), dma((COLS + 2,)),
        ],
        compiler_params=pltpu.CompilerParams(
            collective_id=0, has_side_effects=True, vmem_limit_bytes=64 * 1024 * 1024 - 4096
        ),
        name="encoder_step",
    )(x, dy, ffn_w, ids, attn_w, norm_w)


def local_slice(
    block_input, output_grad, sequence_ids,
    attn_weights, attn_momentum, attn_average,
    norm_params, norm_momentum, norm_average,
    ffn_weights, ffn_momentum, ffn_average,
):
    outputs, grads, ffn_grad, shard, norm_shard, _probs = run_step(
        block_input, output_grad, sequence_ids, attn_weights, norm_params[None], ffn_weights
    )
    attn_grad = shard.T
    norm_grad = norm_shard[0, :WIDTH]
    total_tokens = MB * block_input.shape[1] * lax.axis_size("row") * lax.axis_size("col")
    step_rate = RATE_SCALE * total_tokens ** (-0.5)
    attn = sgd_update(attn_weights, attn_momentum, attn_average, attn_grad, step_rate)
    norm = sgd_update(norm_params, norm_momentum, norm_average, norm_grad, step_rate)
    ffn = sgd_update(ffn_weights, ffn_momentum, ffn_average, ffn_grad, step_rate)
    return (outputs, grads, attn_grad, *attn, norm_grad, *norm, ffn_grad, *ffn)


def local(*args):
    on_slice = (
        lax.axis_size("row") == ROWS
        and lax.axis_size("col") == COLS
        and args[0].shape[1] == LENGTH
        and args[3].shape == (D, WIDTH)
        and args[9].shape == (2, FEATURES, D)
    )
    return (local_slice if on_slice else local_general)(*args)


def solution(mesh):
    return jax.shard_map(
        local,
        mesh=mesh,
        in_specs=(
            P(None, ("row", "col"), None),
            P(None, ("row", "col"), None),
            P(None, ("row", "col")),
            P(None, ("row", "col")),
            P(None, ("row", "col")),
            P(None, ("row", "col")),
            P(("row", "col")),
            P(("row", "col")),
            P(("row", "col")),
            P(None, "row", "col"),
            P(None, "row", "col"),
            P(None, "row", "col"),
        ),
        out_specs=(
            P(None, ("row", "col"), None),
            P(None, ("row", "col"), None),
            P(None, ("row", "col")),
            P(None, ("row", "col")),
            P(None, ("row", "col")),
            P(None, ("row", "col")),
            P(None, ("row", "col")),
            P(("row", "col")),
            P(("row", "col")),
            P(("row", "col")),
            P(("row", "col")),
            P(("row", "col")),
            P(None, "row", "col"),
            P(None, "row", "col"),
            P(None, "row", "col"),
            P(None, "row", "col"),
            P(None, "row", "col"),
        ),
        check_vma=False,
    )
```

```python
import functools
import math

import jax
import jax.numpy as jnp
from jax import lax
from jax.experimental import pallas as pl
from jax.experimental.pallas import tpu as pltpu
from jax.sharding import PartitionSpec as P

D = 640
H = 20
HD = 32
MB = 2


EPSILON = 1e-05
MOMENT_DECAY = 0.9
AVERAGE_DECAY = 0.85
RATE_SCALE = 0.06
MASKED = -1e30


def layer_norm(values, gain, shift):
    center = values - jnp.mean(values, axis=-1, keepdims=True)
    spread = jnp.mean(center * center, axis=-1, keepdims=True)
    return center * lax.rsqrt(spread + EPSILON) * gain + shift


def gelu_exact(values):
    return jax.nn.gelu(values, approximate=False)


def matmul(left_side, right_side):
    return jnp.dot(left_side, right_side, preferred_element_type=jnp.float32)


def contract_rows(left_side, right_side):
    return lax.dot_general(
        left_side, right_side, (((0,), (0,)), ((), ())), preferred_element_type=jnp.float32
    )


def contract_cols(left_side, right_side):
    return lax.dot_general(
        left_side, right_side, (((1,), (1,)), ((), ())), preferred_element_type=jnp.float32
    )


def head_slices(qkv_low, first_col, head_group):
    length = qkv_low.shape[0]
    group_width = head_group * HD
    queries = lax.dynamic_slice_in_dim(qkv_low, first_col, group_width, 1).reshape(
        length, head_group, HD
    )
    keys_part = lax.dynamic_slice_in_dim(qkv_low, D + first_col, group_width, 1).reshape(
        length, head_group, HD
    )
    values = lax.dynamic_slice_in_dim(qkv_low, 2 * D + first_col, group_width, 1).reshape(
        length, head_group, HD
    )
    return (queries, keys_part, values)


def masked_scores(queries, keys_part, same_seq):
    scores = jnp.einsum(
        "qhe,khe->hqk", queries, keys_part, preferred_element_type=jnp.float32
    ) * HD ** (-0.5)
    return jnp.where(same_seq[None], scores, MASKED)


def attend_forward(qkv_low, same_seq):
    length = qkv_low.shape[0]
    head_group = math.gcd(H, 4)
    group_width = head_group * HD

    def one_group(group_index, state_all):
        mixed_all, maxima, totals = state_all
        first_col = group_index * group_width
        queries, keys_part, values = head_slices(qkv_low, first_col, head_group)
        scores = masked_scores(queries, keys_part, same_seq)
        row_max = jnp.max(scores, axis=-1, keepdims=True)
        exponent = jnp.exp(scores - row_max)
        row_total = jnp.sum(exponent, axis=-1, keepdims=True)
        attn_probs = (exponent / row_total).astype(jnp.bfloat16)
        mixed_rows = jnp.einsum(
            "hqk,khe->qhe", attn_probs, values, preferred_element_type=jnp.float32
        )
        mixed_all = lax.dynamic_update_slice_in_dim(
            mixed_all, mixed_rows.reshape(length, group_width), first_col, 1
        )
        maxima = lax.dynamic_update_slice_in_dim(
            maxima, row_max[:, :, 0], group_index * head_group, 0
        )
        totals = lax.dynamic_update_slice_in_dim(
            totals, row_total[:, :, 0], group_index * head_group, 0
        )
        return (mixed_all, maxima, totals)

    initial = (
        jnp.zeros((length, D), jnp.float32),
        jnp.zeros((H, length), jnp.float32),
        jnp.zeros((H, length), jnp.float32),
    )
    return lax.fori_loop(0, H // head_group, one_group, initial)


def attend_backward(qkv_low, same_seq, maxima, totals, grad_mixed):
    length = qkv_low.shape[0]
    head_group = math.gcd(H, 4)
    group_width = head_group * HD

    def one_group(group_index, grad_qkv):
        first_col = group_index * group_width
        queries, keys_part, values = head_slices(qkv_low, first_col, head_group)
        grad_part = lax.dynamic_slice_in_dim(grad_mixed, first_col, group_width, 1).reshape(
            length, head_group, HD
        )
        scores = masked_scores(queries, keys_part, same_seq)
        row_max = lax.dynamic_slice_in_dim(maxima, group_index * head_group, head_group, 0)[
            :, :, None
        ]
        row_total = lax.dynamic_slice_in_dim(totals, group_index * head_group, head_group, 0)[
            :, :, None
        ]
        attn_probs = jnp.exp(scores - row_max) / row_total
        grad_probs = jnp.einsum(
            "qhe,khe->hqk", grad_part, values, preferred_element_type=jnp.float32
        )
        grad_values = jnp.einsum(
            "hqk,qhe->khe",
            attn_probs.astype(jnp.bfloat16),
            grad_part,
            preferred_element_type=jnp.float32,
        )
        grad_scores = attn_probs * (
            grad_probs - jnp.sum(grad_probs * attn_probs, axis=-1, keepdims=True)
        )
        grad_scores = grad_scores.astype(jnp.bfloat16)
        grad_queries = jnp.einsum(
            "hqk,khe->qhe", grad_scores, keys_part, preferred_element_type=jnp.float32
        ) * HD ** (-0.5)
        grad_keys = jnp.einsum(
            "hqk,qhe->khe", grad_scores, queries, preferred_element_type=jnp.float32
        ) * HD ** (-0.5)
        for offset, grad_piece in ((0, grad_queries), (D, grad_keys), (2 * D, grad_values)):
            grad_qkv = lax.dynamic_update_slice_in_dim(
                grad_qkv, grad_piece.reshape(length, group_width), offset + first_col, 1
            )
        return grad_qkv

    return lax.fori_loop(0, H // head_group, one_group, jnp.zeros((length, 3 * D), jnp.float32))


def sgd_update(weights_old, moment, average, grad_sum, step_rate):
    moment_new = MOMENT_DECAY * moment + grad_sum
    weights_new = weights_old - step_rate * (grad_sum + MOMENT_DECAY * moment_new)
    average_new = AVERAGE_DECAY * average + (1.0 - AVERAGE_DECAY) * weights_new
    return (moment_new, weights_new, average_new, weights_new.astype(jnp.bfloat16))


def local_general(
    block_input,
    output_grad,
    sequence_ids,
    attn_weights,
    attn_momentum,
    attn_average,
    norm_params,
    norm_momentum,
    norm_average,
    ffn_weights,
    ffn_momentum,
    ffn_average,
):
    attn_full, norm_full = (
        lax.all_gather(attn_weights.astype(jnp.bfloat16), ("row", "col"), axis=1, tiled=True),
        lax.all_gather(norm_params.astype(jnp.bfloat16), ("row", "col"), axis=0, tiled=True),
    )
    norm_values = norm_full.astype(jnp.float32)
    gain_one = norm_values[:D]
    shift_one = norm_values[D : 2 * D]
    gain_two = norm_values[2 * D : 3 * D]
    shift_two = norm_values[3 * D :]
    qkv_weights = attn_full[:, : 3 * D]
    out_weights = attn_full[:, 3 * D :]
    ffn_rows = lax.all_gather(ffn_weights.astype(jnp.bfloat16), "row", axis=1, tiled=True)
    col_width = ffn_weights.shape[2]
    length = block_input.shape[1]
    attn_acc = jnp.zeros((D, 4 * D), jnp.float32)
    norm_acc = jnp.zeros((4 * D,), jnp.float32)
    ffn_acc = jnp.zeros((2, D, col_width), jnp.float32)
    outputs_all = []
    grads_all = []
    for micro_step in range(MB):
        inputs = block_input[micro_step]
        ids_row = sequence_ids[micro_step]
        same_seq = ids_row[:, None] == ids_row[None, :]
        normed, pull_one = jax.vjp(layer_norm, inputs, gain_one, shift_one)
        normed_low = normed.astype(jnp.bfloat16)
        qkv_low = matmul(normed_low, qkv_weights).astype(jnp.bfloat16)
        mixed_all, maxima, totals = attend_forward(qkv_low, same_seq)
        mixed_low = mixed_all.astype(jnp.bfloat16)
        hidden_in = inputs + matmul(mixed_low, out_weights)
        normed_two, pull_two = jax.vjp(layer_norm, hidden_in, gain_two, shift_two)
        normed_two_low = normed_two.astype(jnp.bfloat16)
        grad_out = output_grad[micro_step]
        grad_out_low = grad_out.astype(jnp.bfloat16)
        normed_all = lax.all_gather(normed_two_low, "col", axis=0, tiled=True)
        up_proj = matmul(normed_all, ffn_rows[0])
        activation, pull_gelu = jax.vjp(gelu_exact, up_proj)
        activ_low = activation.astype(jnp.bfloat16)
        ffn_out = lax.psum_scatter(
            contract_cols(activ_low, ffn_rows[1]).astype(jnp.bfloat16),
            "col",
            scatter_dimension=0,
            tiled=True,
        ).astype(jnp.float32)
        grad_all = lax.all_gather(grad_out_low, "col", axis=0, tiled=True)
        grad_act = matmul(grad_all, ffn_rows[1])
        grad_up = pull_gelu(grad_act)[0].astype(jnp.bfloat16)
        grad_normed_two = lax.psum_scatter(
            contract_cols(grad_up, ffn_rows[0]).astype(jnp.bfloat16),
            "col",
            scatter_dimension=0,
            tiled=True,
        ).astype(jnp.float32)
        ffn_acc = ffn_acc + jnp.stack(
            [contract_rows(normed_all, grad_up), contract_rows(grad_all, activ_low)]
        )
        outputs_all.append(hidden_in + ffn_out)
        grad_ln_two, gain_two_grad, shift_two_grad = pull_two(grad_normed_two)
        grad_hidden = grad_out + grad_ln_two
        grad_branch_low = grad_hidden.astype(jnp.bfloat16)
        out_proj_grad = contract_rows(mixed_low, grad_branch_low)
        grad_mixed_low = contract_cols(grad_branch_low, out_weights).astype(jnp.bfloat16)
        grad_qkv_low = attend_backward(qkv_low, same_seq, maxima, totals, grad_mixed_low).astype(
            jnp.bfloat16
        )
        qkv_grad = contract_rows(normed_low, grad_qkv_low)
        grad_normed = contract_cols(grad_qkv_low, qkv_weights)
        grad_ln_one, gain_one_grad, shift_one_grad = pull_one(grad_normed)
        grads_all.append(grad_hidden + grad_ln_one)
        attn_acc = attn_acc + jnp.concatenate([qkv_grad, out_proj_grad], axis=1)
        norm_acc = norm_acc + jnp.concatenate(
            [gain_one_grad, shift_one_grad, gain_two_grad, shift_two_grad]
        )
    ffn_grad = lax.psum_scatter(
        ffn_acc.astype(jnp.bfloat16), "row", scatter_dimension=1, tiled=True
    ).astype(jnp.float32)
    attn_grad, norm_grad = (
        lax.psum_scatter(attn_acc, ("row", "col"), scatter_dimension=1, tiled=True),
        lax.psum_scatter(norm_acc, ("row", "col"), scatter_dimension=0, tiled=True),
    )
    total_tokens = MB * length * lax.axis_size("row") * lax.axis_size("col")
    step_rate = RATE_SCALE * total_tokens ** (-0.5)
    attn_moment_new, attn_new, attn_avg_new, attn_copy = sgd_update(
        attn_weights, attn_momentum, attn_average, attn_grad, step_rate
    )
    norm_moment_new, norm_new, norm_avg_new, norm_copy = sgd_update(
        norm_params, norm_momentum, norm_average, norm_grad, step_rate
    )
    ffn_moment_new, ffn_new, ffn_avg_new, ffn_copy = sgd_update(
        ffn_weights, ffn_momentum, ffn_average, ffn_grad, step_rate
    )
    return (
        jnp.stack(outputs_all),
        jnp.stack(grads_all),
        attn_grad,
        attn_moment_new,
        attn_new,
        attn_avg_new,
        attn_copy,
        norm_grad,
        norm_moment_new,
        norm_new,
        norm_avg_new,
        norm_copy,
        ffn_grad,
        ffn_moment_new,
        ffn_new,
        ffn_avg_new,
        ffn_copy,
    )


MESH_ID = pl.DeviceIdType.MESH
BF = jnp.bfloat16
F32 = jnp.float32
LANES = 128
HEADS_TILE = LANES // HD
GROUPS = D // LANES
Z_SIZE = 4
COLS = 2 * Z_SIZE
ROWS = 4
WIDTH = D // COLS
LENGTH = 256
FEATURES = D // ROWS
PART_ROWS = (48, 32)
UNITS = ((0, 512), (512, 128), (640, 256), (896, 256), (1152, 128))
FAR_UNITS = (2, 3, 4)
CHUNKS = ((0, 512), (512, 768))


def dot_nn(a, b):
    return lax.dot_general(a, b, (((1,), (0,)), ((), ())), preferred_element_type=F32)


def dot_nt(a, b):
    return lax.dot_general(a, b, (((1,), (1,)), ((), ())), preferred_element_type=F32)


def dot_tn(a, b):
    return lax.dot_general(a, b, (((0,), (0,)), ((), ())), preferred_element_type=F32)


def ln_stats(values):
    center = values - jnp.mean(values, axis=-1, keepdims=True)
    spread = jnp.mean(center * center, axis=-1, keepdims=True)
    inv = lax.rsqrt(spread + EPSILON)
    return center * inv, inv


def ln_backward(normal, inv, gain, grad):
    scaled = grad * gain
    mean_one = jnp.mean(scaled, axis=-1, keepdims=True)
    mean_two = jnp.mean(scaled * normal, axis=-1, keepdims=True)
    return inv * (scaled - mean_one - normal * mean_two)


def gelu_pair(u):
    size = jnp.abs(u) * (2.0 ** -0.5)
    t = 1.0 / (1.0 + 0.3275911 * size)
    poly = 0.5 * 1.061405429
    for coef in (-1.453152027, 1.421413741, -0.284496736, 0.254829592):
        poly = poly * t + 0.5 * coef
    bell = jnp.exp2(u * u * (-0.5 * math.log2(math.e)))
    tail = poly * t * bell
    cap = jnp.where(u < 0.0, tail, 1.0 - tail)
    return u * cap, cap + u * (bell * (1.0 / math.sqrt(2.0 * math.pi)))


def step_kernel(
    x_hbm, dy_hbm, ffn_hbm, ids, attn_w, norm_w,
    yout_hbm, ig_hbm, fgrad_hbm, agrad_hbm, nout, probs_hbm,
    wall, wgrad, fw, n1, qkv, abuf, obuf, tn2, tdy, gb, dub, acc, near, stage, far, dyv,
    fr1, fr2, fr3, rc, ar1, ar2, ar3, bias, dob, nbuf, ngrad, nsum, nr1, nr2, yout, ig, fgrad, agrad, held,
    ld_sem, pb_sem, out_sem, send, fg_s, ag_r, fg_r, sib_r, tok_r, part_r, frs_r, ars_r, rc_r, norm_r,
):
    r = lax.axis_index("row")
    c = lax.axis_index("col")
    y, x, z, k = r // 2, r % 2, c // 2, c % 2
    rx, ry, rd = y * 2 + (1 - x), (1 - y) * 2 + x, (1 - y) * 2 + (1 - x)
    dev_x = (rx, c)
    dev_y = (ry, c)
    dev_d = (rd, c)
    dev_sib = (r, z * 2 + (1 - k))

    def exclusive(a, b):
        return ((a // 2 + b // 2) % 2) * 2 + (a % 2 + b % 2) % 2

    def zat(j):
        return exclusive(z, j)

    def dev_z(j):
        return (r, zat(j) * 2 + k)

    def dev_row(j):
        return (r, zat(j // 2) * 2 + (k + j % 2) % 2)

    def owner(z_rel, k_rel):
        return ((z + z_rel) % 2) * 2 + (k + k_rel) % 2

    def rows16(start, size):
        return pl.ds(pl.multiple_of(start, 16), size)

    (
        S_GATHER, S_SIB, S_TOK, S_OWN, S_PART, S_FAR, S_F_ONE, S_F_TWO, S_F_FAR,
        S_A_ONE, S_A_TWO, S_A_NEAR, S_A_FAR, S_CROSS, S_N_ONE, S_N_TWO, S_G_ONE, S_G_TWO,
    ) = range(18)

    def sent(i, all_bytes):
        remote(all_bytes, all_bytes, send.at[i], send.at[i], dev_sib).wait_send()

    def received(sem, all_bytes):
        remote(all_bytes, all_bytes, sem, sem, dev_sib).wait_recv()

    def remote(src, dst, ss, rs, dev):
        return pltpu.make_async_remote_copy(
            src_ref=src, dst_ref=dst, send_sem=ss, recv_sem=rs, device_id=dev, device_id_type=MESH_ID
        )

    barrier = pltpu.get_barrier_semaphore()
    for dev in (dev_x, dev_y, dev_d, *[dev_row(j) for j in range(1, COLS)]):
        pl.semaphore_signal(barrier, inc=1, device_id=dev, device_id_type=MESH_ID)

    ld_f = [pltpu.make_async_copy(ffn_hbm.at[s], acc.at[0, s, pl.ds(0, FEATURES)], ld_sem.at[2 + s]) for s in range(2)]
    ld_x = pltpu.make_async_copy(x_hbm, ig, ld_sem.at[0])
    ld_y = pltpu.make_async_copy(dy_hbm, dyv, ld_sem.at[1])
    for s in range(2):
        ld_f[s].start()
    ld_y.start()
    ld_x.start()

    wall[r, rows16(c * WIDTH, WIDTH)] = attn_w[...].astype(BF)
    nbuf[r, c] = jnp.zeros((1, LANES), F32)
    nbuf[r, c, :, 0:WIDTH] = norm_w[...].astype(BF).astype(F32)
    pl.semaphore_wait(barrier, COLS + 2)

    def norm_one(j):
        return remote(nbuf.at[r, c], nbuf.at[r, c], send.at[S_N_ONE], norm_r.at[0], dev_row(j))

    def norm_two(i):
        return remote(nbuf.at[r], nbuf.at[r], send.at[S_N_TWO], norm_r.at[1], (dev_x, dev_y, dev_d)[i])

    def a_rows(j, p):
        start = (zat(j) * 2 + k) * WIDTH
        if p is None:
            return rows16(start, WIDTH)
        return rows16(start + PART_ROWS[0] * p, PART_ROWS[p])

    def gather_ops(piece, part, far_piece, far_dev, ss, rs):
        def cz(j):
            return remote(piece(r, 0), far_piece(j), ss(0, j), rs.at[0, j], far_dev(j))

        def cx(j):
            return remote(piece(r, j), piece(r, j), ss(1, j), rs.at[1, j], dev_x)

        def cy(j):
            return remote(piece(r, j), piece(r, j), ss(2, j), rs.at[2, j], dev_y)

        def cd0(j):
            return remote(part(rx, j, 0), part(rx, j, 0), ss(3, j), rs.at[3, j], dev_y)

        def cd1(j):
            return remote(part(ry, j, 1), part(ry, j, 1), ss(4, j), rs.at[4, j], dev_x)

        return cz, cx, cy, cd0, cd1

    az, ax, ay, ad0, ad1 = gather_ops(
        lambda rr, j: wall.at[rr, a_rows(j, None)],
        lambda rr, j, p: wall.at[rr, a_rows(j, p)],
        lambda j: wall.at[r, a_rows(0, None)],
        dev_z, lambda i, j: send.at[S_GATHER], ag_r,
    )
    fz, fx, fy, fd0, fd1 = gather_ops(
        lambda rr, i: fw.at[:, rr, :, pl.ds(i * D, D)],
        lambda rr, i, p: fw.at[p, rr, :, pl.ds(i * D, D)],
        lambda i: fw.at[:, r, :, pl.ds(D, D)],
        lambda i: dev_z(2), lambda i, j: fg_s.at[i, j], fg_r,
    )

    def sib(j):
        ref = wall.at[:, a_rows(j, None)]
        return remote(ref, ref, send.at[S_SIB], sib_r.at[j], dev_sib)

    for j in range(1, COLS):
        norm_one(j).start()
    az(1).start()
    ax(0).start()
    ay(0).start()
    az(2).start()
    az(3).start()

    for s in range(2):
        ld_f[s].wait()
        fw[s, r, :, 0:D] = acc[0, s, 0:FEATURES].astype(BF)
    ld_y.wait()

    def make_bias(m, _):
        across = jnp.broadcast_to(ids[pl.ds(m, 1)].astype(F32), (LENGTH, LENGTH))
        bias[m] = jnp.where(across == across.T, 0.0, MASKED)
        tdy[owner(0, 0), pl.ds(m * LENGTH, LENGTH)] = dyv[m].astype(BF)
        return 0

    lax.fori_loop(0, MB, make_bias, 0)

    def tok_copy(q, n, m, dev, whose):
        ref = (tdy, tn2)[q].at[whose, pl.ds(m * LENGTH, LENGTH)]
        shared = S_OWN if q == 1 and n < 2 else S_TOK
        return remote(ref, ref, send.at[shared], tok_r.at[q, n, m], dev)

    def tok_sib(q, m):
        return tok_copy(q, 0, m, dev_sib, owner(0, 0))

    def tok_far(q, m):
        return tok_copy(q, 1, m, dev_z(1), owner(0, 0))

    def tok_fwd(q, m):
        return tok_copy(q, 2, m, dev_sib, owner(1, 0))

    for m in range(MB):
        tok_sib(0, m).start()

    ax(0).wait_recv()
    ad0(0).start()
    ay(0).wait_recv()
    ad1(0).start()
    az(1).wait_recv()
    ax(1).start()
    ay(1).start()
    received(norm_r.at[0], nr2)
    for i in range(3):
        norm_two(i).start()
    for j in (2, 3):
        az(j).wait_recv()
        ax(j).start()
        ay(j).start()
    fz(1).start()
    for m in range(MB):
        tok_far(0, m).start()
    for j in (1, 2, 3):
        ax(j).wait_recv()
        ad0(j).start()
        ay(j).wait_recv()
        ad1(j).start()
    fx(0).start()
    fy(0).start()
    received(norm_r.at[1], nr1)

    vectors = None
    for cc in range(COLS):
        shard = jnp.concatenate([nbuf[:, cc, 0, :], jnp.zeros((ROWS, D - LANES), F32)], axis=1)
        shard = pltpu.roll(shard, cc * WIDTH, 1) if cc else shard
        vectors = shard if vectors is None else vectors + shard
    gain_one, shift_one, gain_two, shift_two = [vectors[i : i + 1] for i in range(4)]

    ld_x.wait()

    def first_norm(m, _):
        normal, _inv = ln_stats(ig[m])
        n1[m] = (normal * gain_one + shift_one).astype(BF)
        return 0

    lax.fori_loop(0, MB, first_norm, 0)

    for j in range(Z_SIZE):
        ad0(j).wait_recv()
        ad1(j).wait_recv()
        sib(j).start()
    for j in range(Z_SIZE):
        sib(j).wait_recv()

    def project(i, _):
        m, p = i // 3, i % 3
        qkv[m, p] = dot_nt(n1[m], wall[p]).astype(BF)
        return 0

    lax.fori_loop(0, 3 * MB, project, 0)

    lane_head = lax.broadcasted_iota(jnp.int32, (1, LANES), 1) // HD
    head_mask = [jnp.where(lane_head == h, 1.0, 0.0).astype(BF) for h in range(HEADS_TILE)]
    scale = HD ** (-0.5)
    log2_scale = scale * math.log2(math.e)

    def at_step(it, i, fn):
        @pl.when(it == i)
        def _():
            fn()

    def gather_xy(j):
        fz(j).wait_recv()
        fx(j).start()
        fy(j).start()

    def gather_diag(j):
        fx(j).wait_recv()
        fd0(j).start()
        fy(j).wait_recv()
        fd1(j).start()

    def save_probs(it):
        return pltpu.make_async_copy(abuf.at[it % 2], probs_hbm.at[it], pb_sem.at[it % 2])

    def load_probs(it, where):
        return pltpu.make_async_copy(probs_hbm.at[where], abuf.at[it % 2], pb_sem.at[2 + it % 2])

    def second_norm(m):
        hidden = ig[m] + dot_nt(obuf[m], wall[3])
        yout[m] = hidden
        normal, _inv = ln_stats(hidden)
        tn2[owner(0, 0), pl.ds(m * LENGTH, LENGTH)] = (normal * gain_two + shift_two).astype(BF)
        tok_far(1, m).start()
        tok_sib(1, m).start()

    def forward_group(it, _):
        m, g = it // GROUPS, it % GROUPS
        at_step(it, 5, lambda: gather_diag(0))
        at_step(it, 7, lambda: gather_xy(1))
        slot = it % 2

        @pl.when(it >= 2)
        def _():
            save_probs(it - 2).wait()

        lanes = pl.ds(pl.multiple_of(g * LANES, LANES), LANES)
        q = qkv[m, 0, :, lanes]
        kk = qkv[m, 1, :, lanes]
        v = qkv[m, 2, :, lanes]
        mask_bias = bias[m]
        mixed = None
        for h in range(HEADS_TILE):
            scores = dot_nt(q * head_mask[h], kk) * log2_scale + mask_bias
            row_max = jnp.max(scores, axis=-1, keepdims=True)
            expo = jnp.exp2(scores - row_max)
            total = jnp.sum(expo, axis=-1, keepdims=True)
            probs = (expo * (1.0 / total)).astype(BF)
            abuf[slot, h] = probs
            part = dot_nn(probs, v * head_mask[h])
            mixed = part if mixed is None else mixed + part
        obuf[m, :, lanes] = mixed.astype(BF)
        save_probs(it).start()

        @pl.when(g == GROUPS - 1)
        def _():
            second_norm(m)

        return 0

    lax.fori_loop(0, MB * GROUPS, forward_group, 0)
    save_probs(MB * GROUPS - 2).wait()
    save_probs(MB * GROUPS - 1).wait()
    for m in range(MB):
        tok_far(0, m).wait_recv()
        tok_fwd(0, m).start()

    def scatter_ops(block, r1, r1_both, r2, s_one, s_two, rs):
        def one(u, p, b):
            dev = dev_y if p == 0 else dev_x
            rr = rd if b == 1 else (ry if p == 0 else rx)
            return remote(block(rr, u, p), r1(u, p, b), send.at[s_one], rs.at[p, u], dev)

        def two(u, p):
            dev = dev_x if p == 0 else dev_y
            rr = rx if p == 0 else ry
            return remote(block(rr, u, p), r2(u, p), send.at[s_two], rs.at[2 + p, u], dev)

        def start_one(u, parts=(0, 1)):
            for p in parts:
                for b in (1, 0):
                    one(u, p, b).start()

        def start_two(u):
            for p in range(2):
                received(rs.at[p, u], r1_both(u, p))
                mine = block(rx if p == 0 else ry, u, p)
                mine[...] = (mine[...].astype(F32) + r1(u, p, 1)[...].astype(F32)).astype(BF)
                two(u, p).start()

        def own_sum(u, p):
            two(u, p).wait_recv()
            return (
                block(r, u, p)[...].astype(F32)
                + r1(u, p, 0)[...].astype(F32)
                + r2(u, p)[...].astype(F32)
            )

        return start_one, start_two, own_sum

    def unit_lanes(u):
        return pl.ds(UNITS[u][0], UNITS[u][1])

    f_one, f_two, f_sum = scatter_ops(
        lambda rr, u, p: fw.at[p, rr, :, unit_lanes(u)],
        lambda u, p, b: fr1.at[p, b, :, unit_lanes(u)],
        lambda u, p: fr1.at[p, :, :, unit_lanes(u)],
        lambda u, p: fr2.at[p, :, unit_lanes(u)],
        S_F_ONE, S_F_TWO, frs_r,
    )

    def f_far(u, p):
        lanes = pl.ds(UNITS[u][0] - D, UNITS[u][1])
        return remote(fw.at[p, r, :, unit_lanes(u)], fr3.at[p, :, lanes], send.at[S_F_FAR], frs_r.at[4 + p, u], dev_z(2))

    def f_three(u):
        for p in range(2):
            fw[p, r, :, unit_lanes(u)] = f_sum(u, p).astype(BF)
            f_far(u, p).start()

    def g_rows(zz, p, parity):
        start = (zz * 2 + parity) * WIDTH
        if p is None:
            return rows16(start, WIDTH)
        return rows16(start + PART_ROWS[0] * p, PART_ROWS[p])

    def part_rows(p):
        return pl.ds(PART_ROWS[0] * p, PART_ROWS[p])

    a_one, a_two, a_sum = scatter_ops(
        lambda rr, zz, p: wgrad.at[rr, g_rows(zz, p, k)],
        lambda zz, p, b: ar1.at[zz, b, part_rows(p)],
        lambda zz, p: ar1.at[zz, :, part_rows(p)],
        lambda zz, p: ar2.at[zz, part_rows(p)],
        S_A_ONE, S_A_TWO, ars_r,
    )

    def a_near(zz):
        return remote(wgrad.at[r, g_rows(zz, None, k)], ar3.at[zz // 2], send.at[S_A_NEAR], ars_r.at[4, zz // 2], dev_z(1))

    def a_far(zz):
        return remote(wgrad.at[r, g_rows(zz, None, k)], ar3.at[2], send.at[S_A_FAR], ars_r.at[4, 2], dev_z(2))

    def a_three(zz):
        total = [a_sum(zz, p) for p in range(2)]

        @pl.when(z % 2 == zz % 2)
        def _():
            for p in range(2):
                held[zz // 2, part_rows(p)] = total[p]

        @pl.when(z % 2 != zz % 2)
        def _():
            for p in range(2):
                wgrad[r, g_rows(zz, p, k)] = total[p].astype(BF)
            a_near(zz).start()

    def a_four(half):
        zz = half * 2 + z % 2
        a_near(2 * half).wait_recv()
        total = held[half] + ar3[half].astype(F32)

        @pl.when(z == zz)
        def _():
            agrad[...] = total

        @pl.when(z != zz)
        def _():
            wgrad[r, g_rows(zz, None, k)] = total.astype(BF)
            a_far(zz).start()

    def cross(zz):
        return remote(wgrad.at[:, g_rows(zz, None, 1 - k)], rc.at[zz], send.at[S_CROSS], rc_r.at[zz], dev_sib)

    def a_start(zz):
        cross(zz).wait_recv()
        for rr in range(ROWS):
            mine = wgrad.at[rr, g_rows(zz, None, k)]
            mine[...] = (mine[...].astype(F32) + rc[zz, rr].astype(F32)).astype(BF)
        a_one(zz)

    def ffn_tile(i, t, rows=slice(None)):
        first, width = CHUNKS[i]
        up = fw[0, :, :, first : first + width].reshape(D, width)
        down = fw[1, :, :, first : first + width].reshape(D, width)
        act, slope = gelu_pair(dot_nn(tn2[t, rows], up))
        grad_act = dot_nn(tdy[t, rows], down)
        act = act.astype(BF)
        grad_up = (grad_act * slope).astype(BF)
        gb[t, rows, 0:width] = act
        dub[t, rows, 0:width] = grad_up
        dn_part = dot_nt(grad_up, up)
        y_part = dot_nt(act, down)
        if i == 0:
            acc[0, t, rows] = dn_part
            acc[1, t, rows] = y_part
        else:
            acc[0, t, rows] += dn_part
            acc[1, t, rows] += y_part

    def weight_grads(i, units):
        first, width = CHUNKS[i]
        for p, (left, right) in enumerate(((tn2, dub), (tdy, gb))):
            grad = dot_tn(left[...].reshape(4 * MB * LENGTH, D), right[:, :, 0:width].reshape(4 * MB * LENGTH, width))
            fw[p, :, :, first : first + width] = grad.astype(BF).reshape(ROWS, FEATURES, width)
            for u in units:
                f_one(u, (p,))

    fd0(0).wait_recv()
    fd1(0).wait_recv()

    def near_tiles(s, _):
        def sib_tiles():
            for q in range(2):
                for m in range(MB):
                    tok_sib(q, m).wait_recv()

        at_step(s, 1, sib_tiles)
        ffn_tile(0, owner(0, s))
        return 0

    lax.fori_loop(0, 2, near_tiles, 0)

    def far_tiles(s, _):
        m = s // 2
        for m_ in range(MB):

            def arrived(m_=m_):
                tok_far(1, m_).wait_recv()
                tok_fwd(1, m_).start()

            def forwarded(m_=m_):
                for q in range(2):
                    tok_fwd(q, m_).wait_recv()

            at_step(s, 2 * m_, arrived)
            at_step(s, 2 * m_ + 1, forwarded)
        at_step(s, 2, lambda: gather_diag(1))
        ffn_tile(0, owner(1, s % 2), pl.ds(pl.multiple_of(m * LENGTH, LENGTH), LENGTH))
        return 0

    lax.fori_loop(0, 2 * MB, far_tiles, 0)
    fz(1).wait_send()
    for op in (fx, fy, fd0, fd1):
        op(0).wait_send()
    weight_grads(0, (0,))
    fd0(1).wait_recv()
    fd1(1).wait_recv()

    def part_sib(q, n):
        return remote(acc.at[q, owner(n, 1)], near.at[q, n], send.at[S_PART], part_r.at[q, n], dev_sib)

    def part_far(q, m):
        return remote(stage.at[q, m], far.at[q, m], send.at[S_FAR], part_r.at[q, 2 + m], dev_z(1))

    def to_far(q):
        part_sib(q, 1).wait_recv()
        for m in range(MB):
            rows = pl.ds(m * LENGTH, LENGTH)
            stage[q, m] = (acc[q, owner(1, 0), rows] + near[q, 1, rows]).astype(BF)
            part_far(q, m).start()

    def second_block(s, _):
        ffn_tile(1, owner(1 - s // 2, 1 - s % 2))
        for n in range(2):

            def to_sib(n=n):
                part_sib(0, n).start()
                part_sib(1, n).start()

            at_step(s, 2 * (1 - n), to_sib)
        at_step(s, 1, lambda: to_far(0))
        at_step(s, 2, lambda: f_two(0))
        at_step(s, 3, lambda: to_far(1))
        return 0

    lax.fori_loop(0, 4, second_block, 0)
    for op in (fx, fy, fd0, fd1):
        op(1).wait_send()
    weight_grads(1, (2, 3))

    zero = jnp.zeros((1, D), F32)
    sent(S_OWN, tn2.at[pl.ds(0, 2)])
    part_sib(0, 0).wait_recv()

    def whole(q, m):
        rows = pl.ds(m * LENGTH, LENGTH)
        return acc[q, owner(0, 0), rows] + near[q, 0, rows] + far[q, m].astype(F32)

    def second_backward(m):
        part_far(0, m).wait_recv()
        normal, inv = ln_stats(yout[m])
        grad = whole(0, m)
        grad_hidden = dyv[m] + ln_backward(normal, inv, gain_two, grad)
        dyv[m] = grad_hidden
        low = grad_hidden.astype(BF)
        dob[m] = dot_nn(low, wall[3]).astype(BF)
        tn2[owner(0, 0), pl.ds(m * LENGTH, LENGTH)] = low
        nsum[pl.ds(2, 1)] += jnp.sum(grad * normal, axis=0, keepdims=True)
        nsum[pl.ds(3, 1)] += jnp.sum(grad, axis=0, keepdims=True)

    nsum[...] = jnp.zeros(nsum.shape, F32)
    load_probs(0, 0).start()
    second_backward(0)

    def first_backward(m):
        grad = dot_nn(qkv[m, 0], wall[0]) + dot_nn(qkv[m, 1], wall[1]) + dot_nn(qkv[m, 2], wall[2])
        normal, inv = ln_stats(ig[m])
        ig[m] = dyv[m] + ln_backward(normal, inv, gain_one, grad)
        nsum[pl.ds(0, 1)] += jnp.sum(grad * normal, axis=0, keepdims=True)
        nsum[pl.ds(1, 1)] += jnp.sum(grad, axis=0, keepdims=True)

    def backward_at(it):
        m = jnp.where(it < 6, it // 3, it % 2)
        g = jnp.where(it < 6, it % 3, it // 2)
        return m, g

    def group_grads(g):
        lanes = pl.ds(pl.multiple_of(g * LANES, LANES), LANES)
        for p in range(3):
            grad = dot_tn(qkv[0, p, :, lanes], n1[0]) + dot_tn(qkv[1, p, :, lanes], n1[1])
            wgrad[p, lanes] = grad.astype(BF)

    def backward_group(it, _):
        m, g = backward_at(it)

        at_step(it, 3, lambda: f_two(2))
        at_step(it, 3, lambda: f_one(4))
        at_step(it, 3, lambda: f_one(1))

        @pl.when(it == 3)
        def _():
            second_backward(1)
            rows = [tn2[owner(0, 0), pl.ds(i * LENGTH, LENGTH)] for i in range(MB)]
            wgrad[3] = (dot_tn(rows[0], obuf[0]) + dot_tn(rows[1], obuf[1])).astype(BF)

        at_step(it, 5, lambda: f_three(2))
        at_step(it, 5, lambda: f_two(3))
        at_step(it, 6, lambda: a_start(0))
        at_step(it, 7, lambda: f_two(4))
        at_step(it, 7, lambda: a_start(1))
        at_step(it, 8, lambda: f_three(3))
        at_step(it, 8, lambda: f_two(1))
        at_step(it, 9, lambda: first_backward(0))
        at_step(it, 9, lambda: f_three(4))
        at_step(it, 9, lambda: a_two(0))
        at_step(it, 9, lambda: a_start(2))
        slot = it % 2

        @pl.when(it + 1 < MB * GROUPS)
        def _():
            m_next, g_next = backward_at(it + 1)
            load_probs(it + 1, m_next * GROUPS + g_next).start()

        load_probs(it, m * GROUPS + g).wait()
        lanes = pl.ds(pl.multiple_of(g * LANES, LANES), LANES)
        q = qkv[m, 0, :, lanes]
        kk = qkv[m, 1, :, lanes]
        v = qkv[m, 2, :, lanes]
        do = dob[m, :, lanes]
        q_turned = q.T
        do_turned = do.T
        grad_q = None
        grad_k = []
        grad_v = []
        for h in range(HEADS_TILE):
            probs = abuf[slot, h]
            wide = probs.astype(F32)
            grad_probs = dot_nt(do * head_mask[h], v)
            product = grad_probs * wide
            row = jnp.sum(product, axis=-1, keepdims=True)
            grad_scores = (product - wide * row).astype(BF)
            part = dot_nn(grad_scores, kk * head_mask[h])
            grad_q = part if grad_q is None else grad_q + part
            grad_v.append(dot_nn(do_turned[h * HD : (h + 1) * HD], probs))
            grad_k.append(dot_nn(q_turned[h * HD : (h + 1) * HD], grad_scores))
        qkv[m, 0, :, lanes] = (grad_q * scale).astype(BF)
        qkv[m, 1, :, lanes] = (jnp.concatenate(grad_k, axis=0).T * scale).astype(BF)
        qkv[m, 2, :, lanes] = jnp.concatenate(grad_v, axis=0).T.astype(BF)

        @pl.when(m == 1)
        def _():
            group_grads(g)

        at_step(it, 4, lambda: cross(0).start())
        at_step(it, 5, lambda: cross(1).start())
        at_step(it, 7, lambda: cross(2).start())
        at_step(it, 9, lambda: cross(3).start())
        return 0

    lax.fori_loop(0, MB * GROUPS, backward_group, 0)

    def put(i, src, dst):
        return pltpu.make_async_copy(src, dst, out_sem.at[i])

    first_backward(1)
    for m in range(MB):
        put(m, ig.at[m], ig_hbm.at[m]).start()

    sums = nsum[...]
    lane_own = lax.broadcasted_iota(jnp.int32, (8, LANES), 1) < WIDTH
    for cc in range(COLS):
        shard = pltpu.roll(sums, D - cc * WIDTH, 1) if cc else sums
        shard = jnp.where(lane_own, shard[:, 0:LANES], 0.0)
        for rr in range(ROWS):
            ngrad[rr, cc] = shard[rr : rr + 1]

    def grad_rows(i):
        rr = (rx, ry, rd)[i]
        return remote(ngrad.at[rr], nr1.at[i], send.at[S_G_ONE], norm_r.at[2], (dev_x, dev_y, dev_d)[i])

    def grad_cols(j):
        col = zat(j // 2) * 2 + (k + j % 2) % 2
        return remote(ngrad.at[r, col], nr2.at[j - 1], send.at[S_G_TWO], norm_r.at[3], dev_row(j))

    for i in range(3):
        grad_rows(i).start()
    a_start(3)
    a_two(1)
    a_two(2)
    a_three(0)
    received(norm_r.at[2], nr1)
    ngrad[r] = ngrad[r] + nr1[0] + nr1[1] + nr1[2]
    for j in range(1, COLS):
        grad_cols(j).start()
    a_two(3)
    a_three(1)
    a_three(2)
    a_four(0)

    part_sib(1, 0).wait_recv()
    for m in range(MB):
        part_far(1, m).wait_recv()
        yout[m] = yout[m] + whole(1, m)
        put(2 + m, yout.at[m], yout_hbm.at[m]).start()

    a_three(3)
    for u in range(2):
        for p in range(2):
            fgrad[p, :, unit_lanes(u)] = f_sum(u, p)
    a_four(1)

    sent(S_GATHER, wall.at[pl.ds(0, 3), pl.ds(0, 5 * WIDTH)])
    sent(S_SIB, wall.at[pl.ds(0, 2)])
    sent(S_TOK, tdy)
    sent(S_PART, acc.at[0])
    sent(S_FAR, stage)
    sent(S_F_ONE, fw.at[0])
    sent(S_F_TWO, fr2)
    sent(S_A_ONE, wgrad.at[0])
    sent(S_A_TWO, ar2)
    sent(S_CROSS, rc)
    sent(S_N_ONE, nr2)
    sent(S_N_TWO, nr1)
    sent(S_G_ONE, nr1)

    for u in FAR_UNITS:
        lanes = pl.ds(UNITS[u][0] - D, UNITS[u][1])
        for p in range(2):
            f_far(u, p).wait_recv()
            fgrad[p, :, lanes] += fr3[p, :, lanes].astype(F32)
    put(4, fgrad, fgrad_hbm).start()
    received(norm_r.at[3], nr2)
    total = ngrad[r, c]
    for j in range(COLS - 1):
        total = total + nr2[j]
    nout[...] = total
    a_far(z).wait_recv()
    agrad[...] = agrad[...] + ar3[2].astype(F32)
    put(5, agrad, agrad_hbm).start()

    sent(S_G_TWO, nr2)
    sent(S_F_FAR, fr3)
    sent(S_A_NEAR, ar3.at[pl.ds(0, 2)])
    sent(S_A_FAR, ar3.at[2])
    for m in range(MB):
        put(m, ig.at[m], ig_hbm.at[m]).wait()
        put(2 + m, yout.at[m], yout_hbm.at[m]).wait()
    put(4, fgrad, fgrad_hbm).wait()
    put(5, agrad, agrad_hbm).wait()


def run_step(x, dy, ids, attn_w, norm_w, ffn_w):
    vm = pltpu.VMEM
    dma = pltpu.SemaphoreType.DMA
    any_spec = pl.BlockSpec(memory_space=pl.ANY)
    vspec = pl.BlockSpec(memory_space=pltpu.VMEM)
    tokens = MB * LENGTH
    return pl.pallas_call(
        step_kernel,
        out_shape=(
            jax.ShapeDtypeStruct((MB, LENGTH, D), F32),
            jax.ShapeDtypeStruct((MB, LENGTH, D), F32),
            jax.ShapeDtypeStruct((2, FEATURES, D), F32),
            jax.ShapeDtypeStruct((WIDTH, D), F32),
            jax.ShapeDtypeStruct((1, LANES), F32),
            jax.ShapeDtypeStruct((MB * GROUPS, HEADS_TILE, LENGTH, LENGTH), BF),
        ),
        in_specs=[any_spec, any_spec, any_spec, vspec, vspec, vspec],
        out_specs=(any_spec, any_spec, any_spec, any_spec, vspec, any_spec),
        scratch_shapes=[
            vm((ROWS, D, D), BF),
            vm((ROWS, D, D), BF),
            vm((2, ROWS, FEATURES, 2 * D), BF),
            vm((MB, LENGTH, D), BF),
            vm((MB, 3, LENGTH, D), BF),
            vm((2, HEADS_TILE, LENGTH, LENGTH), BF),
            vm((MB, LENGTH, D), BF),
            vm((4, tokens, D), BF),
            vm((4, tokens, D), BF),
            vm((4, tokens, CHUNKS[1][1]), BF),
            vm((4, tokens, CHUNKS[1][1]), BF),
            vm((2, 4, tokens, D), F32),
            vm((2, 2, tokens, D), F32),
            vm((2, MB, LENGTH, D), BF),
            vm((2, MB, LENGTH, D), BF),
            vm((MB, LENGTH, D), F32),
            vm((2, 2, FEATURES, 2 * D), BF),
            vm((2, FEATURES, 2 * D), BF),
            vm((2, FEATURES, D), BF),
            vm((Z_SIZE, ROWS, WIDTH, D), BF),
            vm((Z_SIZE, 2, WIDTH, D), BF),
            vm((Z_SIZE, WIDTH, D), BF),
            vm((Z_SIZE - 1, WIDTH, D), BF),
            vm((MB, LENGTH, LENGTH), F32),
            vm((MB, LENGTH, D), BF),
            vm((ROWS, COLS, 1, LANES), F32),
            vm((ROWS, COLS, 1, LANES), F32),
            vm((8, D), F32),
            vm((3, COLS, 1, LANES), F32),
            vm((COLS - 1, 1, LANES), F32),
            vm((MB, LENGTH, D), F32),
            vm((MB, LENGTH, D), F32),
            vm((2, FEATURES, D), F32),
            vm((WIDTH, D), F32),
            vm((2, WIDTH, D), F32),
            dma((4,)), dma((4,)), dma((6,)),
            dma((18,)),
            dma((5, 2)),
            dma((5, Z_SIZE)),
            dma((5, 2)),
            dma((Z_SIZE,)),
            dma((2, 3, MB)),
            dma((2, 4)),
            dma((6, len(UNITS))),
            dma((5, Z_SIZE)),
            dma((Z_SIZE,)),
            dma((4,)),
        ],
        compiler_params=pltpu.CompilerParams(
            collective_id=0, has_side_effects=True, vmem_limit_bytes=64 * 1024 * 1024 - 4096
        ),
        name="encoder_step",
    )(x, dy, ffn_w, ids, attn_w, norm_w)


def update_kernel(rate, *refs):
    y_in, g_in, a_in, n_in, f_in = refs[0], refs[1], refs[2:6], refs[6:10], refs[10:14]
    y_out, g_out, a_out, n_out, f_out = refs[14], refs[15], refs[16:21], refs[21:26], refs[26:31]
    yb, gbuf, a_held, f_held, a_low, f_low, in_sem, out_sem = refs[31:]

    def load(i, src, dst):
        return pltpu.make_async_copy(src, dst, in_sem.at[i])

    def save(i, src, dst):
        return pltpu.make_async_copy(src, dst, out_sem.at[i])

    pieces = []
    for s in range(2):
        pieces.append(([v.at[s] for v in f_in], [v.at[s] for v in f_out], f_held.at[s], f_low.at[s]))
    pieces.append((list(a_in), list(a_out), a_held, a_low))
    loads = [
        [load(4 * n + i, src[i], held.at[i]) for i in range(4)]
        for n, (src, dst, held, low) in enumerate(pieces)
    ]
    through = [(load(12, y_in, yb), save(15, yb, y_out)), (load(13, g_in, gbuf), save(16, gbuf, g_out))]
    for copies in loads:
        for copy in copies:
            copy.start()
    for first, _second in through:
        first.start()

    def update(weights, moment, average, grad):
        moment_new = MOMENT_DECAY * moment + grad
        weights_new = weights - rate * (grad + MOMENT_DECAY * moment_new)
        average_new = AVERAGE_DECAY * average + (1.0 - AVERAGE_DECAY) * weights_new
        return moment_new, weights_new, average_new

    grad = n_in[3][:, 0:WIDTH]
    moment, weights, average = update(n_in[0][...], n_in[1][...], n_in[2][...], grad)
    for ref, value in zip(n_out, (grad, moment, weights, average, weights.astype(BF))):
        ref[...] = value

    saves = []
    for n, (src, dst, held, low) in enumerate(pieces):
        for copy in loads[n]:
            copy.wait()
        moment, weights, average = update(held[0], held[1], held[2], held[3])
        held[0] = weights
        held[1] = moment
        held[2] = average
        low[...] = weights.astype(BF)
        for i, value in enumerate((held.at[3], held.at[1], held.at[0], held.at[2], low)):
            saves.append(save(5 * n + i, value, dst[i]))
            saves[-1].start()
    for i, (first, second) in enumerate(through):
        first.wait()
        second.start()
    for copy in saves:
        copy.wait()
    for _first, second in through:
        second.wait()


def run_update(rate, carried, attn, norm, ffn):
    vm = pltpu.VMEM
    any_spec = pl.BlockSpec(memory_space=pltpu.HBM)
    vspec = pl.BlockSpec(memory_space=pltpu.VMEM)
    five = lambda like: [jax.ShapeDtypeStruct(like.shape, F32)] * 4 + [jax.ShapeDtypeStruct(like.shape, BF)]
    out = pl.pallas_call(
        functools.partial(update_kernel, rate),
        out_shape=[jax.ShapeDtypeStruct(v.shape, F32) for v in carried] + five(attn[0]) + five(norm[0]) + five(ffn[0]),
        in_specs=[any_spec] * 6 + [vspec] * 4 + [any_spec] * 4,
        out_specs=[any_spec] * 7 + [vspec] * 5 + [any_spec] * 5,
        scratch_shapes=[
            vm(carried[0].shape, F32),
            vm(carried[1].shape, F32),
            vm((4, *attn[0].shape), F32),
            vm((2, 4, *ffn[0].shape[1:]), F32),
            vm(attn[0].shape, BF),
            vm(ffn[0].shape, BF),
            pltpu.SemaphoreType.DMA((14,)),
            pltpu.SemaphoreType.DMA((17,)),
        ],
        compiler_params=pltpu.CompilerParams(vmem_limit_bytes=64 * 1024 * 1024 - 4096),
        name="update",
    )(*carried, *attn, *norm, *ffn)
    return out[0], out[1], out[2:7], out[7:12], out[12:17]


def local_slice(
    block_input, output_grad, sequence_ids,
    attn_weights, attn_momentum, attn_average,
    norm_params, norm_momentum, norm_average,
    ffn_weights, ffn_momentum, ffn_average,
):
    outputs, grads, ffn_grad, shard, norm_shard, _probs = run_step(
        block_input, output_grad, sequence_ids, attn_weights.T, norm_params[None], ffn_weights
    )
    total_tokens = MB * block_input.shape[1] * lax.axis_size("row") * lax.axis_size("col")
    step_rate = RATE_SCALE * total_tokens ** (-0.5)
    outputs, grads, attn, norm, ffn = run_update(
        step_rate,
        (outputs, grads),
        (attn_weights.T, attn_momentum.T, attn_average.T, shard),
        (norm_params[None], norm_momentum[None], norm_average[None], norm_shard),
        (ffn_weights, ffn_momentum, ffn_average, ffn_grad),
    )
    return (outputs, grads, *[v.T for v in attn], *[v[0] for v in norm], *ffn)


def local(*args):
    on_slice = (
        lax.axis_size("row") == ROWS
        and lax.axis_size("col") == COLS
        and args[0].shape[1] == LENGTH
        and args[3].shape == (D, WIDTH)
        and args[9].shape == (2, FEATURES, D)
    )
    return (local_slice if on_slice else local_general)(*args)


def solution(mesh):
    return jax.shard_map(
        local,
        mesh=mesh,
        in_specs=(
            P(None, ("row", "col"), None),
            P(None, ("row", "col"), None),
            P(None, ("row", "col")),
            P(None, ("row", "col")),
            P(None, ("row", "col")),
            P(None, ("row", "col")),
            P(("row", "col")),
            P(("row", "col")),
            P(("row", "col")),
            P(None, "row", "col"),
            P(None, "row", "col"),
            P(None, "row", "col"),
        ),
        out_specs=(
            P(None, ("row", "col"), None),
            P(None, ("row", "col"), None),
            P(None, ("row", "col")),
            P(None, ("row", "col")),
            P(None, ("row", "col")),
            P(None, ("row", "col")),
            P(None, ("row", "col")),
            P(("row", "col")),
            P(("row", "col")),
            P(("row", "col")),
            P(("row", "col")),
            P(("row", "col")),
            P(None, "row", "col"),
            P(None, "row", "col"),
            P(None, "row", "col"),
            P(None, "row", "col"),
            P(None, "row", "col"),
        ),
        check_vma=False,
    )
```

```python
import functools
import math

import jax
import jax.numpy as jnp
from jax import lax
from jax.experimental import pallas as pl
from jax.experimental.pallas import tpu as pltpu
from jax.sharding import PartitionSpec as P

D = 640
H = 20
HD = 32
MB = 2


EPSILON = 1e-05
MOMENT_DECAY = 0.9
AVERAGE_DECAY = 0.85
RATE_SCALE = 0.06
MASKED = -1e30


def layer_norm(values, gain, shift):
    center = values - jnp.mean(values, axis=-1, keepdims=True)
    spread = jnp.mean(center * center, axis=-1, keepdims=True)
    return center * lax.rsqrt(spread + EPSILON) * gain + shift


def gelu_exact(values):
    return jax.nn.gelu(values, approximate=False)


def matmul(left_side, right_side):
    return jnp.dot(left_side, right_side, preferred_element_type=jnp.float32)


def contract_rows(left_side, right_side):
    return lax.dot_general(
        left_side, right_side, (((0,), (0,)), ((), ())), preferred_element_type=jnp.float32
    )


def contract_cols(left_side, right_side):
    return lax.dot_general(
        left_side, right_side, (((1,), (1,)), ((), ())), preferred_element_type=jnp.float32
    )


def head_slices(qkv_low, first_col, head_group):
    length = qkv_low.shape[0]
    group_width = head_group * HD
    queries = lax.dynamic_slice_in_dim(qkv_low, first_col, group_width, 1).reshape(
        length, head_group, HD
    )
    keys_part = lax.dynamic_slice_in_dim(qkv_low, D + first_col, group_width, 1).reshape(
        length, head_group, HD
    )
    values = lax.dynamic_slice_in_dim(qkv_low, 2 * D + first_col, group_width, 1).reshape(
        length, head_group, HD
    )
    return (queries, keys_part, values)


def masked_scores(queries, keys_part, same_seq):
    scores = jnp.einsum(
        "qhe,khe->hqk", queries, keys_part, preferred_element_type=jnp.float32
    ) * HD ** (-0.5)
    return jnp.where(same_seq[None], scores, MASKED)


def attend_forward(qkv_low, same_seq):
    length = qkv_low.shape[0]
    head_group = math.gcd(H, 4)
    group_width = head_group * HD

    def one_group(group_index, state_all):
        mixed_all, maxima, totals = state_all
        first_col = group_index * group_width
        queries, keys_part, values = head_slices(qkv_low, first_col, head_group)
        scores = masked_scores(queries, keys_part, same_seq)
        row_max = jnp.max(scores, axis=-1, keepdims=True)
        exponent = jnp.exp(scores - row_max)
        row_total = jnp.sum(exponent, axis=-1, keepdims=True)
        attn_probs = (exponent / row_total).astype(jnp.bfloat16)
        mixed_rows = jnp.einsum(
            "hqk,khe->qhe", attn_probs, values, preferred_element_type=jnp.float32
        )
        mixed_all = lax.dynamic_update_slice_in_dim(
            mixed_all, mixed_rows.reshape(length, group_width), first_col, 1
        )
        maxima = lax.dynamic_update_slice_in_dim(
            maxima, row_max[:, :, 0], group_index * head_group, 0
        )
        totals = lax.dynamic_update_slice_in_dim(
            totals, row_total[:, :, 0], group_index * head_group, 0
        )
        return (mixed_all, maxima, totals)

    initial = (
        jnp.zeros((length, D), jnp.float32),
        jnp.zeros((H, length), jnp.float32),
        jnp.zeros((H, length), jnp.float32),
    )
    return lax.fori_loop(0, H // head_group, one_group, initial)


def attend_backward(qkv_low, same_seq, maxima, totals, grad_mixed):
    length = qkv_low.shape[0]
    head_group = math.gcd(H, 4)
    group_width = head_group * HD

    def one_group(group_index, grad_qkv):
        first_col = group_index * group_width
        queries, keys_part, values = head_slices(qkv_low, first_col, head_group)
        grad_part = lax.dynamic_slice_in_dim(grad_mixed, first_col, group_width, 1).reshape(
            length, head_group, HD
        )
        scores = masked_scores(queries, keys_part, same_seq)
        row_max = lax.dynamic_slice_in_dim(maxima, group_index * head_group, head_group, 0)[
            :, :, None
        ]
        row_total = lax.dynamic_slice_in_dim(totals, group_index * head_group, head_group, 0)[
            :, :, None
        ]
        attn_probs = jnp.exp(scores - row_max) / row_total
        grad_probs = jnp.einsum(
            "qhe,khe->hqk", grad_part, values, preferred_element_type=jnp.float32
        )
        grad_values = jnp.einsum(
            "hqk,qhe->khe",
            attn_probs.astype(jnp.bfloat16),
            grad_part,
            preferred_element_type=jnp.float32,
        )
        grad_scores = attn_probs * (
            grad_probs - jnp.sum(grad_probs * attn_probs, axis=-1, keepdims=True)
        )
        grad_scores = grad_scores.astype(jnp.bfloat16)
        grad_queries = jnp.einsum(
            "hqk,khe->qhe", grad_scores, keys_part, preferred_element_type=jnp.float32
        ) * HD ** (-0.5)
        grad_keys = jnp.einsum(
            "hqk,qhe->khe", grad_scores, queries, preferred_element_type=jnp.float32
        ) * HD ** (-0.5)
        for offset, grad_piece in ((0, grad_queries), (D, grad_keys), (2 * D, grad_values)):
            grad_qkv = lax.dynamic_update_slice_in_dim(
                grad_qkv, grad_piece.reshape(length, group_width), offset + first_col, 1
            )
        return grad_qkv

    return lax.fori_loop(0, H // head_group, one_group, jnp.zeros((length, 3 * D), jnp.float32))


def sgd_update(weights_old, moment, average, grad_sum, step_rate):
    moment_new = MOMENT_DECAY * moment + grad_sum
    weights_new = weights_old - step_rate * (grad_sum + MOMENT_DECAY * moment_new)
    average_new = AVERAGE_DECAY * average + (1.0 - AVERAGE_DECAY) * weights_new
    return (moment_new, weights_new, average_new, weights_new.astype(jnp.bfloat16))


def local_general(
    block_input,
    output_grad,
    sequence_ids,
    attn_weights,
    attn_momentum,
    attn_average,
    norm_params,
    norm_momentum,
    norm_average,
    ffn_weights,
    ffn_momentum,
    ffn_average,
):
    attn_full, norm_full = (
        lax.all_gather(attn_weights.astype(jnp.bfloat16), ("row", "col"), axis=1, tiled=True),
        lax.all_gather(norm_params.astype(jnp.bfloat16), ("row", "col"), axis=0, tiled=True),
    )
    norm_values = norm_full.astype(jnp.float32)
    gain_one = norm_values[:D]
    shift_one = norm_values[D : 2 * D]
    gain_two = norm_values[2 * D : 3 * D]
    shift_two = norm_values[3 * D :]
    qkv_weights = attn_full[:, : 3 * D]
    out_weights = attn_full[:, 3 * D :]
    ffn_rows = lax.all_gather(ffn_weights.astype(jnp.bfloat16), "row", axis=1, tiled=True)
    col_width = ffn_weights.shape[2]
    length = block_input.shape[1]
    attn_acc = jnp.zeros((D, 4 * D), jnp.float32)
    norm_acc = jnp.zeros((4 * D,), jnp.float32)
    ffn_acc = jnp.zeros((2, D, col_width), jnp.float32)
    outputs_all = []
    grads_all = []
    for micro_step in range(MB):
        inputs = block_input[micro_step]
        ids_row = sequence_ids[micro_step]
        same_seq = ids_row[:, None] == ids_row[None, :]
        normed, pull_one = jax.vjp(layer_norm, inputs, gain_one, shift_one)
        normed_low = normed.astype(jnp.bfloat16)
        qkv_low = matmul(normed_low, qkv_weights).astype(jnp.bfloat16)
        mixed_all, maxima, totals = attend_forward(qkv_low, same_seq)
        mixed_low = mixed_all.astype(jnp.bfloat16)
        hidden_in = inputs + matmul(mixed_low, out_weights)
        normed_two, pull_two = jax.vjp(layer_norm, hidden_in, gain_two, shift_two)
        normed_two_low = normed_two.astype(jnp.bfloat16)
        grad_out = output_grad[micro_step]
        grad_out_low = grad_out.astype(jnp.bfloat16)
        normed_all = lax.all_gather(normed_two_low, "col", axis=0, tiled=True)
        up_proj = matmul(normed_all, ffn_rows[0])
        activation, pull_gelu = jax.vjp(gelu_exact, up_proj)
        activ_low = activation.astype(jnp.bfloat16)
        ffn_out = lax.psum_scatter(
            contract_cols(activ_low, ffn_rows[1]).astype(jnp.bfloat16),
            "col",
            scatter_dimension=0,
            tiled=True,
        ).astype(jnp.float32)
        grad_all = lax.all_gather(grad_out_low, "col", axis=0, tiled=True)
        grad_act = matmul(grad_all, ffn_rows[1])
        grad_up = pull_gelu(grad_act)[0].astype(jnp.bfloat16)
        grad_normed_two = lax.psum_scatter(
            contract_cols(grad_up, ffn_rows[0]).astype(jnp.bfloat16),
            "col",
            scatter_dimension=0,
            tiled=True,
        ).astype(jnp.float32)
        ffn_acc = ffn_acc + jnp.stack(
            [contract_rows(normed_all, grad_up), contract_rows(grad_all, activ_low)]
        )
        outputs_all.append(hidden_in + ffn_out)
        grad_ln_two, gain_two_grad, shift_two_grad = pull_two(grad_normed_two)
        grad_hidden = grad_out + grad_ln_two
        grad_branch_low = grad_hidden.astype(jnp.bfloat16)
        out_proj_grad = contract_rows(mixed_low, grad_branch_low)
        grad_mixed_low = contract_cols(grad_branch_low, out_weights).astype(jnp.bfloat16)
        grad_qkv_low = attend_backward(qkv_low, same_seq, maxima, totals, grad_mixed_low).astype(
            jnp.bfloat16
        )
        qkv_grad = contract_rows(normed_low, grad_qkv_low)
        grad_normed = contract_cols(grad_qkv_low, qkv_weights)
        grad_ln_one, gain_one_grad, shift_one_grad = pull_one(grad_normed)
        grads_all.append(grad_hidden + grad_ln_one)
        attn_acc = attn_acc + jnp.concatenate([qkv_grad, out_proj_grad], axis=1)
        norm_acc = norm_acc + jnp.concatenate(
            [gain_one_grad, shift_one_grad, gain_two_grad, shift_two_grad]
        )
    ffn_grad = lax.psum_scatter(
        ffn_acc.astype(jnp.bfloat16), "row", scatter_dimension=1, tiled=True
    ).astype(jnp.float32)
    attn_grad, norm_grad = (
        lax.psum_scatter(attn_acc, ("row", "col"), scatter_dimension=1, tiled=True),
        lax.psum_scatter(norm_acc, ("row", "col"), scatter_dimension=0, tiled=True),
    )
    total_tokens = MB * length * lax.axis_size("row") * lax.axis_size("col")
    step_rate = RATE_SCALE * total_tokens ** (-0.5)
    attn_moment_new, attn_new, attn_avg_new, attn_copy = sgd_update(
        attn_weights, attn_momentum, attn_average, attn_grad, step_rate
    )
    norm_moment_new, norm_new, norm_avg_new, norm_copy = sgd_update(
        norm_params, norm_momentum, norm_average, norm_grad, step_rate
    )
    ffn_moment_new, ffn_new, ffn_avg_new, ffn_copy = sgd_update(
        ffn_weights, ffn_momentum, ffn_average, ffn_grad, step_rate
    )
    return (
        jnp.stack(outputs_all),
        jnp.stack(grads_all),
        attn_grad,
        attn_moment_new,
        attn_new,
        attn_avg_new,
        attn_copy,
        norm_grad,
        norm_moment_new,
        norm_new,
        norm_avg_new,
        norm_copy,
        ffn_grad,
        ffn_moment_new,
        ffn_new,
        ffn_avg_new,
        ffn_copy,
    )


MESH_ID = pl.DeviceIdType.MESH
BF = jnp.bfloat16
F32 = jnp.float32
LANES = 128
HEADS_TILE = LANES // HD
GROUPS = D // LANES
Z_SIZE = 4
COLS = 2 * Z_SIZE
ROWS = 4
WIDTH = D // COLS
LENGTH = 256
FEATURES = D // ROWS
PART_ROWS = (48, 32)
UNITS = ((0, 512), (512, 128), (640, 256), (896, 256), (1152, 128))
FAR_UNITS = (2, 3, 4)
CHUNKS = ((0, 512), (512, 768))


def dot_nn(a, b):
    return lax.dot_general(a, b, (((1,), (0,)), ((), ())), preferred_element_type=F32)


def dot_nt(a, b):
    return lax.dot_general(a, b, (((1,), (1,)), ((), ())), preferred_element_type=F32)


def dot_tn(a, b):
    return lax.dot_general(a, b, (((0,), (0,)), ((), ())), preferred_element_type=F32)


def ln_stats(values):
    center = values - jnp.mean(values, axis=-1, keepdims=True)
    spread = jnp.mean(center * center, axis=-1, keepdims=True)
    inv = lax.rsqrt(spread + EPSILON)
    return center * inv, inv


def ln_backward(normal, inv, gain, grad):
    scaled = grad * gain
    mean_one = jnp.mean(scaled, axis=-1, keepdims=True)
    mean_two = jnp.mean(scaled * normal, axis=-1, keepdims=True)
    return inv * (scaled - mean_one - normal * mean_two)


def gelu_pair(u):
    size = jnp.abs(u) * (2.0 ** -0.5)
    t = 1.0 / (1.0 + 0.3275911 * size)
    poly = 0.5 * 1.061405429
    for coef in (-1.453152027, 1.421413741, -0.284496736, 0.254829592):
        poly = poly * t + 0.5 * coef
    bell = jnp.exp2(u * u * (-0.5 * math.log2(math.e)))
    tail = poly * t * bell
    cap = jnp.where(u < 0.0, tail, 1.0 - tail)
    return u * cap, cap + u * (bell * (1.0 / math.sqrt(2.0 * math.pi)))


def step_kernel(
    x_hbm, dy_hbm, ffn_hbm, ids, attn_hbm, norm_w,
    yout_hbm, ig_hbm, fgrad_hbm, agrad_hbm, nout, probs_hbm,
    wall, wgrad, fw, n1, qkv, obuf, tn2, tdy, gb, dub, acc, near, stage, far, dyv,
    fr1, fr2, fr3, rc, ar1, ar2, ar3, nbuf, ngrad, nsum, nr1, nr2, yout, ig,
    ld_sem, pb_sem, out_sem, send, fg_s, ag_r, fg_r, sib_r, tok_r, part_r, frs_r, ars_r, rc_r, norm_r,
):
    r = lax.axis_index("row")
    c = lax.axis_index("col")
    y, x, z, k = r // 2, r % 2, c // 2, c % 2
    rx, ry, rd = y * 2 + (1 - x), (1 - y) * 2 + x, (1 - y) * 2 + (1 - x)
    dev_x = (rx, c)
    dev_y = (ry, c)
    dev_d = (rd, c)
    dev_sib = (r, z * 2 + (1 - k))

    def exclusive(a, b):
        return ((a // 2 + b // 2) % 2) * 2 + (a % 2 + b % 2) % 2

    def zat(j):
        return exclusive(z, j)

    def dev_z(j):
        return (r, zat(j) * 2 + k)

    def dev_row(j):
        return (r, zat(j // 2) * 2 + (k + j % 2) % 2)

    def owner(z_rel, k_rel):
        return ((z + z_rel) % 2) * 2 + (k + k_rel) % 2

    def rows16(start, size):
        return pl.ds(pl.multiple_of(start, 16), size)

    (
        S_GATHER, S_SIB, S_TOK, S_OWN, S_PART, S_FAR, S_F_ONE, S_F_TWO, S_F_FAR,
        S_A_ONE, S_A_TWO, S_A_NEAR, S_A_FAR, S_CROSS, S_N_ONE, S_N_TWO, S_G_ONE, S_G_TWO, S_FAR_DN,
    ) = range(19)

    def sent(i, all_bytes):
        remote(all_bytes, all_bytes, send.at[i], send.at[i], dev_sib).wait_send()

    def received(sem, all_bytes):
        remote(all_bytes, all_bytes, sem, sem, dev_sib).wait_recv()

    def remote(src, dst, ss, rs, dev):
        return pltpu.make_async_remote_copy(
            src_ref=src, dst_ref=dst, send_sem=ss, recv_sem=rs, device_id=dev, device_id_type=MESH_ID
        )

    barrier = pltpu.get_barrier_semaphore()
    for dev in (dev_x, dev_y, dev_d, *[dev_row(j) for j in range(1, COLS)]):
        pl.semaphore_signal(barrier, inc=1, device_id=dev, device_id_type=MESH_ID)

    ld_f = [pltpu.make_async_copy(ffn_hbm.at[s], acc.at[0, s, pl.ds(0, FEATURES)], ld_sem.at[2 + s]) for s in range(2)]
    ld_x = pltpu.make_async_copy(x_hbm, ig, ld_sem.at[0])
    ld_y = pltpu.make_async_copy(dy_hbm, dyv, ld_sem.at[1])
    for s in range(2):
        ld_f[s].start()
    ld_w = pltpu.make_async_copy(attn_hbm, acc.at[1, 2, pl.ds(0, WIDTH)], ld_sem.at[4])
    ld_w.start()
    ld_y.start()
    ld_x.start()

    ld_w.wait()
    wall[r, rows16(c * WIDTH, WIDTH)] = acc[1, 2, 0:WIDTH].astype(BF)
    nbuf[r, c] = jnp.zeros((1, LANES), F32)
    nbuf[r, c, :, 0:WIDTH] = norm_w[...].astype(BF).astype(F32)
    pl.semaphore_wait(barrier, COLS + 2)

    def norm_one(j):
        return remote(nbuf.at[r, c], nbuf.at[r, c], send.at[S_N_ONE], norm_r.at[0], dev_row(j))

    def norm_two(i):
        return remote(nbuf.at[r], nbuf.at[r], send.at[S_N_TWO], norm_r.at[1], (dev_x, dev_y, dev_d)[i])

    def a_rows(j, p):
        start = (zat(j) * 2 + k) * WIDTH
        if p is None:
            return rows16(start, WIDTH)
        return rows16(start + PART_ROWS[0] * p, PART_ROWS[p])

    def gather_ops(piece, part, far_piece, far_dev, ss, rs):
        def cz(j):
            return remote(piece(r, 0), far_piece(j), ss(0, j), rs.at[0, j], far_dev(j))

        def cx(j):
            return remote(piece(r, j), piece(r, j), ss(1, j), rs.at[1, j], dev_x)

        def cy(j):
            return remote(piece(r, j), piece(r, j), ss(2, j), rs.at[2, j], dev_y)

        def cd0(j):
            return remote(part(rx, j, 0), part(rx, j, 0), ss(3, j), rs.at[3, j], dev_y)

        def cd1(j):
            return remote(part(ry, j, 1), part(ry, j, 1), ss(4, j), rs.at[4, j], dev_x)

        return cz, cx, cy, cd0, cd1

    az, ax, ay, ad0, ad1 = gather_ops(
        lambda rr, j: wall.at[rr, a_rows(j, None)],
        lambda rr, j, p: wall.at[rr, a_rows(j, p)],
        lambda j: wall.at[r, a_rows(0, None)],
        dev_z, lambda i, j: send.at[S_GATHER], ag_r,
    )
    def f_copy(src, dst, kind, j, dev):
        return remote(src, dst, fg_s.at[kind, j], fg_r.at[kind, j], dev)

    def f_part(rr, i, p):
        return fw.at[p, rr, :, pl.ds(i * D, D)]

    def fz():
        return f_copy(fw.at[:, r, :, pl.ds(0, D)], fw.at[:, r, :, pl.ds(D, D)], 0, 0, dev_z(2))

    def fx(j, p):
        return f_copy(f_part(r, j, p), f_part(r, j, p), 1 + p, j, dev_x)

    def fy(j, p):
        return f_copy(f_part(r, j, p), f_part(r, j, p), 3 + p, j, dev_y)

    def fd(j, p):
        whose, dev = ((rx, dev_y), (ry, dev_x))[p]
        return f_copy(f_part(whose, j, p), f_part(whose, j, p), 5 + p, j, dev)

    def gather_first(j):
        fx(j, 0).start()
        fy(j, 1).start()

    def gather_second(j):
        fx(j, 1).start()
        fy(j, 0).start()

    def gather_diag(j):
        fx(j, 0).wait_recv()
        fd(j, 0).start()
        fy(j, 1).wait_recv()
        fd(j, 1).start()

    def gathered(j):
        fx(j, 1).wait_recv()
        fy(j, 0).wait_recv()
        fd(j, 0).wait_recv()
        fd(j, 1).wait_recv()

    def gather_sent(j):
        for p in range(2):
            fx(j, p).wait_send()
            fy(j, p).wait_send()
            fd(j, p).wait_send()

    def sib(j):
        ref = wall.at[:, a_rows(j, None)]
        return remote(ref, ref, send.at[S_SIB], sib_r.at[j], dev_sib)

    for j in range(1, COLS):
        norm_one(j).start()
    az(1).start()
    ax(0).start()
    ay(0).start()
    az(2).start()
    az(3).start()

    for s in range(2):
        ld_f[s].wait()
        fw[s, r, :, 0:D] = acc[0, s, 0:FEATURES].astype(BF)
    ld_y.wait()

    def make_bias(m, _):
        across = jnp.broadcast_to(ids[pl.ds(m, 1)].astype(F32), (LENGTH, LENGTH))
        acc[1, m, 0:LENGTH, 0:LENGTH] = jnp.where(across == across.T, 0.0, MASKED)
        tdy[owner(0, 0), pl.ds(m * LENGTH, LENGTH)] = dyv[m].astype(BF)
        return 0

    lax.fori_loop(0, MB, make_bias, 0)

    def tok_copy(q, n, m, dev, whose):
        ref = (tdy, tn2)[q].at[whose, pl.ds(m * LENGTH, LENGTH)]
        shared = S_OWN if q == 1 and n < 2 else S_TOK
        return remote(ref, ref, send.at[shared], tok_r.at[q, n, m], dev)

    def tok_sib(q, m):
        return tok_copy(q, 0, m, dev_sib, owner(0, 0))

    def tok_far(q, m):
        return tok_copy(q, 1, m, dev_z(1), owner(0, 0))

    def tok_fwd(q, m):
        return tok_copy(q, 2, m, dev_sib, owner(1, 0))

    for m in range(MB):
        tok_sib(0, m).start()

    ax(0).wait_recv()
    ad0(0).start()
    ay(0).wait_recv()
    ad1(0).start()
    az(1).wait_recv()
    ax(1).start()
    ay(1).start()
    for m in range(MB):
        tok_far(0, m).start()
    received(norm_r.at[0], nr2)
    for i in range(3):
        norm_two(i).start()
    for j in (2, 3):
        az(j).wait_recv()
        ax(j).start()
        ay(j).start()
    fz().start()
    for j in (1, 2, 3):
        ax(j).wait_recv()
        ad0(j).start()
        ay(j).wait_recv()
        ad1(j).start()
    gather_first(0)
    received(norm_r.at[1], nr1)

    vectors = None
    for cc in range(COLS):
        shard = jnp.concatenate([nbuf[:, cc, 0, :], jnp.zeros((ROWS, D - LANES), F32)], axis=1)
        shard = pltpu.roll(shard, cc * WIDTH, 1) if cc else shard
        vectors = shard if vectors is None else vectors + shard
    gain_one, shift_one, gain_two, shift_two = [vectors[i : i + 1] for i in range(4)]

    ld_x.wait()

    def first_norm(m, _):
        normal, _inv = ln_stats(ig[m])
        n1[m] = (normal * gain_one + shift_one).astype(BF)
        return 0

    lax.fori_loop(0, MB, first_norm, 0)

    for j in range(Z_SIZE):
        ad0(j).wait_recv()
        ad1(j).wait_recv()
        sib(j).start()
    for j in range(Z_SIZE):
        sib(j).wait_recv()

    gather_second(0)

    def project(i, _):
        m, p = i // 3, i % 3
        qkv[m, p] = dot_nt(n1[m], wall[p]).astype(BF)
        return 0

    lax.fori_loop(0, 3 * MB, project, 0)

    lane_head = lax.broadcasted_iota(jnp.int32, (1, LANES), 1) // HD
    head_mask = [jnp.where(lane_head == h, 1.0, 0.0).astype(BF) for h in range(HEADS_TILE)]
    scale = HD ** (-0.5)
    log2_scale = scale * math.log2(math.e)

    def at_step(it, i, fn):
        @pl.when(it == i)
        def _():
            fn()

    def slot_lanes(it, first, size):
        return pl.ds(pl.multiple_of((it % 2) * LENGTH + first, LANES), size)

    def slot_of(it):
        return gb.at[:, pl.ds(LENGTH, LENGTH), slot_lanes(it, 0, LENGTH)]

    def save_probs(it):
        return pltpu.make_async_copy(slot_of(it), probs_hbm.at[it], pb_sem.at[it % 2])

    def load_probs(it, where):
        return pltpu.make_async_copy(probs_hbm.at[where], slot_of(it), pb_sem.at[2 + it % 2])

    def second_norm(m):
        hidden = ig[m] + dot_nt(obuf[m], wall[3])
        yout[m] = hidden
        normal, _inv = ln_stats(hidden)
        tn2[owner(0, 0), pl.ds(m * LENGTH, LENGTH)] = (normal * gain_two + shift_two).astype(BF)
        tok_far(1, m).start()
        tok_sib(1, m).start()

    def forward_group(it, _):
        m, g = it // GROUPS, it % GROUPS
        at_step(it, 1, lambda: gather_diag(0))

        @pl.when(it == 8)
        def _():
            fz().wait_recv()
            gather_first(1)
            gather_second(1)


        @pl.when(it >= 2)
        def _():
            save_probs(it - 2).wait()

        lanes = pl.ds(pl.multiple_of(g * LANES, LANES), LANES)
        q = qkv[m, 0, :, lanes]
        kk = qkv[m, 1, :, lanes]
        v = qkv[m, 2, :, lanes]
        v_turned = v.T
        for h in range(HEADS_TILE):
            scores = dot_nt(kk, q * head_mask[h])
            for part in range(LENGTH // LANES):
                cols = slice(part * LANES, (part + 1) * LANES)
                shifted = scores[:, cols] * log2_scale + acc[1, m, 0:LENGTH, cols]
                expo = jnp.exp2(shifted - jnp.max(shifted, axis=0, keepdims=True))
                total = jnp.sum(expo, axis=0, keepdims=True)
                gb[h, LENGTH : 2 * LENGTH, slot_lanes(it, part * LANES, LANES)] = (expo * (1.0 / total)).astype(BF)
        mixed = [dot_nn(v_turned[h * HD : (h + 1) * HD], gb[h, LENGTH : 2 * LENGTH, slot_lanes(it, 0, LENGTH)]) for h in range(HEADS_TILE)]
        obuf[m, :, lanes] = jnp.concatenate(mixed, axis=0).T.astype(BF)
        save_probs(it).start()

        @pl.when(g == GROUPS - 1)
        def _():
            second_norm(m)

        return 0

    lax.fori_loop(0, MB * GROUPS, forward_group, 0)
    save_probs(MB * GROUPS - 2).wait()
    save_probs(MB * GROUPS - 1).wait()
    for m in range(MB):
        tok_far(0, m).wait_recv()
        tok_fwd(0, m).start()

    def scatter_ops(block, r1, r1_both, r2, s_one, s_two, rs):
        def one(u, p, b):
            dev = dev_y if p == 0 else dev_x
            rr = rd if b == 1 else (ry if p == 0 else rx)
            return remote(block(rr, u, p), r1(u, p, b), send.at[s_one], rs.at[p, u], dev)

        def two(u, p):
            dev = dev_x if p == 0 else dev_y
            rr = rx if p == 0 else ry
            return remote(block(rr, u, p), r2(u, p), send.at[s_two], rs.at[2 + p, u], dev)

        def start_one(u, parts=(0, 1)):
            for p in parts:
                for b in (1, 0):
                    one(u, p, b).start()

        def start_two(u):
            for p in range(2):
                received(rs.at[p, u], r1_both(u, p))
                mine = block(rx if p == 0 else ry, u, p)
                mine[...] = (mine[...].astype(F32) + r1(u, p, 1)[...].astype(F32)).astype(BF)
                two(u, p).start()

        def own_sum(u, p):
            two(u, p).wait_recv()
            return (
                block(r, u, p)[...].astype(F32)
                + r1(u, p, 0)[...].astype(F32)
                + r2(u, p)[...].astype(F32)
            )

        return start_one, start_two, own_sum

    def unit_lanes(u):
        return pl.ds(UNITS[u][0], UNITS[u][1])

    f_one, f_two, f_sum = scatter_ops(
        lambda rr, u, p: fw.at[p, rr, :, unit_lanes(u)],
        lambda u, p, b: fr1.at[p, b, :, unit_lanes(u)],
        lambda u, p: fr1.at[p, :, :, unit_lanes(u)],
        lambda u, p: fr2.at[p, :, unit_lanes(u)],
        S_F_ONE, S_F_TWO, frs_r,
    )

    def f_far(u, p):
        lanes = pl.ds(UNITS[u][0] - D, UNITS[u][1])
        return remote(fw.at[p, r, :, unit_lanes(u)], fr3.at[p, :, lanes], send.at[S_F_FAR], frs_r.at[4 + p, u], dev_z(2))

    def f_three(u):
        for p in range(2):
            fw[p, r, :, unit_lanes(u)] = f_sum(u, p).astype(BF)
            f_far(u, p).start()

    def g_rows(zz, p, parity):
        start = (zz * 2 + parity) * WIDTH
        if p is None:
            return rows16(start, WIDTH)
        return rows16(start + PART_ROWS[0] * p, PART_ROWS[p])

    def part_rows(p):
        return pl.ds(PART_ROWS[0] * p, PART_ROWS[p])

    a_one, a_two, a_sum = scatter_ops(
        lambda rr, zz, p: wgrad.at[rr, g_rows(zz, p, k)],
        lambda zz, p, b: ar1.at[zz, b, part_rows(p)],
        lambda zz, p: ar1.at[zz, :, part_rows(p)],
        lambda zz, p: ar2.at[zz, part_rows(p)],
        S_A_ONE, S_A_TWO, ars_r,
    )

    def a_near(zz):
        return remote(wgrad.at[r, g_rows(zz, None, k)], ar3.at[zz // 2], send.at[S_A_NEAR], ars_r.at[4, zz // 2], dev_z(1))

    def a_far(zz):
        return remote(wgrad.at[r, g_rows(zz, None, k)], ar3.at[2], send.at[S_A_FAR], ars_r.at[4, 2], dev_z(2))

    def held(i):
        return acc.at[0, owner(1, 0), pl.ds(FEATURES + i * WIDTH, WIDTH)]

    agrad = held(2)

    def a_three(zz):
        total = [a_sum(zz, p) for p in range(2)]

        @pl.when(z % 2 == zz % 2)
        def _():
            for p in range(2):
                held(zz // 2)[part_rows(p)] = total[p]

        @pl.when(z % 2 != zz % 2)
        def _():
            for p in range(2):
                wgrad[r, g_rows(zz, p, k)] = total[p].astype(BF)
            a_near(zz).start()

    def a_four(half):
        zz = half * 2 + z % 2
        a_near(2 * half).wait_recv()
        total = held(half)[...] + ar3[half].astype(F32)

        @pl.when(z == zz)
        def _():
            agrad[...] = total

        @pl.when(z != zz)
        def _():
            wgrad[r, g_rows(zz, None, k)] = total.astype(BF)
            a_far(zz).start()

    def cross(zz):
        return remote(wgrad.at[:, g_rows(zz, None, 1 - k)], rc.at[zz], send.at[S_CROSS], rc_r.at[zz], dev_sib)

    def a_start(zz):
        cross(zz).wait_recv()
        for rr in range(ROWS):
            mine = wgrad.at[rr, g_rows(zz, None, k)]
            mine[...] = (mine[...].astype(F32) + rc[zz, rr].astype(F32)).astype(BF)
        a_one(zz)

    def ffn_tile(i, t, rows=slice(None)):
        first, width = CHUNKS[i]
        up = fw[0, :, :, first : first + width].reshape(D, width)
        down = fw[1, :, :, first : first + width].reshape(D, width)
        act, slope = gelu_pair(dot_nn(tn2[t, rows], up))
        grad_act = dot_nn(tdy[t, rows], down)
        act = act.astype(BF)
        grad_up = (grad_act * slope).astype(BF)
        gb[t, rows, first : first + width] = act
        dub[t, rows, first : first + width] = grad_up
        dn_part = dot_nt(grad_up, up)
        y_part = dot_nt(act, down)
        if i == 0:
            acc[0, t, rows] = dn_part
            acc[1, t, rows] = y_part
        else:
            acc[0, t, rows] += dn_part
            acc[1, t, rows] += y_part

    def token_sums(i, left, right, first_owner, owners):
        first, width = CHUNKS[i]
        rows = owners * MB * LENGTH
        span = pl.ds(first_owner, owners)
        return dot_tn(left[span].reshape(rows, D), right[span, :, first : first + width].reshape(rows, width))

    pairs = ((tn2, dub), (tdy, gb))

    def weight_grads_near(i):
        for p, (left, right) in enumerate(pairs):
            wgrad[p, :, 0 : CHUNKS[0][1]] = token_sums(i, left, right, (z % 2) * 2, 2).astype(BF)

    def weight_grads(i, units):
        first, width = CHUNKS[i]
        for p, (left, right) in enumerate(pairs):
            if i == 0:
                grad = wgrad[p, :, 0:width].astype(F32) + token_sums(i, left, right, (1 - z % 2) * 2, 2)
            else:
                grad = token_sums(i, left, right, 0, 4)
            fw[p, :, :, first : first + width] = grad.astype(BF).reshape(ROWS, FEATURES, width)
            for u in units:
                f_one(u, (p,))
            if i == 1 and p == 0:
                f_two(0)

    gathered(0)

    def near_tiles(s, _):
        def sib_tiles():
            for q in range(2):
                for m in range(MB):
                    tok_sib(q, m).wait_recv()

        at_step(s, 1, sib_tiles)
        ffn_tile(0, owner(0, s))
        return 0

    lax.fori_loop(0, 2, near_tiles, 0)

    def far_tiles(s, _):
        m = s // 2
        for m_ in range(MB):

            def arrived(m_=m_):
                tok_far(1, m_).wait_recv()
                tok_fwd(1, m_).start()

            def forwarded(m_=m_):
                for q in range(2):
                    tok_fwd(q, m_).wait_recv()

            if m_ == 1:
                at_step(s, 2, lambda: gather_diag(1))
                at_step(s, 2, lambda: weight_grads_near(0))
            at_step(s, 2 * m_, arrived)
            at_step(s, 2 * m_ + 1, forwarded)
        ffn_tile(0, owner(1, s % 2), pl.ds(pl.multiple_of(m * LENGTH, LENGTH), LENGTH))
        return 0

    lax.fori_loop(0, 2 * MB, far_tiles, 0)
    fz().wait_send()
    gather_sent(0)
    gathered(1)

    def part_sib(q, n):
        return remote(acc.at[q, owner(n, 1)], near.at[q, n], send.at[S_PART], part_r.at[q, n], dev_sib)

    def stage_of(q, m):
        return stage.at[m] if q else wgrad.at[2, pl.ds(m * LENGTH, LENGTH)]

    def part_far(q, m):
        return remote(stage_of(q, m), far.at[q, m], send.at[(S_FAR_DN, S_FAR)[q]], part_r.at[q, 2 + m], dev_z(1))

    def to_far(q):
        part_sib(q, 1).wait_recv()
        for m in range(MB):
            rows = pl.ds(m * LENGTH, LENGTH)
            stage_of(q, m)[...] = (acc[q, owner(1, 0), rows] + near[q, 1, rows]).astype(BF)
            part_far(q, m).start()

    def second_block(s, _):
        ffn_tile(1, owner(1 - s // 2, 1 - s % 2))
        for n in range(2):

            def to_sib(n=n):
                part_sib(0, n).start()
                part_sib(1, n).start()

            at_step(s, 2 * (1 - n), to_sib)
        at_step(s, 1, lambda: to_far(0))
        at_step(s, 1, lambda: weight_grads(0, (0,)))
        at_step(s, 3, lambda: to_far(1))
        return 0

    lax.fori_loop(0, 4, second_block, 0)
    gather_sent(1)
    weight_grads(1, (2,))

    zero = jnp.zeros((1, D), F32)
    sent(S_OWN, tn2.at[pl.ds(0, 2)])
    part_sib(0, 0).wait_recv()

    def whole(q, m):
        rows = pl.ds(m * LENGTH, LENGTH)
        return acc[q, owner(0, 0), rows] + near[q, 0, rows] + far[q, m].astype(F32)

    def second_backward(m):
        part_far(0, m).wait_recv()
        normal, inv = ln_stats(yout[m])
        grad = whole(0, m)
        grad_hidden = dyv[m] + ln_backward(normal, inv, gain_two, grad)
        dyv[m] = grad_hidden
        low = grad_hidden.astype(BF)
        dub[m, 0:LENGTH, 0:D] = dot_nn(low, wall[3]).astype(BF)
        tn2[owner(0, 0), pl.ds(m * LENGTH, LENGTH)] = low
        nsum[pl.ds(2, 1)] += jnp.sum(grad * normal, axis=0, keepdims=True)
        nsum[pl.ds(3, 1)] += jnp.sum(grad, axis=0, keepdims=True)

    nsum[...] = jnp.zeros(nsum.shape, F32)
    load_probs(0, 0).start()
    second_backward(0)

    def first_backward(m):
        grad = dot_nn(qkv[m, 0], wall[0]) + dot_nn(qkv[m, 1], wall[1]) + dot_nn(qkv[m, 2], wall[2])
        normal, inv = ln_stats(ig[m])
        ig[m] = dyv[m] + ln_backward(normal, inv, gain_one, grad)
        nsum[pl.ds(0, 1)] += jnp.sum(grad * normal, axis=0, keepdims=True)
        nsum[pl.ds(1, 1)] += jnp.sum(grad, axis=0, keepdims=True)

    def backward_at(it):
        m = jnp.where(it < 6, it // 3, it % 2)
        g = jnp.where(it < 6, it % 3, it // 2)
        return m, g

    def group_grads(g):
        lanes = pl.ds(pl.multiple_of(g * LANES, LANES), LANES)
        for p in range(3):
            grad = dot_tn(qkv[0, p, :, lanes], n1[0]) + dot_tn(qkv[1, p, :, lanes], n1[1])
            wgrad[p, lanes] = grad.astype(BF)

    def backward_group(it, _):
        m, g = backward_at(it)

        at_step(it, 1, lambda: f_one(3))
        at_step(it, 3, lambda: f_two(2))

        @pl.when(it == 3)
        def _():
            second_backward(1)
            sent(S_FAR_DN, wgrad.at[2, pl.ds(0, MB * LENGTH)])
            rows = [tn2[owner(0, 0), pl.ds(i * LENGTH, LENGTH)] for i in range(MB)]
            wgrad[3] = (dot_tn(rows[0], obuf[0]) + dot_tn(rows[1], obuf[1])).astype(BF)

        at_step(it, 4, lambda: f_one(4))
        at_step(it, 4, lambda: f_three(2))
        at_step(it, 5, lambda: f_two(3))
        at_step(it, 6, lambda: a_start(0))
        at_step(it, 7, lambda: f_two(4))
        at_step(it, 7, lambda: f_three(3))
        at_step(it, 7, lambda: a_start(1))
        at_step(it, 8, lambda: f_one(1))
        at_step(it, 9, lambda: a_two(0))
        at_step(it, 9, lambda: a_start(2))
        at_step(it, 9, lambda: f_three(4))

        @pl.when(it + 1 < MB * GROUPS)
        def _():
            m_next, g_next = backward_at(it + 1)
            load_probs(it + 1, m_next * GROUPS + g_next).start()

        load_probs(it, m * GROUPS + g).wait()
        lanes = pl.ds(pl.multiple_of(g * LANES, LANES), LANES)
        q = qkv[m, 0, :, lanes]
        kk = qkv[m, 1, :, lanes]
        v = qkv[m, 2, :, lanes]
        do = dub[m, 0:LENGTH, lanes]
        k_turned = kk.T
        for h in range(HEADS_TILE):
            do_head = do * head_mask[h]
            for part in range(LENGTH // LANES):
                cols = slice(part * LANES, (part + 1) * LANES)
                wide = gb[h, LENGTH : 2 * LENGTH, slot_lanes(it, part * LANES, LANES)].astype(F32)
                product = dot_nt(v, do_head[cols]) * wide
                total = jnp.sum(product, axis=0, keepdims=True)
                gb[h, 0:LENGTH, cols] = (product - wide * total).astype(BF)
        grad_q, grad_k, grad_v = [], None, None
        for h in range(HEADS_TILE):
            v_part = dot_nn(gb[h, LENGTH : 2 * LENGTH, slot_lanes(it, 0, LENGTH)], do * head_mask[h])
            k_part = dot_nn(gb[h, 0:LENGTH, 0:LENGTH], q * head_mask[h])
            grad_v = v_part if grad_v is None else grad_v + v_part
            grad_k = k_part if grad_k is None else grad_k + k_part
            grad_q.append(dot_nn(k_turned[h * HD : (h + 1) * HD], gb[h, 0:LENGTH, 0:LENGTH]))
        qkv[m, 0, :, lanes] = (jnp.concatenate(grad_q, axis=0).T * scale).astype(BF)
        qkv[m, 1, :, lanes] = (grad_k * scale).astype(BF)
        qkv[m, 2, :, lanes] = grad_v.astype(BF)

        @pl.when(m == 1)
        def _():
            group_grads(g)

        at_step(it, 4, lambda: cross(0).start())
        at_step(it, 5, lambda: cross(1).start())
        at_step(it, 7, lambda: cross(2).start())
        at_step(it, 9, lambda: cross(3).start())
        return 0

    lax.fori_loop(0, MB * GROUPS, backward_group, 0)

    def put(i, src, dst):
        return pltpu.make_async_copy(src, dst, out_sem.at[i])

    def put_ffn(p):
        return put(4 + p, acc.at[p, owner(1, 0), pl.ds(0, FEATURES)], fgrad_hbm.at[p])

    first_backward(0)
    a_start(3)
    a_two(1)
    a_two(2)
    first_backward(1)
    for m in range(MB):
        put(m, ig.at[m], ig_hbm.at[m]).start()

    sums = nsum[...]
    lane_own = lax.broadcasted_iota(jnp.int32, (8, LANES), 1) < WIDTH
    for cc in range(COLS):
        shard = pltpu.roll(sums, D - cc * WIDTH, 1) if cc else sums
        shard = jnp.where(lane_own, shard[:, 0:LANES], 0.0)
        for rr in range(ROWS):
            ngrad[rr, cc] = shard[rr : rr + 1]

    def grad_rows(i):
        rr = (rx, ry, rd)[i]
        return remote(ngrad.at[rr], nr1.at[i], send.at[S_G_ONE], norm_r.at[2], (dev_x, dev_y, dev_d)[i])

    def grad_cols(j):
        col = zat(j // 2) * 2 + (k + j % 2) % 2
        return remote(ngrad.at[r, col], nr2.at[j - 1], send.at[S_G_TWO], norm_r.at[3], dev_row(j))

    for i in range(3):
        grad_rows(i).start()
    a_three(0)
    a_two(3)
    a_three(1)
    received(norm_r.at[2], nr1)
    ngrad[r] = ngrad[r] + nr1[0] + nr1[1] + nr1[2]
    for j in range(1, COLS):
        grad_cols(j).start()
    a_three(2)
    a_four(0)
    f_two(1)

    part_sib(1, 0).wait_recv()
    for m in range(MB):
        part_far(1, m).wait_recv()
        yout[m] = yout[m] + whole(1, m)
        put(2 + m, yout.at[m], yout_hbm.at[m]).start()

    a_three(3)
    for u in range(2):
        for p in range(2):
            acc[p, owner(1, 0), 0:FEATURES, unit_lanes(u)] = f_sum(u, p)
    a_four(1)

    sent(S_GATHER, wall.at[pl.ds(0, 3), pl.ds(0, 5 * WIDTH)])
    sent(S_SIB, wall.at[pl.ds(0, 2)])
    sent(S_TOK, tdy)
    sent(S_PART, acc.at[0])
    sent(S_FAR, stage)
    sent(S_F_ONE, fw.at[0])
    sent(S_F_TWO, fr2)
    sent(S_A_ONE, wgrad.at[0])
    sent(S_A_TWO, ar2)
    sent(S_CROSS, rc)
    sent(S_N_ONE, nr2)
    sent(S_N_TWO, nr1)
    sent(S_G_ONE, nr1)

    for u in FAR_UNITS:
        lanes = pl.ds(UNITS[u][0] - D, UNITS[u][1])
        for p in range(2):
            f_far(u, p).wait_recv()
            acc[p, owner(1, 0), 0:FEATURES, lanes] += fr3[p, :, lanes].astype(F32)
    for p in range(2):
        put_ffn(p).start()
    received(norm_r.at[3], nr2)
    total = ngrad[r, c]
    for j in range(COLS - 1):
        total = total + nr2[j]
    nout[...] = total
    a_far(z).wait_recv()
    agrad[...] = agrad[...] + ar3[2].astype(F32)
    put(6, agrad, agrad_hbm).start()

    sent(S_G_TWO, nr2)
    sent(S_F_FAR, fr3)
    sent(S_A_NEAR, ar3.at[pl.ds(0, 2)])
    sent(S_A_FAR, ar3.at[2])
    for m in range(MB):
        put(m, ig.at[m], ig_hbm.at[m]).wait()
        put(2 + m, yout.at[m], yout_hbm.at[m]).wait()
    for p in range(2):
        put_ffn(p).wait()
    put(6, agrad, agrad_hbm).wait()


def run_step(x, dy, ids, attn_w, norm_w, ffn_w):
    vm = pltpu.VMEM
    dma = pltpu.SemaphoreType.DMA
    any_spec = pl.BlockSpec(memory_space=pl.ANY)
    vspec = pl.BlockSpec(memory_space=pltpu.VMEM)
    tokens = MB * LENGTH
    return pl.pallas_call(
        step_kernel,
        out_shape=(
            jax.ShapeDtypeStruct((MB, LENGTH, D), F32),
            jax.ShapeDtypeStruct((MB, LENGTH, D), F32),
            jax.ShapeDtypeStruct((2, FEATURES, D), F32),
            jax.ShapeDtypeStruct((WIDTH, D), F32),
            jax.ShapeDtypeStruct((1, LANES), F32),
            jax.ShapeDtypeStruct((MB * GROUPS, HEADS_TILE, LENGTH, LENGTH), BF),
        ),
        in_specs=[any_spec, any_spec, any_spec, vspec, any_spec, vspec],
        out_specs=(any_spec, any_spec, any_spec, any_spec, vspec, any_spec),
        scratch_shapes=[
            vm((ROWS, D, D), BF),
            vm((ROWS, D, D), BF),
            vm((2, ROWS, FEATURES, 2 * D), BF),
            vm((MB, LENGTH, D), BF),
            vm((MB, 3, LENGTH, D), BF),
            vm((MB, LENGTH, D), BF),
            vm((4, tokens, D), BF),
            vm((4, tokens, D), BF),
            vm((4, tokens, 2 * D), BF),
            vm((4, tokens, 2 * D), BF),
            vm((2, 4, tokens, D), F32),
            vm((2, 2, tokens, D), F32),
            vm((MB, LENGTH, D), BF),
            vm((2, MB, LENGTH, D), BF),
            vm((MB, LENGTH, D), F32),
            vm((2, 2, FEATURES, 2 * D), BF),
            vm((2, FEATURES, 2 * D), BF),
            vm((2, FEATURES, D), BF),
            vm((Z_SIZE, ROWS, WIDTH, D), BF),
            vm((Z_SIZE, 2, WIDTH, D), BF),
            vm((Z_SIZE, WIDTH, D), BF),
            vm((Z_SIZE - 1, WIDTH, D), BF),
            vm((ROWS, COLS, 1, LANES), F32),
            vm((ROWS, COLS, 1, LANES), F32),
            vm((8, D), F32),
            vm((3, COLS, 1, LANES), F32),
            vm((COLS - 1, 1, LANES), F32),
            vm((MB, LENGTH, D), F32),
            vm((MB, LENGTH, D), F32),
            dma((5,)), dma((4,)), dma((7,)),
            dma((19,)),
            dma((7, 2)),
            dma((5, Z_SIZE)),
            dma((7, 2)),
            dma((Z_SIZE,)),
            dma((2, 3, MB)),
            dma((2, 4)),
            dma((6, len(UNITS))),
            dma((5, Z_SIZE)),
            dma((Z_SIZE,)),
            dma((4,)),
        ],
        compiler_params=pltpu.CompilerParams(
            collective_id=0, has_side_effects=True, vmem_limit_bytes=64 * 1024 * 1024 - 4096
        ),
        name="encoder_step",
    )(x, dy, ffn_w, ids, attn_w, norm_w)


def update_kernel(rate, *refs):
    y_in, g_in, a_in, n_in, f_in = refs[0], refs[1], refs[2:6], refs[6:10], refs[10:14]
    y_out, g_out, a_out, n_out, f_out = refs[14], refs[15], refs[16:21], refs[21:26], refs[26:31]
    yb, gbuf, a_held, f_held, a_low, f_low, in_sem, out_sem = refs[31:]

    def load(i, src, dst):
        return pltpu.make_async_copy(src, dst, in_sem.at[i])

    def save(i, src, dst):
        return pltpu.make_async_copy(src, dst, out_sem.at[i])

    pieces = []
    for s in range(2):
        pieces.append(([v.at[s] for v in f_in], [v.at[s] for v in f_out], f_held.at[s], f_low.at[s]))
    pieces.append((list(a_in), list(a_out), a_held, a_low))
    loads = [
        [load(4 * n + i, src[i], held.at[i]) for i in range(4)]
        for n, (src, dst, held, low) in enumerate(pieces)
    ]
    through = [(load(12, y_in, yb), save(15, yb, y_out)), (load(13, g_in, gbuf), save(16, gbuf, g_out))]
    for copies in loads:
        for copy in copies:
            copy.start()
    for first, _second in through:
        first.start()

    def update(weights, moment, average, grad):
        moment_new = MOMENT_DECAY * moment + grad
        weights_new = weights - rate * (grad + MOMENT_DECAY * moment_new)
        average_new = AVERAGE_DECAY * average + (1.0 - AVERAGE_DECAY) * weights_new
        return moment_new, weights_new, average_new

    grad = n_in[3][:, 0:WIDTH]
    moment, weights, average = update(n_in[0][...], n_in[1][...], n_in[2][...], grad)
    for ref, value in zip(n_out, (grad, moment, weights, average, weights.astype(BF))):
        ref[...] = value

    saves = []
    for n, (src, dst, held, low) in enumerate(pieces):
        for copy in loads[n]:
            copy.wait()
        moment, weights, average = update(held[0], held[1], held[2], held[3])
        held[0] = weights
        held[1] = moment
        held[2] = average
        low[...] = weights.astype(BF)
        for i, value in enumerate((held.at[3], held.at[1], held.at[0], held.at[2], low)):
            saves.append(save(5 * n + i, value, dst[i]))
            saves[-1].start()
    for i, (first, second) in enumerate(through):
        first.wait()
        second.start()
    for copy in saves:
        copy.wait()
    for _first, second in through:
        second.wait()


def run_update(rate, carried, attn, norm, ffn):
    vm = pltpu.VMEM
    any_spec = pl.BlockSpec(memory_space=pltpu.HBM)
    vspec = pl.BlockSpec(memory_space=pltpu.VMEM)
    five = lambda like: [jax.ShapeDtypeStruct(like.shape, F32)] * 4 + [jax.ShapeDtypeStruct(like.shape, BF)]
    out = pl.pallas_call(
        functools.partial(update_kernel, rate),
        out_shape=[jax.ShapeDtypeStruct(v.shape, F32) for v in carried] + five(attn[0]) + five(norm[0]) + five(ffn[0]),
        in_specs=[any_spec] * 6 + [vspec] * 4 + [any_spec] * 4,
        out_specs=[any_spec] * 7 + [vspec] * 5 + [any_spec] * 5,
        scratch_shapes=[
            vm(carried[0].shape, F32),
            vm(carried[1].shape, F32),
            vm((4, *attn[0].shape), F32),
            vm((2, 4, *ffn[0].shape[1:]), F32),
            vm(attn[0].shape, BF),
            vm(ffn[0].shape, BF),
            pltpu.SemaphoreType.DMA((14,)),
            pltpu.SemaphoreType.DMA((17,)),
        ],
        compiler_params=pltpu.CompilerParams(vmem_limit_bytes=64 * 1024 * 1024 - 4096),
        name="update",
    )(*carried, *attn, *norm, *ffn)
    return out[0], out[1], out[2:7], out[7:12], out[12:17]


def local_slice(
    block_input, output_grad, sequence_ids,
    attn_weights, attn_momentum, attn_average,
    norm_params, norm_momentum, norm_average,
    ffn_weights, ffn_momentum, ffn_average,
):
    outputs, grads, ffn_grad, shard, norm_shard, _probs = run_step(
        block_input, output_grad, sequence_ids, attn_weights.T, norm_params[None], ffn_weights
    )
    total_tokens = MB * block_input.shape[1] * lax.axis_size("row") * lax.axis_size("col")
    step_rate = RATE_SCALE * total_tokens ** (-0.5)
    outputs, grads, attn, norm, ffn = run_update(
        step_rate,
        (outputs, grads),
        (attn_weights.T, attn_momentum.T, attn_average.T, shard),
        (norm_params[None], norm_momentum[None], norm_average[None], norm_shard),
        (ffn_weights, ffn_momentum, ffn_average, ffn_grad),
    )
    return (outputs, grads, *[v.T for v in attn], *[v[0] for v in norm], *ffn)


def local(*args):
    on_slice = (
        lax.axis_size("row") == ROWS
        and lax.axis_size("col") == COLS
        and args[0].shape[1] == LENGTH
        and args[3].shape == (D, WIDTH)
        and args[9].shape == (2, FEATURES, D)
    )
    return (local_slice if on_slice else local_general)(*args)


def solution(mesh):
    return jax.shard_map(
        local,
        mesh=mesh,
        in_specs=(
            P(None, ("row", "col"), None),
            P(None, ("row", "col"), None),
            P(None, ("row", "col")),
            P(None, ("row", "col")),
            P(None, ("row", "col")),
            P(None, ("row", "col")),
            P(("row", "col")),
            P(("row", "col")),
            P(("row", "col")),
            P(None, "row", "col"),
            P(None, "row", "col"),
            P(None, "row", "col"),
        ),
        out_specs=(
            P(None, ("row", "col"), None),
            P(None, ("row", "col"), None),
            P(None, ("row", "col")),
            P(None, ("row", "col")),
            P(None, ("row", "col")),
            P(None, ("row", "col")),
            P(None, ("row", "col")),
            P(("row", "col")),
            P(("row", "col")),
            P(("row", "col")),
            P(("row", "col")),
            P(("row", "col")),
            P(None, "row", "col"),
            P(None, "row", "col"),
            P(None, "row", "col"),
            P(None, "row", "col"),
            P(None, "row", "col"),
        ),
        check_vma=False,
    )
```

```python
import functools
import math

import jax
import jax.numpy as jnp
from jax import lax
from jax.experimental import pallas as pl
from jax.experimental.pallas import tpu as pltpu
from jax.sharding import PartitionSpec as P

D = 640
H = 20
HD = 32
MB = 2


EPSILON = 1e-05
MOMENT_DECAY = 0.9
AVERAGE_DECAY = 0.85
RATE_SCALE = 0.06
MASKED = -1e30


def layer_norm(values, gain, shift):
    center = values - jnp.mean(values, axis=-1, keepdims=True)
    spread = jnp.mean(center * center, axis=-1, keepdims=True)
    return center * lax.rsqrt(spread + EPSILON) * gain + shift


def gelu_exact(values):
    return jax.nn.gelu(values, approximate=False)


def matmul(left_side, right_side):
    return jnp.dot(left_side, right_side, preferred_element_type=jnp.float32)


def contract_rows(left_side, right_side):
    return lax.dot_general(
        left_side, right_side, (((0,), (0,)), ((), ())), preferred_element_type=jnp.float32
    )


def contract_cols(left_side, right_side):
    return lax.dot_general(
        left_side, right_side, (((1,), (1,)), ((), ())), preferred_element_type=jnp.float32
    )


def head_slices(qkv_low, first_col, head_group):
    length = qkv_low.shape[0]
    group_width = head_group * HD
    queries = lax.dynamic_slice_in_dim(qkv_low, first_col, group_width, 1).reshape(
        length, head_group, HD
    )
    keys_part = lax.dynamic_slice_in_dim(qkv_low, D + first_col, group_width, 1).reshape(
        length, head_group, HD
    )
    values = lax.dynamic_slice_in_dim(qkv_low, 2 * D + first_col, group_width, 1).reshape(
        length, head_group, HD
    )
    return (queries, keys_part, values)


def masked_scores(queries, keys_part, same_seq):
    scores = jnp.einsum(
        "qhe,khe->hqk", queries, keys_part, preferred_element_type=jnp.float32
    ) * HD ** (-0.5)
    return jnp.where(same_seq[None], scores, MASKED)


def attend_forward(qkv_low, same_seq):
    length = qkv_low.shape[0]
    head_group = math.gcd(H, 4)
    group_width = head_group * HD

    def one_group(group_index, state_all):
        mixed_all, maxima, totals = state_all
        first_col = group_index * group_width
        queries, keys_part, values = head_slices(qkv_low, first_col, head_group)
        scores = masked_scores(queries, keys_part, same_seq)
        row_max = jnp.max(scores, axis=-1, keepdims=True)
        exponent = jnp.exp(scores - row_max)
        row_total = jnp.sum(exponent, axis=-1, keepdims=True)
        attn_probs = (exponent / row_total).astype(jnp.bfloat16)
        mixed_rows = jnp.einsum(
            "hqk,khe->qhe", attn_probs, values, preferred_element_type=jnp.float32
        )
        mixed_all = lax.dynamic_update_slice_in_dim(
            mixed_all, mixed_rows.reshape(length, group_width), first_col, 1
        )
        maxima = lax.dynamic_update_slice_in_dim(
            maxima, row_max[:, :, 0], group_index * head_group, 0
        )
        totals = lax.dynamic_update_slice_in_dim(
            totals, row_total[:, :, 0], group_index * head_group, 0
        )
        return (mixed_all, maxima, totals)

    initial = (
        jnp.zeros((length, D), jnp.float32),
        jnp.zeros((H, length), jnp.float32),
        jnp.zeros((H, length), jnp.float32),
    )
    return lax.fori_loop(0, H // head_group, one_group, initial)


def attend_backward(qkv_low, same_seq, maxima, totals, grad_mixed):
    length = qkv_low.shape[0]
    head_group = math.gcd(H, 4)
    group_width = head_group * HD

    def one_group(group_index, grad_qkv):
        first_col = group_index * group_width
        queries, keys_part, values = head_slices(qkv_low, first_col, head_group)
        grad_part = lax.dynamic_slice_in_dim(grad_mixed, first_col, group_width, 1).reshape(
            length, head_group, HD
        )
        scores = masked_scores(queries, keys_part, same_seq)
        row_max = lax.dynamic_slice_in_dim(maxima, group_index * head_group, head_group, 0)[
            :, :, None
        ]
        row_total = lax.dynamic_slice_in_dim(totals, group_index * head_group, head_group, 0)[
            :, :, None
        ]
        attn_probs = jnp.exp(scores - row_max) / row_total
        grad_probs = jnp.einsum(
            "qhe,khe->hqk", grad_part, values, preferred_element_type=jnp.float32
        )
        grad_values = jnp.einsum(
            "hqk,qhe->khe",
            attn_probs.astype(jnp.bfloat16),
            grad_part,
            preferred_element_type=jnp.float32,
        )
        grad_scores = attn_probs * (
            grad_probs - jnp.sum(grad_probs * attn_probs, axis=-1, keepdims=True)
        )
        grad_scores = grad_scores.astype(jnp.bfloat16)
        grad_queries = jnp.einsum(
            "hqk,khe->qhe", grad_scores, keys_part, preferred_element_type=jnp.float32
        ) * HD ** (-0.5)
        grad_keys = jnp.einsum(
            "hqk,qhe->khe", grad_scores, queries, preferred_element_type=jnp.float32
        ) * HD ** (-0.5)
        for offset, grad_piece in ((0, grad_queries), (D, grad_keys), (2 * D, grad_values)):
            grad_qkv = lax.dynamic_update_slice_in_dim(
                grad_qkv, grad_piece.reshape(length, group_width), offset + first_col, 1
            )
        return grad_qkv

    return lax.fori_loop(0, H // head_group, one_group, jnp.zeros((length, 3 * D), jnp.float32))


def sgd_update(weights_old, moment, average, grad_sum, step_rate):
    moment_new = MOMENT_DECAY * moment + grad_sum
    weights_new = weights_old - step_rate * (grad_sum + MOMENT_DECAY * moment_new)
    average_new = AVERAGE_DECAY * average + (1.0 - AVERAGE_DECAY) * weights_new
    return (moment_new, weights_new, average_new, weights_new.astype(jnp.bfloat16))


def local_general(
    block_input,
    output_grad,
    sequence_ids,
    attn_weights,
    attn_momentum,
    attn_average,
    norm_params,
    norm_momentum,
    norm_average,
    ffn_weights,
    ffn_momentum,
    ffn_average,
):
    attn_full, norm_full = (
        lax.all_gather(attn_weights.astype(jnp.bfloat16), ("row", "col"), axis=1, tiled=True),
        lax.all_gather(norm_params.astype(jnp.bfloat16), ("row", "col"), axis=0, tiled=True),
    )
    norm_values = norm_full.astype(jnp.float32)
    gain_one = norm_values[:D]
    shift_one = norm_values[D : 2 * D]
    gain_two = norm_values[2 * D : 3 * D]
    shift_two = norm_values[3 * D :]
    qkv_weights = attn_full[:, : 3 * D]
    out_weights = attn_full[:, 3 * D :]
    ffn_rows = lax.all_gather(ffn_weights.astype(jnp.bfloat16), "row", axis=1, tiled=True)
    col_width = ffn_weights.shape[2]
    length = block_input.shape[1]
    attn_acc = jnp.zeros((D, 4 * D), jnp.float32)
    norm_acc = jnp.zeros((4 * D,), jnp.float32)
    ffn_acc = jnp.zeros((2, D, col_width), jnp.float32)
    outputs_all = []
    grads_all = []
    for micro_step in range(MB):
        inputs = block_input[micro_step]
        ids_row = sequence_ids[micro_step]
        same_seq = ids_row[:, None] == ids_row[None, :]
        normed, pull_one = jax.vjp(layer_norm, inputs, gain_one, shift_one)
        normed_low = normed.astype(jnp.bfloat16)
        qkv_low = matmul(normed_low, qkv_weights).astype(jnp.bfloat16)
        mixed_all, maxima, totals = attend_forward(qkv_low, same_seq)
        mixed_low = mixed_all.astype(jnp.bfloat16)
        hidden_in = inputs + matmul(mixed_low, out_weights)
        normed_two, pull_two = jax.vjp(layer_norm, hidden_in, gain_two, shift_two)
        normed_two_low = normed_two.astype(jnp.bfloat16)
        grad_out = output_grad[micro_step]
        grad_out_low = grad_out.astype(jnp.bfloat16)
        normed_all = lax.all_gather(normed_two_low, "col", axis=0, tiled=True)
        up_proj = matmul(normed_all, ffn_rows[0])
        activation, pull_gelu = jax.vjp(gelu_exact, up_proj)
        activ_low = activation.astype(jnp.bfloat16)
        ffn_out = lax.psum_scatter(
            contract_cols(activ_low, ffn_rows[1]).astype(jnp.bfloat16),
            "col",
            scatter_dimension=0,
            tiled=True,
        ).astype(jnp.float32)
        grad_all = lax.all_gather(grad_out_low, "col", axis=0, tiled=True)
        grad_act = matmul(grad_all, ffn_rows[1])
        grad_up = pull_gelu(grad_act)[0].astype(jnp.bfloat16)
        grad_normed_two = lax.psum_scatter(
            contract_cols(grad_up, ffn_rows[0]).astype(jnp.bfloat16),
            "col",
            scatter_dimension=0,
            tiled=True,
        ).astype(jnp.float32)
        ffn_acc = ffn_acc + jnp.stack(
            [contract_rows(normed_all, grad_up), contract_rows(grad_all, activ_low)]
        )
        outputs_all.append(hidden_in + ffn_out)
        grad_ln_two, gain_two_grad, shift_two_grad = pull_two(grad_normed_two)
        grad_hidden = grad_out + grad_ln_two
        grad_branch_low = grad_hidden.astype(jnp.bfloat16)
        out_proj_grad = contract_rows(mixed_low, grad_branch_low)
        grad_mixed_low = contract_cols(grad_branch_low, out_weights).astype(jnp.bfloat16)
        grad_qkv_low = attend_backward(qkv_low, same_seq, maxima, totals, grad_mixed_low).astype(
            jnp.bfloat16
        )
        qkv_grad = contract_rows(normed_low, grad_qkv_low)
        grad_normed = contract_cols(grad_qkv_low, qkv_weights)
        grad_ln_one, gain_one_grad, shift_one_grad = pull_one(grad_normed)
        grads_all.append(grad_hidden + grad_ln_one)
        attn_acc = attn_acc + jnp.concatenate([qkv_grad, out_proj_grad], axis=1)
        norm_acc = norm_acc + jnp.concatenate(
            [gain_one_grad, shift_one_grad, gain_two_grad, shift_two_grad]
        )
    ffn_grad = lax.psum_scatter(
        ffn_acc.astype(jnp.bfloat16), "row", scatter_dimension=1, tiled=True
    ).astype(jnp.float32)
    attn_grad, norm_grad = (
        lax.psum_scatter(attn_acc, ("row", "col"), scatter_dimension=1, tiled=True),
        lax.psum_scatter(norm_acc, ("row", "col"), scatter_dimension=0, tiled=True),
    )
    total_tokens = MB * length * lax.axis_size("row") * lax.axis_size("col")
    step_rate = RATE_SCALE * total_tokens ** (-0.5)
    attn_moment_new, attn_new, attn_avg_new, attn_copy = sgd_update(
        attn_weights, attn_momentum, attn_average, attn_grad, step_rate
    )
    norm_moment_new, norm_new, norm_avg_new, norm_copy = sgd_update(
        norm_params, norm_momentum, norm_average, norm_grad, step_rate
    )
    ffn_moment_new, ffn_new, ffn_avg_new, ffn_copy = sgd_update(
        ffn_weights, ffn_momentum, ffn_average, ffn_grad, step_rate
    )
    return (
        jnp.stack(outputs_all),
        jnp.stack(grads_all),
        attn_grad,
        attn_moment_new,
        attn_new,
        attn_avg_new,
        attn_copy,
        norm_grad,
        norm_moment_new,
        norm_new,
        norm_avg_new,
        norm_copy,
        ffn_grad,
        ffn_moment_new,
        ffn_new,
        ffn_avg_new,
        ffn_copy,
    )


MESH_ID = pl.DeviceIdType.MESH
BF = jnp.bfloat16
F32 = jnp.float32
LANES = 128
HEADS_TILE = LANES // HD
GROUPS = D // LANES
Z_SIZE = 4
COLS = 2 * Z_SIZE
ROWS = 4
WIDTH = D // COLS
LENGTH = 256
FEATURES = D // ROWS
PART_ROWS = (48, 32)
UNITS = ((0, 512), (512, 128), (640, 256), (896, 256), (1152, 128))
FAR_UNITS = (2, 3, 4)
CHUNKS = ((0, 512), (512, 768))


def dot_nn(a, b):
    return lax.dot_general(a, b, (((1,), (0,)), ((), ())), preferred_element_type=F32)


def dot_nt(a, b):
    return lax.dot_general(a, b, (((1,), (1,)), ((), ())), preferred_element_type=F32)


def dot_tn(a, b):
    return lax.dot_general(a, b, (((0,), (0,)), ((), ())), preferred_element_type=F32)


def ln_stats(values):
    center = values - jnp.mean(values, axis=-1, keepdims=True)
    spread = jnp.mean(center * center, axis=-1, keepdims=True)
    inv = lax.rsqrt(spread + EPSILON)
    return center * inv, inv


def ln_backward(normal, inv, gain, grad):
    scaled = grad * gain
    mean_one = jnp.mean(scaled, axis=-1, keepdims=True)
    mean_two = jnp.mean(scaled * normal, axis=-1, keepdims=True)
    return inv * (scaled - mean_one - normal * mean_two)


def gelu_pair(u):
    size = jnp.abs(u) * (2.0 ** -0.5)
    t = 1.0 / (1.0 + 0.3275911 * size)
    poly = 0.5 * 1.061405429
    for coef in (-1.453152027, 1.421413741, -0.284496736, 0.254829592):
        poly = poly * t + 0.5 * coef
    bell = jnp.exp2(u * u * (-0.5 * math.log2(math.e)))
    tail = poly * t * bell
    cap = jnp.where(u < 0.0, tail, 1.0 - tail)
    return u * cap, cap + u * (bell * (1.0 / math.sqrt(2.0 * math.pi)))


def step_kernel(
    x_hbm, dy_hbm, ffn_hbm, ids, attn_hbm, norm_w,
    yout_hbm, ig_hbm, fgrad_hbm, agrad_hbm, nout, probs_hbm,
    wall, wgrad, fw, n1, qkv, obuf, tn2, tdy, gb, dub, acc, near, stage, far, dyv,
    fr1, fr2, fr3, rc, ar1, ar2, ar3, nbuf, ngrad, nsum, nr1, nr2, yout, ig,
    ld_sem, pb_sem, out_sem, send, fg_s, ag_r, fg_r, sib_r, tok_r, part_r, frs_r, ars_r, rc_r, norm_r,
):
    r = lax.axis_index("row")
    c = lax.axis_index("col")
    y, x, z, k = r // 2, r % 2, c // 2, c % 2
    rx, ry, rd = y * 2 + (1 - x), (1 - y) * 2 + x, (1 - y) * 2 + (1 - x)
    dev_x = (rx, c)
    dev_y = (ry, c)
    dev_d = (rd, c)
    dev_sib = (r, z * 2 + (1 - k))

    def exclusive(a, b):
        return ((a // 2 + b // 2) % 2) * 2 + (a % 2 + b % 2) % 2

    def zat(j):
        return exclusive(z, j)

    def dev_z(j):
        return (r, zat(j) * 2 + k)

    def dev_row(j):
        return (r, zat(j // 2) * 2 + (k + j % 2) % 2)

    def owner(z_rel, k_rel):
        return ((z + z_rel) % 2) * 2 + (k + k_rel) % 2

    def rows16(start, size):
        return pl.ds(pl.multiple_of(start, 16), size)

    (
        S_GATHER, S_SIB, S_TOK, S_OWN, S_PART, S_FAR, S_F_ONE, S_F_TWO, S_F_FAR,
        S_A_ONE, S_A_TWO, S_A_NEAR, S_A_FAR, S_CROSS, S_N_ONE, S_N_TWO, S_G_ONE, S_G_TWO, S_FAR_DN,
    ) = range(19)

    def sent(i, all_bytes):
        remote(all_bytes, all_bytes, send.at[i], send.at[i], dev_sib).wait_send()

    def received(sem, all_bytes):
        remote(all_bytes, all_bytes, sem, sem, dev_sib).wait_recv()

    def remote(src, dst, ss, rs, dev):
        return pltpu.make_async_remote_copy(
            src_ref=src, dst_ref=dst, send_sem=ss, recv_sem=rs, device_id=dev, device_id_type=MESH_ID
        )

    barrier = pltpu.get_barrier_semaphore()
    for dev in (dev_x, dev_y, dev_d, *[dev_row(j) for j in range(1, COLS)]):
        pl.semaphore_signal(barrier, inc=1, device_id=dev, device_id_type=MESH_ID)

    ld_f = [pltpu.make_async_copy(ffn_hbm.at[s], acc.at[0, s, pl.ds(0, FEATURES)], ld_sem.at[2 + s]) for s in range(2)]
    ld_x = pltpu.make_async_copy(x_hbm, ig, ld_sem.at[0])
    ld_y = pltpu.make_async_copy(dy_hbm, dyv, ld_sem.at[1])
    for s in range(2):
        ld_f[s].start()
    ld_w = pltpu.make_async_copy(attn_hbm, acc.at[1, 2, pl.ds(0, WIDTH)], ld_sem.at[4])
    ld_w.start()
    ld_y.start()
    ld_x.start()

    ld_w.wait()
    wall[r, rows16(c * WIDTH, WIDTH)] = acc[1, 2, 0:WIDTH].astype(BF)
    nbuf[r, c] = jnp.zeros((1, LANES), F32)
    nbuf[r, c, :, 0:WIDTH] = norm_w[...].astype(BF).astype(F32)
    pl.semaphore_wait(barrier, COLS + 2)

    def norm_one(j):
        return remote(nbuf.at[r, c], nbuf.at[r, c], send.at[S_N_ONE], norm_r.at[0], dev_row(j))

    def norm_two(i):
        return remote(nbuf.at[r], nbuf.at[r], send.at[S_N_TWO], norm_r.at[1], (dev_x, dev_y, dev_d)[i])

    def a_rows(j, p):
        start = (zat(j) * 2 + k) * WIDTH
        if p is None:
            return rows16(start, WIDTH)
        return rows16(start + PART_ROWS[0] * p, PART_ROWS[p])

    def gather_ops(piece, part, far_piece, far_dev, ss, rs):
        def cz(j):
            return remote(piece(r, 0), far_piece(j), ss(0, j), rs.at[0, j], far_dev(j))

        def cx(j):
            return remote(piece(r, j), piece(r, j), ss(1, j), rs.at[1, j], dev_x)

        def cy(j):
            return remote(piece(r, j), piece(r, j), ss(2, j), rs.at[2, j], dev_y)

        def cd0(j):
            return remote(part(rx, j, 0), part(rx, j, 0), ss(3, j), rs.at[3, j], dev_y)

        def cd1(j):
            return remote(part(ry, j, 1), part(ry, j, 1), ss(4, j), rs.at[4, j], dev_x)

        return cz, cx, cy, cd0, cd1

    az, ax, ay, ad0, ad1 = gather_ops(
        lambda rr, j: wall.at[rr, a_rows(j, None)],
        lambda rr, j, p: wall.at[rr, a_rows(j, p)],
        lambda j: wall.at[r, a_rows(0, None)],
        dev_z, lambda i, j: send.at[S_GATHER], ag_r,
    )
    def f_copy(src, dst, kind, j, dev):
        return remote(src, dst, fg_s.at[kind, j], fg_r.at[kind, j], dev)

    def f_part(rr, i, p):
        return fw.at[p, rr, :, pl.ds(i * D, D)]

    def fz():
        return f_copy(fw.at[:, r, :, pl.ds(0, D)], fw.at[:, r, :, pl.ds(D, D)], 0, 0, dev_z(2))

    def fx(j, p):
        return f_copy(f_part(r, j, p), f_part(r, j, p), 1 + p, j, dev_x)

    def fy(j, p):
        return f_copy(f_part(r, j, p), f_part(r, j, p), 3 + p, j, dev_y)

    def fd(j, p):
        whose, dev = ((rx, dev_y), (ry, dev_x))[p]
        return f_copy(f_part(whose, j, p), f_part(whose, j, p), 5 + p, j, dev)

    def gather_first(j):
        fx(j, 0).start()
        fy(j, 1).start()

    def gather_second(j):
        fx(j, 1).start()
        fy(j, 0).start()

    def gather_diag(j):
        fx(j, 0).wait_recv()
        fd(j, 0).start()
        fy(j, 1).wait_recv()
        fd(j, 1).start()

    def gathered(j):
        fx(j, 1).wait_recv()
        fy(j, 0).wait_recv()
        fd(j, 0).wait_recv()
        fd(j, 1).wait_recv()

    def gather_sent(j):
        for p in range(2):
            fx(j, p).wait_send()
            fy(j, p).wait_send()
            fd(j, p).wait_send()

    def sib(j):
        ref = wall.at[:, a_rows(j, None)]
        return remote(ref, ref, send.at[S_SIB], sib_r.at[j], dev_sib)

    for j in range(1, COLS):
        norm_one(j).start()
    az(1).start()
    ax(0).start()
    ay(0).start()
    az(2).start()
    az(3).start()

    for s in range(2):
        ld_f[s].wait()
        fw[s, r, :, 0:D] = acc[0, s, 0:FEATURES].astype(BF)
    ld_y.wait()

    def make_bias(m, _):
        across = jnp.broadcast_to(ids[pl.ds(m, 1)].astype(F32), (LENGTH, LENGTH))
        acc[1, m, 0:LENGTH, 0:LENGTH] = jnp.where(across == across.T, 0.0, MASKED)
        tdy[owner(0, 0), pl.ds(m * LENGTH, LENGTH)] = dyv[m].astype(BF)
        return 0

    lax.fori_loop(0, MB, make_bias, 0)

    def tok_copy(q, n, m, dev, whose):
        ref = (tdy, tn2)[q].at[whose, pl.ds(m * LENGTH, LENGTH)]
        shared = S_OWN if q == 1 and n < 2 else S_TOK
        return remote(ref, ref, send.at[shared], tok_r.at[q, n, m], dev)

    def tok_sib(q, m):
        return tok_copy(q, 0, m, dev_sib, owner(0, 0))

    def tok_far(q, m):
        return tok_copy(q, 1, m, dev_z(1), owner(0, 0))

    def tok_fwd(q, m):
        return tok_copy(q, 2, m, dev_sib, owner(1, 0))

    for m in range(MB):
        tok_sib(0, m).start()

    ax(0).wait_recv()
    ad0(0).start()
    ay(0).wait_recv()
    ad1(0).start()
    az(1).wait_recv()
    ax(1).start()
    ay(1).start()
    for m in range(MB):
        tok_far(0, m).start()
    received(norm_r.at[0], nr2)
    for i in range(3):
        norm_two(i).start()
    for j in (2, 3):
        az(j).wait_recv()
        ax(j).start()
        ay(j).start()
    fz().start()
    for j in (1, 2, 3):
        ax(j).wait_recv()
        ad0(j).start()
        ay(j).wait_recv()
        ad1(j).start()
    gather_first(0)
    received(norm_r.at[1], nr1)

    vectors = None
    for cc in range(COLS):
        shard = jnp.concatenate([nbuf[:, cc, 0, :], jnp.zeros((ROWS, D - LANES), F32)], axis=1)
        shard = pltpu.roll(shard, cc * WIDTH, 1) if cc else shard
        vectors = shard if vectors is None else vectors + shard
    gain_one, shift_one, gain_two, shift_two = [vectors[i : i + 1] for i in range(4)]

    ld_x.wait()

    def first_norm(m, _):
        normal, _inv = ln_stats(ig[m])
        n1[m] = (normal * gain_one + shift_one).astype(BF)
        return 0

    lax.fori_loop(0, MB, first_norm, 0)

    for j in range(Z_SIZE):
        ad0(j).wait_recv()
        ad1(j).wait_recv()
        sib(j).start()
    for j in range(Z_SIZE):
        sib(j).wait_recv()

    gather_second(0)

    def project(i, _):
        rows = dot_nt(n1[...].reshape(MB * LENGTH, D), wall[i]).astype(BF)
        for m in range(MB):
            qkv[m, i] = rows[m * LENGTH : (m + 1) * LENGTH]
        return 0

    lax.fori_loop(0, 3, project, 0)

    lane_head = lax.broadcasted_iota(jnp.int32, (1, LANES), 1) // HD
    head_mask = [jnp.where(lane_head == h, 1.0, 0.0).astype(BF) for h in range(HEADS_TILE)]
    scale = HD ** (-0.5)
    log2_scale = scale * math.log2(math.e)

    def at_step(it, i, fn):
        @pl.when(it == i)
        def _():
            fn()

    def slot_lanes(it, first, size):
        return pl.ds(pl.multiple_of((it % 2) * LENGTH + first, LANES), size)

    def slot_of(it):
        return gb.at[:, pl.ds(LENGTH, LENGTH), slot_lanes(it, 0, LENGTH)]

    def save_probs(it):
        return pltpu.make_async_copy(slot_of(it), probs_hbm.at[it], pb_sem.at[it % 2])

    def load_probs(it, where):
        return pltpu.make_async_copy(probs_hbm.at[where], slot_of(it), pb_sem.at[2 + it % 2])

    def second_norm(m):
        hidden = ig[m] + dot_nt(obuf[m], wall[3])
        yout[m] = hidden
        normal, _inv = ln_stats(hidden)
        tn2[owner(0, 0), pl.ds(m * LENGTH, LENGTH)] = (normal * gain_two + shift_two).astype(BF)
        tok_far(1, m).start()
        tok_sib(1, m).start()

    def forward_group(it, _):
        m, g = it // GROUPS, it % GROUPS
        at_step(it, 1, lambda: gather_diag(0))

        @pl.when(it == 8)
        def _():
            fz().wait_recv()
            gather_first(1)
            gather_second(1)


        @pl.when(it >= 2)
        def _():
            save_probs(it - 2).wait()

        lanes = pl.ds(pl.multiple_of(g * LANES, LANES), LANES)
        q = qkv[m, 0, :, lanes]
        kk = qkv[m, 1, :, lanes]
        v = qkv[m, 2, :, lanes]
        v_turned = v.T
        for h in range(HEADS_TILE):
            scores = dot_nt(kk, q * head_mask[h])
            for part in range(LENGTH // LANES):
                cols = slice(part * LANES, (part + 1) * LANES)
                shifted = scores[:, cols] * log2_scale + acc[1, m, 0:LENGTH, cols]
                expo = jnp.exp2(shifted - jnp.max(shifted, axis=0, keepdims=True))
                total = jnp.sum(expo, axis=0, keepdims=True)
                gb[h, LENGTH : 2 * LENGTH, slot_lanes(it, part * LANES, LANES)] = (expo * (1.0 / total)).astype(BF)
        mixed = [dot_nn(v_turned[h * HD : (h + 1) * HD], gb[h, LENGTH : 2 * LENGTH, slot_lanes(it, 0, LENGTH)]) for h in range(HEADS_TILE)]
        obuf[m, :, lanes] = jnp.concatenate(mixed, axis=0).T.astype(BF)
        save_probs(it).start()

        @pl.when(g == GROUPS - 1)
        def _():
            second_norm(m)

        return 0

    lax.fori_loop(0, MB * GROUPS, forward_group, 0)
    save_probs(MB * GROUPS - 2).wait()
    save_probs(MB * GROUPS - 1).wait()
    for m in range(MB):
        tok_far(0, m).wait_recv()
        tok_fwd(0, m).start()

    def scatter_ops(block, r1, r1_both, r2, s_one, s_two, rs):
        def one(u, p, b):
            dev = dev_y if p == 0 else dev_x
            rr = rd if b == 1 else (ry if p == 0 else rx)
            return remote(block(rr, u, p), r1(u, p, b), send.at[s_one], rs.at[p, u], dev)

        def two(u, p):
            dev = dev_x if p == 0 else dev_y
            rr = rx if p == 0 else ry
            return remote(block(rr, u, p), r2(u, p), send.at[s_two], rs.at[2 + p, u], dev)

        def start_one(u, parts=(0, 1)):
            for p in parts:
                for b in (1, 0):
                    one(u, p, b).start()

        def start_two(u):
            for p in range(2):
                received(rs.at[p, u], r1_both(u, p))
                mine = block(rx if p == 0 else ry, u, p)
                mine[...] = (mine[...].astype(F32) + r1(u, p, 1)[...].astype(F32)).astype(BF)
                two(u, p).start()

        def own_sum(u, p):
            two(u, p).wait_recv()
            return (
                block(r, u, p)[...].astype(F32)
                + r1(u, p, 0)[...].astype(F32)
                + r2(u, p)[...].astype(F32)
            )

        return start_one, start_two, own_sum

    def unit_lanes(u):
        return pl.ds(UNITS[u][0], UNITS[u][1])

    f_one, f_two, f_sum = scatter_ops(
        lambda rr, u, p: fw.at[p, rr, :, unit_lanes(u)],
        lambda u, p, b: fr1.at[p, b, :, unit_lanes(u)],
        lambda u, p: fr1.at[p, :, :, unit_lanes(u)],
        lambda u, p: fr2.at[p, :, unit_lanes(u)],
        S_F_ONE, S_F_TWO, frs_r,
    )

    def f_far(u, p):
        lanes = pl.ds(UNITS[u][0] - D, UNITS[u][1])
        return remote(fw.at[p, r, :, unit_lanes(u)], fr3.at[p, :, lanes], send.at[S_F_FAR], frs_r.at[4 + p, u], dev_z(2))

    def f_three(u):
        for p in range(2):
            fw[p, r, :, unit_lanes(u)] = f_sum(u, p).astype(BF)
            f_far(u, p).start()

    def g_rows(zz, p, parity):
        start = (zz * 2 + parity) * WIDTH
        if p is None:
            return rows16(start, WIDTH)
        return rows16(start + PART_ROWS[0] * p, PART_ROWS[p])

    def part_rows(p):
        return pl.ds(PART_ROWS[0] * p, PART_ROWS[p])

    a_one, a_two, a_sum = scatter_ops(
        lambda rr, zz, p: wgrad.at[rr, g_rows(zz, p, k)],
        lambda zz, p, b: ar1.at[zz, b, part_rows(p)],
        lambda zz, p: ar1.at[zz, :, part_rows(p)],
        lambda zz, p: ar2.at[zz, part_rows(p)],
        S_A_ONE, S_A_TWO, ars_r,
    )

    def a_near(zz):
        return remote(wgrad.at[r, g_rows(zz, None, k)], ar3.at[zz // 2], send.at[S_A_NEAR], ars_r.at[4, zz // 2], dev_z(1))

    def a_far(zz):
        return remote(wgrad.at[r, g_rows(zz, None, k)], ar3.at[2], send.at[S_A_FAR], ars_r.at[4, 2], dev_z(2))

    def held(i):
        return acc.at[0, owner(1, 0), pl.ds(FEATURES + i * WIDTH, WIDTH)]

    agrad = held(2)

    def a_three(zz):
        total = [a_sum(zz, p) for p in range(2)]

        @pl.when(z % 2 == zz % 2)
        def _():
            for p in range(2):
                held(zz // 2)[part_rows(p)] = total[p]

        @pl.when(z % 2 != zz % 2)
        def _():
            for p in range(2):
                wgrad[r, g_rows(zz, p, k)] = total[p].astype(BF)
            a_near(zz).start()

    def a_four(half):
        zz = half * 2 + z % 2
        a_near(2 * half).wait_recv()
        total = held(half)[...] + ar3[half].astype(F32)

        @pl.when(z == zz)
        def _():
            agrad[...] = total

        @pl.when(z != zz)
        def _():
            wgrad[r, g_rows(zz, None, k)] = total.astype(BF)
            a_far(zz).start()

    def cross(zz):
        return remote(wgrad.at[:, g_rows(zz, None, 1 - k)], rc.at[zz], send.at[S_CROSS], rc_r.at[zz], dev_sib)

    def a_start(zz):
        cross(zz).wait_recv()
        for rr in range(ROWS):
            mine = wgrad.at[rr, g_rows(zz, None, k)]
            mine[...] = (mine[...].astype(F32) + rc[zz, rr].astype(F32)).astype(BF)
        a_one(zz)

    def ffn_tile(i, t, rows=slice(None)):
        first, width = CHUNKS[i]
        up = fw[0, :, :, first : first + width].reshape(D, width)
        down = fw[1, :, :, first : first + width].reshape(D, width)
        act, slope = gelu_pair(dot_nn(tn2[t, rows], up))
        grad_act = dot_nn(tdy[t, rows], down)
        act = act.astype(BF)
        grad_up = (grad_act * slope).astype(BF)
        gb[t, rows, first : first + width] = act
        dub[t, rows, first : first + width] = grad_up
        dn_part = dot_nt(grad_up, up)
        y_part = dot_nt(act, down)
        if i == 0:
            acc[0, t, rows] = dn_part
            acc[1, t, rows] = y_part
        else:
            acc[0, t, rows] += dn_part
            acc[1, t, rows] += y_part

    def token_sums(lanes, left, right, first_owner, owners):
        first, width = lanes
        rows = owners * MB * LENGTH
        span = pl.ds(first_owner, owners)
        return dot_tn(left[span].reshape(rows, D), right[span, :, first : first + width].reshape(rows, width))

    pairs = ((tn2, dub), (tdy, gb))

    def near_grads(unit):
        for p, (left, right) in enumerate(pairs):
            grad = token_sums(UNITS[unit], left, right, (z % 2) * 2, 2)
            wgrad[p, :, 0 : UNITS[unit][1]] = grad.astype(BF)

    def unit_grads(unit, held_near=False):
        first, width = UNITS[unit]
        for p, (left, right) in enumerate(pairs):
            if held_near:
                grad = wgrad[p, :, 0:width].astype(F32) + token_sums(UNITS[unit], left, right, (1 - z % 2) * 2, 2)
            else:
                grad = token_sums(UNITS[unit], left, right, 0, 4)
            fw[p, :, :, first : first + width] = grad.astype(BF).reshape(ROWS, FEATURES, width)

    gathered(0)

    def near_tiles(s, _):
        def sib_tiles():
            for q in range(2):
                for m in range(MB):
                    tok_sib(q, m).wait_recv()

        at_step(s, 1, sib_tiles)
        ffn_tile(0, owner(0, s))
        return 0

    lax.fori_loop(0, 2, near_tiles, 0)

    def far_tiles(s, _):
        m = s // 2
        for m_ in range(MB):

            def arrived(m_=m_):
                tok_far(1, m_).wait_recv()
                tok_fwd(1, m_).start()

            def forwarded(m_=m_):
                for q in range(2):
                    tok_fwd(q, m_).wait_recv()

            if m_ == 1:
                at_step(s, 2, lambda: gather_diag(1))
                at_step(s, 2, lambda: near_grads(0))
            at_step(s, 2 * m_, arrived)
            at_step(s, 2 * m_ + 1, forwarded)
        ffn_tile(0, owner(1, s % 2), pl.ds(pl.multiple_of(m * LENGTH, LENGTH), LENGTH))
        return 0

    lax.fori_loop(0, 2 * MB, far_tiles, 0)
    fz().wait_send()
    gather_sent(0)
    gathered(1)

    def part_sib(q, n):
        return remote(acc.at[q, owner(n, 1)], near.at[q, n], send.at[S_PART], part_r.at[q, n], dev_sib)

    def stage_of(q, m):
        return stage.at[m] if q else wgrad.at[2, pl.ds(m * LENGTH, LENGTH)]

    def part_far(q, m):
        return remote(stage_of(q, m), far.at[q, m], send.at[(S_FAR_DN, S_FAR)[q]], part_r.at[q, 2 + m], dev_z(1))

    def to_far(q):
        part_sib(q, 1).wait_recv()
        for m in range(MB):
            rows = pl.ds(m * LENGTH, LENGTH)
            stage_of(q, m)[...] = (acc[q, owner(1, 0), rows] + near[q, 1, rows]).astype(BF)
            part_far(q, m).start()

    def second_block(s, _):
        ffn_tile(1, owner(1 - s // 2, 1 - s % 2))
        for n in range(2):

            def to_sib(n=n):
                part_sib(0, n).start()
                part_sib(1, n).start()

            at_step(s, 2 * (1 - n), to_sib)
        at_step(s, 1, lambda: to_far(0))

        @pl.when(s == 1)
        def _():
            unit_grads(0, held_near=True)
            f_one(0)

        at_step(s, 3, lambda: to_far(1))
        return 0

    lax.fori_loop(0, 4, second_block, 0)
    gather_sent(1)
    unit_grads(2)
    f_one(2)
    unit_grads(3)
    f_one(3)
    unit_grads(4)
    unit_grads(1)

    zero = jnp.zeros((1, D), F32)
    sent(S_OWN, tn2.at[pl.ds(0, 2)])
    part_sib(0, 0).wait_recv()

    def whole(q, m):
        rows = pl.ds(m * LENGTH, LENGTH)
        return acc[q, owner(0, 0), rows] + near[q, 0, rows] + far[q, m].astype(F32)

    def second_backward(m):
        part_far(0, m).wait_recv()
        normal, inv = ln_stats(yout[m])
        grad = whole(0, m)
        grad_hidden = dyv[m] + ln_backward(normal, inv, gain_two, grad)
        dyv[m] = grad_hidden
        low = grad_hidden.astype(BF)
        dub[m, 0:LENGTH, 0:D] = dot_nn(low, wall[3]).astype(BF)
        tn2[owner(0, 0), pl.ds(m * LENGTH, LENGTH)] = low
        nsum[pl.ds(2, 1)] += jnp.sum(grad * normal, axis=0, keepdims=True)
        nsum[pl.ds(3, 1)] += jnp.sum(grad, axis=0, keepdims=True)

    nsum[...] = jnp.zeros(nsum.shape, F32)
    load_probs(0, 0).start()
    second_backward(0)

    def first_backward(m):
        grad = dot_nn(qkv[m, 0], wall[0]) + dot_nn(qkv[m, 1], wall[1]) + dot_nn(qkv[m, 2], wall[2])
        normal, inv = ln_stats(ig[m])
        ig[m] = dyv[m] + ln_backward(normal, inv, gain_one, grad)
        nsum[pl.ds(0, 1)] += jnp.sum(grad * normal, axis=0, keepdims=True)
        nsum[pl.ds(1, 1)] += jnp.sum(grad, axis=0, keepdims=True)

    def backward_at(it):
        m = jnp.where(it < 6, it // 3, it % 2)
        g = jnp.where(it < 6, it % 3, it // 2)
        return m, g

    def group_grads(g):
        lanes = pl.ds(pl.multiple_of(g * LANES, LANES), LANES)
        for p in range(3):
            grad = dot_tn(qkv[0, p, :, lanes], n1[0]) + dot_tn(qkv[1, p, :, lanes], n1[1])
            wgrad[p, lanes] = grad.astype(BF)

    def backward_group(it, _):
        m, g = backward_at(it)

        at_step(it, 1, lambda: f_two(2))
        at_step(it, 2, lambda: f_one(4))

        @pl.when(it == 3)
        def _():
            second_backward(1)
            sent(S_FAR_DN, wgrad.at[2, pl.ds(0, MB * LENGTH)])
            rows = [tn2[owner(0, 0), pl.ds(i * LENGTH, LENGTH)] for i in range(MB)]
            wgrad[3] = (dot_tn(rows[0], obuf[0]) + dot_tn(rows[1], obuf[1])).astype(BF)

        at_step(it, 3, lambda: f_three(2))
        at_step(it, 3, lambda: f_two(3))
        at_step(it, 5, lambda: f_two(4))
        at_step(it, 5, lambda: f_three(3))
        at_step(it, 6, lambda: a_start(0))
        at_step(it, 7, lambda: f_three(4))
        at_step(it, 7, lambda: a_start(1))
        at_step(it, 9, lambda: a_start(2))
        at_step(it, 9, lambda: a_two(0))

        @pl.when(it + 1 < MB * GROUPS)
        def _():
            m_next, g_next = backward_at(it + 1)
            load_probs(it + 1, m_next * GROUPS + g_next).start()

        load_probs(it, m * GROUPS + g).wait()
        lanes = pl.ds(pl.multiple_of(g * LANES, LANES), LANES)
        q = qkv[m, 0, :, lanes]
        kk = qkv[m, 1, :, lanes]
        v = qkv[m, 2, :, lanes]
        do = dub[m, 0:LENGTH, lanes]
        k_turned = kk.T
        for h in range(HEADS_TILE):
            do_head = do * head_mask[h]
            for part in range(LENGTH // LANES):
                cols = slice(part * LANES, (part + 1) * LANES)
                wide = gb[h, LENGTH : 2 * LENGTH, slot_lanes(it, part * LANES, LANES)].astype(F32)
                product = dot_nt(v, do_head[cols]) * wide
                total = jnp.sum(product, axis=0, keepdims=True)
                gb[h, 0:LENGTH, cols] = (product - wide * total).astype(BF)
        grad_q, grad_k, grad_v = [], None, None
        for h in range(HEADS_TILE):
            v_part = dot_nn(gb[h, LENGTH : 2 * LENGTH, slot_lanes(it, 0, LENGTH)], do * head_mask[h])
            k_part = dot_nn(gb[h, 0:LENGTH, 0:LENGTH], q * head_mask[h])
            grad_v = v_part if grad_v is None else grad_v + v_part
            grad_k = k_part if grad_k is None else grad_k + k_part
            grad_q.append(dot_nn(k_turned[h * HD : (h + 1) * HD], gb[h, 0:LENGTH, 0:LENGTH]))
        qkv[m, 0, :, lanes] = (jnp.concatenate(grad_q, axis=0).T * scale).astype(BF)
        qkv[m, 1, :, lanes] = (grad_k * scale).astype(BF)
        qkv[m, 2, :, lanes] = grad_v.astype(BF)

        @pl.when(m == 1)
        def _():
            group_grads(g)

        at_step(it, 4, lambda: cross(0).start())
        at_step(it, 5, lambda: cross(1).start())
        at_step(it, 7, lambda: cross(2).start())
        at_step(it, 9, lambda: cross(3).start())
        return 0

    lax.fori_loop(0, MB * GROUPS, backward_group, 0)

    def put(i, src, dst):
        return pltpu.make_async_copy(src, dst, out_sem.at[i])

    def put_ffn(p):
        return put(4 + p, acc.at[p, owner(1, 0), pl.ds(0, FEATURES)], fgrad_hbm.at[p])

    first_backward(0)
    a_start(3)
    a_two(1)
    a_two(2)
    first_backward(1)
    for m in range(MB):
        put(m, ig.at[m], ig_hbm.at[m]).start()

    sums = nsum[...]
    lane_own = lax.broadcasted_iota(jnp.int32, (8, LANES), 1) < WIDTH
    for cc in range(COLS):
        shard = pltpu.roll(sums, D - cc * WIDTH, 1) if cc else sums
        shard = jnp.where(lane_own, shard[:, 0:LANES], 0.0)
        for rr in range(ROWS):
            ngrad[rr, cc] = shard[rr : rr + 1]

    def grad_rows(i):
        rr = (rx, ry, rd)[i]
        return remote(ngrad.at[rr], nr1.at[i], send.at[S_G_ONE], norm_r.at[2], (dev_x, dev_y, dev_d)[i])

    def grad_cols(j):
        col = zat(j // 2) * 2 + (k + j % 2) % 2
        return remote(ngrad.at[r, col], nr2.at[j - 1], send.at[S_G_TWO], norm_r.at[3], dev_row(j))

    for i in range(3):
        grad_rows(i).start()
    a_three(0)
    part_sib(1, 0).wait_recv()
    for m in range(MB):
        part_far(1, m).wait_recv()
        yout[m] = yout[m] + whole(1, m)
        put(2 + m, yout.at[m], yout_hbm.at[m]).start()
    a_two(3)
    f_one(1)
    f_two(0)
    a_three(1)
    a_three(2)
    a_three(3)
    received(norm_r.at[2], nr1)
    ngrad[r] = ngrad[r] + nr1[0] + nr1[1] + nr1[2]
    for j in range(1, COLS):
        grad_cols(j).start()
    a_four(0)
    f_two(1)
    a_four(1)
    for u in range(2):
        for p in range(2):
            acc[p, owner(1, 0), 0:FEATURES, unit_lanes(u)] = f_sum(u, p)

    sent(S_GATHER, wall.at[pl.ds(0, 3), pl.ds(0, 5 * WIDTH)])
    sent(S_SIB, wall.at[pl.ds(0, 2)])
    sent(S_TOK, tdy)
    sent(S_PART, acc.at[0])
    sent(S_FAR, stage)
    sent(S_F_ONE, fw.at[0])
    sent(S_F_TWO, fr2)
    sent(S_A_ONE, wgrad.at[0])
    sent(S_A_TWO, ar2)
    sent(S_CROSS, rc)
    sent(S_N_ONE, nr2)
    sent(S_N_TWO, nr1)
    sent(S_G_ONE, nr1)

    for u in FAR_UNITS:
        lanes = pl.ds(UNITS[u][0] - D, UNITS[u][1])
        for p in range(2):
            f_far(u, p).wait_recv()
            acc[p, owner(1, 0), 0:FEATURES, lanes] += fr3[p, :, lanes].astype(F32)
    for p in range(2):
        put_ffn(p).start()
    received(norm_r.at[3], nr2)
    total = ngrad[r, c]
    for j in range(COLS - 1):
        total = total + nr2[j]
    nout[...] = total
    a_far(z).wait_recv()
    agrad[...] = agrad[...] + ar3[2].astype(F32)
    put(6, agrad, agrad_hbm).start()

    sent(S_G_TWO, nr2)
    sent(S_F_FAR, fr3)
    sent(S_A_NEAR, ar3.at[pl.ds(0, 2)])
    sent(S_A_FAR, ar3.at[2])
    for m in range(MB):
        put(m, ig.at[m], ig_hbm.at[m]).wait()
        put(2 + m, yout.at[m], yout_hbm.at[m]).wait()
    for p in range(2):
        put_ffn(p).wait()
    put(6, agrad, agrad_hbm).wait()


def run_step(x, dy, ids, attn_w, norm_w, ffn_w):
    vm = pltpu.VMEM
    dma = pltpu.SemaphoreType.DMA
    any_spec = pl.BlockSpec(memory_space=pl.ANY)
    vspec = pl.BlockSpec(memory_space=pltpu.VMEM)
    tokens = MB * LENGTH
    return pl.pallas_call(
        step_kernel,
        out_shape=(
            jax.ShapeDtypeStruct((MB, LENGTH, D), F32),
            jax.ShapeDtypeStruct((MB, LENGTH, D), F32),
            jax.ShapeDtypeStruct((2, FEATURES, D), F32),
            jax.ShapeDtypeStruct((WIDTH, D), F32),
            jax.ShapeDtypeStruct((1, LANES), F32),
            jax.ShapeDtypeStruct((MB * GROUPS, HEADS_TILE, LENGTH, LENGTH), BF),
        ),
        in_specs=[any_spec, any_spec, any_spec, vspec, any_spec, vspec],
        out_specs=(any_spec, any_spec, any_spec, any_spec, vspec, any_spec),
        scratch_shapes=[
            vm((ROWS, D, D), BF),
            vm((ROWS, D, D), BF),
            vm((2, ROWS, FEATURES, 2 * D), BF),
            vm((MB, LENGTH, D), BF),
            vm((MB, 3, LENGTH, D), BF),
            vm((MB, LENGTH, D), BF),
            vm((4, tokens, D), BF),
            vm((4, tokens, D), BF),
            vm((4, tokens, 2 * D), BF),
            vm((4, tokens, 2 * D), BF),
            vm((2, 4, tokens, D), F32),
            vm((2, 2, tokens, D), F32),
            vm((MB, LENGTH, D), BF),
            vm((2, MB, LENGTH, D), BF),
            vm((MB, LENGTH, D), F32),
            vm((2, 2, FEATURES, 2 * D), BF),
            vm((2, FEATURES, 2 * D), BF),
            vm((2, FEATURES, D), BF),
            vm((Z_SIZE, ROWS, WIDTH, D), BF),
            vm((Z_SIZE, 2, WIDTH, D), BF),
            vm((Z_SIZE, WIDTH, D), BF),
            vm((Z_SIZE - 1, WIDTH, D), BF),
            vm((ROWS, COLS, 1, LANES), F32),
            vm((ROWS, COLS, 1, LANES), F32),
            vm((8, D), F32),
            vm((3, COLS, 1, LANES), F32),
            vm((COLS - 1, 1, LANES), F32),
            vm((MB, LENGTH, D), F32),
            vm((MB, LENGTH, D), F32),
            dma((5,)), dma((4,)), dma((7,)),
            dma((19,)),
            dma((7, 2)),
            dma((5, Z_SIZE)),
            dma((7, 2)),
            dma((Z_SIZE,)),
            dma((2, 3, MB)),
            dma((2, 4)),
            dma((6, len(UNITS))),
            dma((5, Z_SIZE)),
            dma((Z_SIZE,)),
            dma((4,)),
        ],
        compiler_params=pltpu.CompilerParams(
            collective_id=0, has_side_effects=True, vmem_limit_bytes=64 * 1024 * 1024 - 4096
        ),
        name="encoder_step",
    )(x, dy, ffn_w, ids, attn_w, norm_w)


def update_kernel(rate, *refs):
    y_in, g_in, a_in, n_in, f_in = refs[0], refs[1], refs[2:6], refs[6:10], refs[10:14]
    y_out, g_out, a_out, n_out, f_out = refs[14], refs[15], refs[16:21], refs[21:26], refs[26:31]
    yb, gbuf, a_held, f_held, a_low, f_low, in_sem, out_sem = refs[31:]

    def load(i, src, dst):
        return pltpu.make_async_copy(src, dst, in_sem.at[i])

    def save(i, src, dst):
        return pltpu.make_async_copy(src, dst, out_sem.at[i])

    pieces = []
    for s in range(2):
        pieces.append(([v.at[s] for v in f_in], [v.at[s] for v in f_out], f_held.at[s], f_low.at[s]))
    pieces.append((list(a_in), list(a_out), a_held, a_low))
    loads = [
        [load(4 * n + i, src[i], held.at[i]) for i in range(4)]
        for n, (src, dst, held, low) in enumerate(pieces)
    ]
    through = [(load(12, y_in, yb), save(15, yb, y_out)), (load(13, g_in, gbuf), save(16, gbuf, g_out))]
    for copies in loads:
        for copy in copies:
            copy.start()
    for first, _second in through:
        first.start()

    def update(weights, moment, average, grad):
        moment_new = MOMENT_DECAY * moment + grad
        weights_new = weights - rate * (grad + MOMENT_DECAY * moment_new)
        average_new = AVERAGE_DECAY * average + (1.0 - AVERAGE_DECAY) * weights_new
        return moment_new, weights_new, average_new

    grad = n_in[3][:, 0:WIDTH]
    moment, weights, average = update(n_in[0][...], n_in[1][...], n_in[2][...], grad)
    for ref, value in zip(n_out, (grad, moment, weights, average, weights.astype(BF))):
        ref[...] = value

    saves = []
    for n, (src, dst, held, low) in enumerate(pieces):
        for copy in loads[n]:
            copy.wait()
        moment, weights, average = update(held[0], held[1], held[2], held[3])
        held[0] = weights
        held[1] = moment
        held[2] = average
        low[...] = weights.astype(BF)
        for i, value in enumerate((held.at[3], held.at[1], held.at[0], held.at[2], low)):
            saves.append(save(5 * n + i, value, dst[i]))
            saves[-1].start()
    for i, (first, second) in enumerate(through):
        first.wait()
        second.start()
    for copy in saves:
        copy.wait()
    for _first, second in through:
        second.wait()


def run_update(rate, carried, attn, norm, ffn):
    vm = pltpu.VMEM
    any_spec = pl.BlockSpec(memory_space=pltpu.HBM)
    vspec = pl.BlockSpec(memory_space=pltpu.VMEM)
    five = lambda like: [jax.ShapeDtypeStruct(like.shape, F32)] * 4 + [jax.ShapeDtypeStruct(like.shape, BF)]
    out = pl.pallas_call(
        functools.partial(update_kernel, rate),
        out_shape=[jax.ShapeDtypeStruct(v.shape, F32) for v in carried] + five(attn[0]) + five(norm[0]) + five(ffn[0]),
        in_specs=[any_spec] * 6 + [vspec] * 4 + [any_spec] * 4,
        out_specs=[any_spec] * 7 + [vspec] * 5 + [any_spec] * 5,
        scratch_shapes=[
            vm(carried[0].shape, F32),
            vm(carried[1].shape, F32),
            vm((4, *attn[0].shape), F32),
            vm((2, 4, *ffn[0].shape[1:]), F32),
            vm(attn[0].shape, BF),
            vm(ffn[0].shape, BF),
            pltpu.SemaphoreType.DMA((14,)),
            pltpu.SemaphoreType.DMA((17,)),
        ],
        compiler_params=pltpu.CompilerParams(vmem_limit_bytes=64 * 1024 * 1024 - 4096),
        name="update",
    )(*carried, *attn, *norm, *ffn)
    return out[0], out[1], out[2:7], out[7:12], out[12:17]


def local_slice(
    block_input, output_grad, sequence_ids,
    attn_weights, attn_momentum, attn_average,
    norm_params, norm_momentum, norm_average,
    ffn_weights, ffn_momentum, ffn_average,
):
    outputs, grads, ffn_grad, shard, norm_shard, _probs = run_step(
        block_input, output_grad, sequence_ids, attn_weights.T, norm_params[None], ffn_weights
    )
    total_tokens = MB * block_input.shape[1] * lax.axis_size("row") * lax.axis_size("col")
    step_rate = RATE_SCALE * total_tokens ** (-0.5)
    outputs, grads, attn, norm, ffn = run_update(
        step_rate,
        (outputs, grads),
        (attn_weights.T, attn_momentum.T, attn_average.T, shard),
        (norm_params[None], norm_momentum[None], norm_average[None], norm_shard),
        (ffn_weights, ffn_momentum, ffn_average, ffn_grad),
    )
    return (outputs, grads, *[v.T for v in attn], *[v[0] for v in norm], *ffn)


def local(*args):
    on_slice = (
        lax.axis_size("row") == ROWS
        and lax.axis_size("col") == COLS
        and args[0].shape[1] == LENGTH
        and args[3].shape == (D, WIDTH)
        and args[9].shape == (2, FEATURES, D)
    )
    return (local_slice if on_slice else local_general)(*args)


def solution(mesh):
    return jax.shard_map(
        local,
        mesh=mesh,
        in_specs=(
            P(None, ("row", "col"), None),
            P(None, ("row", "col"), None),
            P(None, ("row", "col")),
            P(None, ("row", "col")),
            P(None, ("row", "col")),
            P(None, ("row", "col")),
            P(("row", "col")),
            P(("row", "col")),
            P(("row", "col")),
            P(None, "row", "col"),
            P(None, "row", "col"),
            P(None, "row", "col"),
        ),
        out_specs=(
            P(None, ("row", "col"), None),
            P(None, ("row", "col"), None),
            P(None, ("row", "col")),
            P(None, ("row", "col")),
            P(None, ("row", "col")),
            P(None, ("row", "col")),
            P(None, ("row", "col")),
            P(("row", "col")),
            P(("row", "col")),
            P(("row", "col")),
            P(("row", "col")),
            P(("row", "col")),
            P(None, "row", "col"),
            P(None, "row", "col"),
            P(None, "row", "col"),
            P(None, "row", "col"),
            P(None, "row", "col"),
        ),
        check_vma=False,
    )
```

```python
import functools
import math

import jax
import jax.numpy as jnp
from jax import lax
from jax.experimental import pallas as pl
from jax.experimental.pallas import tpu as pltpu
from jax.sharding import PartitionSpec as P

D = 640
H = 20
HD = 32
MB = 2


EPSILON = 1e-05
MOMENT_DECAY = 0.9
AVERAGE_DECAY = 0.85
RATE_SCALE = 0.06
MASKED = -1e30


def layer_norm(values, gain, shift):
    center = values - jnp.mean(values, axis=-1, keepdims=True)
    spread = jnp.mean(center * center, axis=-1, keepdims=True)
    return center * lax.rsqrt(spread + EPSILON) * gain + shift


def gelu_exact(values):
    return jax.nn.gelu(values, approximate=False)


def matmul(left_side, right_side):
    return jnp.dot(left_side, right_side, preferred_element_type=jnp.float32)


def contract_rows(left_side, right_side):
    return lax.dot_general(
        left_side, right_side, (((0,), (0,)), ((), ())), preferred_element_type=jnp.float32
    )


def contract_cols(left_side, right_side):
    return lax.dot_general(
        left_side, right_side, (((1,), (1,)), ((), ())), preferred_element_type=jnp.float32
    )


def head_slices(qkv_low, first_col, head_group):
    length = qkv_low.shape[0]
    group_width = head_group * HD
    queries = lax.dynamic_slice_in_dim(qkv_low, first_col, group_width, 1).reshape(
        length, head_group, HD
    )
    keys_part = lax.dynamic_slice_in_dim(qkv_low, D + first_col, group_width, 1).reshape(
        length, head_group, HD
    )
    values = lax.dynamic_slice_in_dim(qkv_low, 2 * D + first_col, group_width, 1).reshape(
        length, head_group, HD
    )
    return (queries, keys_part, values)


def masked_scores(queries, keys_part, same_seq):
    scores = jnp.einsum(
        "qhe,khe->hqk", queries, keys_part, preferred_element_type=jnp.float32
    ) * HD ** (-0.5)
    return jnp.where(same_seq[None], scores, MASKED)


def attend_forward(qkv_low, same_seq):
    length = qkv_low.shape[0]
    head_group = math.gcd(H, 4)
    group_width = head_group * HD

    def one_group(group_index, state_all):
        mixed_all, maxima, totals = state_all
        first_col = group_index * group_width
        queries, keys_part, values = head_slices(qkv_low, first_col, head_group)
        scores = masked_scores(queries, keys_part, same_seq)
        row_max = jnp.max(scores, axis=-1, keepdims=True)
        exponent = jnp.exp(scores - row_max)
        row_total = jnp.sum(exponent, axis=-1, keepdims=True)
        attn_probs = (exponent / row_total).astype(jnp.bfloat16)
        mixed_rows = jnp.einsum(
            "hqk,khe->qhe", attn_probs, values, preferred_element_type=jnp.float32
        )
        mixed_all = lax.dynamic_update_slice_in_dim(
            mixed_all, mixed_rows.reshape(length, group_width), first_col, 1
        )
        maxima = lax.dynamic_update_slice_in_dim(
            maxima, row_max[:, :, 0], group_index * head_group, 0
        )
        totals = lax.dynamic_update_slice_in_dim(
            totals, row_total[:, :, 0], group_index * head_group, 0
        )
        return (mixed_all, maxima, totals)

    initial = (
        jnp.zeros((length, D), jnp.float32),
        jnp.zeros((H, length), jnp.float32),
        jnp.zeros((H, length), jnp.float32),
    )
    return lax.fori_loop(0, H // head_group, one_group, initial)


def attend_backward(qkv_low, same_seq, maxima, totals, grad_mixed):
    length = qkv_low.shape[0]
    head_group = math.gcd(H, 4)
    group_width = head_group * HD

    def one_group(group_index, grad_qkv):
        first_col = group_index * group_width
        queries, keys_part, values = head_slices(qkv_low, first_col, head_group)
        grad_part = lax.dynamic_slice_in_dim(grad_mixed, first_col, group_width, 1).reshape(
            length, head_group, HD
        )
        scores = masked_scores(queries, keys_part, same_seq)
        row_max = lax.dynamic_slice_in_dim(maxima, group_index * head_group, head_group, 0)[
            :, :, None
        ]
        row_total = lax.dynamic_slice_in_dim(totals, group_index * head_group, head_group, 0)[
            :, :, None
        ]
        attn_probs = jnp.exp(scores - row_max) / row_total
        grad_probs = jnp.einsum(
            "qhe,khe->hqk", grad_part, values, preferred_element_type=jnp.float32
        )
        grad_values = jnp.einsum(
            "hqk,qhe->khe",
            attn_probs.astype(jnp.bfloat16),
            grad_part,
            preferred_element_type=jnp.float32,
        )
        grad_scores = attn_probs * (
            grad_probs - jnp.sum(grad_probs * attn_probs, axis=-1, keepdims=True)
        )
        grad_scores = grad_scores.astype(jnp.bfloat16)
        grad_queries = jnp.einsum(
            "hqk,khe->qhe", grad_scores, keys_part, preferred_element_type=jnp.float32
        ) * HD ** (-0.5)
        grad_keys = jnp.einsum(
            "hqk,qhe->khe", grad_scores, queries, preferred_element_type=jnp.float32
        ) * HD ** (-0.5)
        for offset, grad_piece in ((0, grad_queries), (D, grad_keys), (2 * D, grad_values)):
            grad_qkv = lax.dynamic_update_slice_in_dim(
                grad_qkv, grad_piece.reshape(length, group_width), offset + first_col, 1
            )
        return grad_qkv

    return lax.fori_loop(0, H // head_group, one_group, jnp.zeros((length, 3 * D), jnp.float32))


def sgd_update(weights_old, moment, average, grad_sum, step_rate):
    moment_new = MOMENT_DECAY * moment + grad_sum
    weights_new = weights_old - step_rate * (grad_sum + MOMENT_DECAY * moment_new)
    average_new = AVERAGE_DECAY * average + (1.0 - AVERAGE_DECAY) * weights_new
    return (moment_new, weights_new, average_new, weights_new.astype(jnp.bfloat16))


def local_general(
    block_input,
    output_grad,
    sequence_ids,
    attn_weights,
    attn_momentum,
    attn_average,
    norm_params,
    norm_momentum,
    norm_average,
    ffn_weights,
    ffn_momentum,
    ffn_average,
):
    attn_full, norm_full = (
        lax.all_gather(attn_weights.astype(jnp.bfloat16), ("row", "col"), axis=1, tiled=True),
        lax.all_gather(norm_params.astype(jnp.bfloat16), ("row", "col"), axis=0, tiled=True),
    )
    norm_values = norm_full.astype(jnp.float32)
    gain_one = norm_values[:D]
    shift_one = norm_values[D : 2 * D]
    gain_two = norm_values[2 * D : 3 * D]
    shift_two = norm_values[3 * D :]
    qkv_weights = attn_full[:, : 3 * D]
    out_weights = attn_full[:, 3 * D :]
    ffn_rows = lax.all_gather(ffn_weights.astype(jnp.bfloat16), "row", axis=1, tiled=True)
    col_width = ffn_weights.shape[2]
    length = block_input.shape[1]
    attn_acc = jnp.zeros((D, 4 * D), jnp.float32)
    norm_acc = jnp.zeros((4 * D,), jnp.float32)
    ffn_acc = jnp.zeros((2, D, col_width), jnp.float32)
    outputs_all = []
    grads_all = []
    for micro_step in range(MB):
        inputs = block_input[micro_step]
        ids_row = sequence_ids[micro_step]
        same_seq = ids_row[:, None] == ids_row[None, :]
        normed, pull_one = jax.vjp(layer_norm, inputs, gain_one, shift_one)
        normed_low = normed.astype(jnp.bfloat16)
        qkv_low = matmul(normed_low, qkv_weights).astype(jnp.bfloat16)
        mixed_all, maxima, totals = attend_forward(qkv_low, same_seq)
        mixed_low = mixed_all.astype(jnp.bfloat16)
        hidden_in = inputs + matmul(mixed_low, out_weights)
        normed_two, pull_two = jax.vjp(layer_norm, hidden_in, gain_two, shift_two)
        normed_two_low = normed_two.astype(jnp.bfloat16)
        grad_out = output_grad[micro_step]
        grad_out_low = grad_out.astype(jnp.bfloat16)
        normed_all = lax.all_gather(normed_two_low, "col", axis=0, tiled=True)
        up_proj = matmul(normed_all, ffn_rows[0])
        activation, pull_gelu = jax.vjp(gelu_exact, up_proj)
        activ_low = activation.astype(jnp.bfloat16)
        ffn_out = lax.psum_scatter(
            contract_cols(activ_low, ffn_rows[1]).astype(jnp.bfloat16),
            "col",
            scatter_dimension=0,
            tiled=True,
        ).astype(jnp.float32)
        grad_all = lax.all_gather(grad_out_low, "col", axis=0, tiled=True)
        grad_act = matmul(grad_all, ffn_rows[1])
        grad_up = pull_gelu(grad_act)[0].astype(jnp.bfloat16)
        grad_normed_two = lax.psum_scatter(
            contract_cols(grad_up, ffn_rows[0]).astype(jnp.bfloat16),
            "col",
            scatter_dimension=0,
            tiled=True,
        ).astype(jnp.float32)
        ffn_acc = ffn_acc + jnp.stack(
            [contract_rows(normed_all, grad_up), contract_rows(grad_all, activ_low)]
        )
        outputs_all.append(hidden_in + ffn_out)
        grad_ln_two, gain_two_grad, shift_two_grad = pull_two(grad_normed_two)
        grad_hidden = grad_out + grad_ln_two
        grad_branch_low = grad_hidden.astype(jnp.bfloat16)
        out_proj_grad = contract_rows(mixed_low, grad_branch_low)
        grad_mixed_low = contract_cols(grad_branch_low, out_weights).astype(jnp.bfloat16)
        grad_qkv_low = attend_backward(qkv_low, same_seq, maxima, totals, grad_mixed_low).astype(
            jnp.bfloat16
        )
        qkv_grad = contract_rows(normed_low, grad_qkv_low)
        grad_normed = contract_cols(grad_qkv_low, qkv_weights)
        grad_ln_one, gain_one_grad, shift_one_grad = pull_one(grad_normed)
        grads_all.append(grad_hidden + grad_ln_one)
        attn_acc = attn_acc + jnp.concatenate([qkv_grad, out_proj_grad], axis=1)
        norm_acc = norm_acc + jnp.concatenate(
            [gain_one_grad, shift_one_grad, gain_two_grad, shift_two_grad]
        )
    ffn_grad = lax.psum_scatter(
        ffn_acc.astype(jnp.bfloat16), "row", scatter_dimension=1, tiled=True
    ).astype(jnp.float32)
    attn_grad, norm_grad = (
        lax.psum_scatter(attn_acc, ("row", "col"), scatter_dimension=1, tiled=True),
        lax.psum_scatter(norm_acc, ("row", "col"), scatter_dimension=0, tiled=True),
    )
    total_tokens = MB * length * lax.axis_size("row") * lax.axis_size("col")
    step_rate = RATE_SCALE * total_tokens ** (-0.5)
    attn_moment_new, attn_new, attn_avg_new, attn_copy = sgd_update(
        attn_weights, attn_momentum, attn_average, attn_grad, step_rate
    )
    norm_moment_new, norm_new, norm_avg_new, norm_copy = sgd_update(
        norm_params, norm_momentum, norm_average, norm_grad, step_rate
    )
    ffn_moment_new, ffn_new, ffn_avg_new, ffn_copy = sgd_update(
        ffn_weights, ffn_momentum, ffn_average, ffn_grad, step_rate
    )
    return (
        jnp.stack(outputs_all),
        jnp.stack(grads_all),
        attn_grad,
        attn_moment_new,
        attn_new,
        attn_avg_new,
        attn_copy,
        norm_grad,
        norm_moment_new,
        norm_new,
        norm_avg_new,
        norm_copy,
        ffn_grad,
        ffn_moment_new,
        ffn_new,
        ffn_avg_new,
        ffn_copy,
    )


MESH_ID = pl.DeviceIdType.MESH
BF = jnp.bfloat16
F32 = jnp.float32
LANES = 128
HEADS_TILE = LANES // HD
GROUPS = D // LANES
Z_SIZE = 4
COLS = 2 * Z_SIZE
ROWS = 4
WIDTH = D // COLS
LENGTH = 256
FEATURES = D // ROWS
PART_ROWS = (48, 32)
UNITS = ((0, 512), (512, 128), (640, 256), (896, 256), (1152, 128))
FAR_UNITS = (2, 3, 4)
CHUNKS = ((0, 512), (512, 768))


def dot_nn(a, b):
    return lax.dot_general(a, b, (((1,), (0,)), ((), ())), preferred_element_type=F32)


def dot_nt(a, b):
    return lax.dot_general(a, b, (((1,), (1,)), ((), ())), preferred_element_type=F32)


def dot_tn(a, b):
    return lax.dot_general(a, b, (((0,), (0,)), ((), ())), preferred_element_type=F32)


def ln_stats(values):
    center = values - jnp.mean(values, axis=-1, keepdims=True)
    spread = jnp.mean(center * center, axis=-1, keepdims=True)
    inv = lax.rsqrt(spread + EPSILON)
    return center * inv, inv


def ln_backward(normal, inv, gain, grad):
    scaled = grad * gain
    mean_one = jnp.mean(scaled, axis=-1, keepdims=True)
    mean_two = jnp.mean(scaled * normal, axis=-1, keepdims=True)
    return inv * (scaled - mean_one - normal * mean_two)


def gelu_pair(u):
    size = jnp.abs(u) * (2.0 ** -0.5)
    t = 1.0 / (1.0 + 0.3275911 * size)
    poly = 0.5 * 1.061405429
    for coef in (-1.453152027, 1.421413741, -0.284496736, 0.254829592):
        poly = poly * t + 0.5 * coef
    bell = jnp.exp2(u * u * (-0.5 * math.log2(math.e)))
    tail = poly * t * bell
    cap = jnp.where(u < 0.0, tail, 1.0 - tail)
    return u * cap, cap + u * (bell * (1.0 / math.sqrt(2.0 * math.pi)))


def step_kernel(
    x_hbm, dy_hbm, ffn_hbm, ids_hbm, attn_hbm, norm_hbm,
    yout_hbm, ig_hbm, fgrad_hbm, agrad_hbm, nout_hbm, probs_hbm,
    wall, wgrad, fw, n1, qkv, obuf, tn2, tdy, gb, dub, acc, near, stage, far, dyv,
    fr1, fr2, fr3, rc, ar1, ar2, ar3, nbuf, ngrad, nsum, nr1, nr2, yout, ig, ids, norm_w, nout,
    ld_sem, pb_sem, out_sem, send, fg_s, ag_r, fg_r, sib_r, tok_r, part_r, frs_r, ars_r, rc_r, norm_r,
):
    r = lax.axis_index("row")
    c = lax.axis_index("col")
    y, x, z, k = r // 2, r % 2, c // 2, c % 2
    rx, ry, rd = y * 2 + (1 - x), (1 - y) * 2 + x, (1 - y) * 2 + (1 - x)
    dev_x = (rx, c)
    dev_y = (ry, c)
    dev_d = (rd, c)
    dev_sib = (r, z * 2 + (1 - k))

    def exclusive(a, b):
        return ((a // 2 + b // 2) % 2) * 2 + (a % 2 + b % 2) % 2

    def zat(j):
        return exclusive(z, j)

    def dev_z(j):
        return (r, zat(j) * 2 + k)

    def dev_row(j):
        return (r, zat(j // 2) * 2 + (k + j % 2) % 2)

    def owner(z_rel, k_rel):
        return ((z + z_rel) % 2) * 2 + (k + k_rel) % 2

    def rows16(start, size):
        return pl.ds(pl.multiple_of(start, 16), size)

    (
        S_GATHER, S_SIB, S_TOK, S_OWN, S_PART, S_FAR, S_F_ONE, S_F_TWO, S_F_FAR,
        S_A_ONE, S_A_TWO, S_A_NEAR, S_A_FAR, S_CROSS, S_N_ONE, S_N_TWO, S_G_ONE, S_G_TWO, S_FAR_DN,
    ) = range(19)

    def sent(i, all_bytes):
        remote(all_bytes, all_bytes, send.at[i], send.at[i], dev_sib).wait_send()

    def received(sem, all_bytes):
        remote(all_bytes, all_bytes, sem, sem, dev_sib).wait_recv()

    def remote(src, dst, ss, rs, dev):
        return pltpu.make_async_remote_copy(
            src_ref=src, dst_ref=dst, send_sem=ss, recv_sem=rs, device_id=dev, device_id_type=MESH_ID
        )

    barrier = pltpu.get_barrier_semaphore()
    for dev in (dev_x, dev_y, dev_d, *[dev_row(j) for j in range(1, COLS)]):
        pl.semaphore_signal(barrier, inc=1, device_id=dev, device_id_type=MESH_ID)

    ld_f = [pltpu.make_async_copy(ffn_hbm.at[s], acc.at[0, s, pl.ds(0, FEATURES)], ld_sem.at[2 + s]) for s in range(2)]
    ld_x = pltpu.make_async_copy(x_hbm, ig, ld_sem.at[0])
    ld_y = pltpu.make_async_copy(dy_hbm, dyv, ld_sem.at[1])
    for s in range(2):
        ld_f[s].start()
    ld_w = pltpu.make_async_copy(attn_hbm, acc.at[1, 2, pl.ds(0, WIDTH)], ld_sem.at[4])
    ld_n = pltpu.make_async_copy(norm_hbm, norm_w, ld_sem.at[5])
    ld_i = pltpu.make_async_copy(ids_hbm, ids, ld_sem.at[6])
    ld_w.start()
    ld_n.start()
    ld_i.start()
    ld_y.start()
    ld_x.start()

    ld_w.wait()
    wall[r, rows16(c * WIDTH, WIDTH)] = acc[1, 2, 0:WIDTH].astype(BF)
    nbuf[r, c] = jnp.zeros((1, LANES), F32)
    ld_n.wait()
    nbuf[r, c, :, 0:WIDTH] = norm_w[...].astype(BF).astype(F32)
    pl.semaphore_wait(barrier, COLS + 2)

    def norm_one(j):
        return remote(nbuf.at[r, c], nbuf.at[r, c], send.at[S_N_ONE], norm_r.at[0], dev_row(j))

    def norm_two(i):
        return remote(nbuf.at[r], nbuf.at[r], send.at[S_N_TWO], norm_r.at[1], (dev_x, dev_y, dev_d)[i])

    def a_rows(j, p):
        start = (zat(j) * 2 + k) * WIDTH
        if p is None:
            return rows16(start, WIDTH)
        return rows16(start + PART_ROWS[0] * p, PART_ROWS[p])

    def gather_ops(piece, part, far_piece, far_dev, ss, rs):
        def cz(j):
            return remote(piece(r, 0), far_piece(j), ss(0, j), rs.at[0, j], far_dev(j))

        def cx(j):
            return remote(piece(r, j), piece(r, j), ss(1, j), rs.at[1, j], dev_x)

        def cy(j):
            return remote(piece(r, j), piece(r, j), ss(2, j), rs.at[2, j], dev_y)

        def cd0(j):
            return remote(part(rx, j, 0), part(rx, j, 0), ss(3, j), rs.at[3, j], dev_y)

        def cd1(j):
            return remote(part(ry, j, 1), part(ry, j, 1), ss(4, j), rs.at[4, j], dev_x)

        return cz, cx, cy, cd0, cd1

    az, ax, ay, ad0, ad1 = gather_ops(
        lambda rr, j: wall.at[rr, a_rows(j, None)],
        lambda rr, j, p: wall.at[rr, a_rows(j, p)],
        lambda j: wall.at[r, a_rows(0, None)],
        dev_z, lambda i, j: send.at[S_GATHER], ag_r,
    )
    def f_copy(src, dst, kind, j, dev):
        return remote(src, dst, fg_s.at[kind, j], fg_r.at[kind, j], dev)

    def f_part(rr, i, p):
        return fw.at[p, rr, :, pl.ds(i * D, D)]

    def fz():
        return f_copy(fw.at[:, r, :, pl.ds(0, D)], fw.at[:, r, :, pl.ds(D, D)], 0, 0, dev_z(2))

    def fx(j, p):
        return f_copy(f_part(r, j, p), f_part(r, j, p), 1 + p, j, dev_x)

    def fy(j, p):
        return f_copy(f_part(r, j, p), f_part(r, j, p), 3 + p, j, dev_y)

    def fd(j, p):
        whose, dev = ((rx, dev_y), (ry, dev_x))[p]
        return f_copy(f_part(whose, j, p), f_part(whose, j, p), 5 + p, j, dev)

    def gather_first(j):
        fx(j, 0).start()
        fy(j, 1).start()

    def gather_second(j):
        fx(j, 1).start()
        fy(j, 0).start()

    def gather_diag(j):
        fx(j, 0).wait_recv()
        fd(j, 0).start()
        fy(j, 1).wait_recv()
        fd(j, 1).start()

    def gathered(j):
        fx(j, 1).wait_recv()
        fy(j, 0).wait_recv()
        fd(j, 0).wait_recv()
        fd(j, 1).wait_recv()

    def gather_sent(j):
        for p in range(2):
            fx(j, p).wait_send()
            fy(j, p).wait_send()
            fd(j, p).wait_send()

    def sib(j):
        ref = wall.at[:, a_rows(j, None)]
        return remote(ref, ref, send.at[S_SIB], sib_r.at[j], dev_sib)

    for j in range(1, COLS):
        norm_one(j).start()
    az(1).start()
    ax(0).start()
    ay(0).start()
    az(2).start()
    az(3).start()

    for s in range(2):
        ld_f[s].wait()
        fw[s, r, :, 0:D] = acc[0, s, 0:FEATURES].astype(BF)
    ld_i.wait()
    ld_y.wait()

    def make_bias(m, _):
        across = jnp.broadcast_to(ids[pl.ds(m, 1)].astype(F32), (LENGTH, LENGTH))
        acc[1, m, 0:LENGTH, 0:LENGTH] = jnp.where(across == across.T, 0.0, MASKED)
        tdy[owner(0, 0), pl.ds(m * LENGTH, LENGTH)] = dyv[m].astype(BF)
        return 0

    lax.fori_loop(0, MB, make_bias, 0)

    def tok_copy(q, n, m, dev, whose):
        ref = (tdy, tn2)[q].at[whose, pl.ds(m * LENGTH, LENGTH)]
        shared = S_OWN if q == 1 and n < 2 else S_TOK
        return remote(ref, ref, send.at[shared], tok_r.at[q, n, m], dev)

    def tok_sib(q, m):
        return tok_copy(q, 0, m, dev_sib, owner(0, 0))

    def tok_far(q, m):
        return tok_copy(q, 1, m, dev_z(1), owner(0, 0))

    def tok_fwd(q, m):
        return tok_copy(q, 2, m, dev_sib, owner(1, 0))

    for m in range(MB):
        tok_sib(0, m).start()

    ax(0).wait_recv()
    ad0(0).start()
    ay(0).wait_recv()
    ad1(0).start()
    az(1).wait_recv()
    ax(1).start()
    ay(1).start()
    for m in range(MB):
        tok_far(0, m).start()
    received(norm_r.at[0], nr2)
    for i in range(3):
        norm_two(i).start()
    for j in (2, 3):
        az(j).wait_recv()
        ax(j).start()
        ay(j).start()
    fz().start()
    for j in (1, 2, 3):
        ax(j).wait_recv()
        ad0(j).start()
        ay(j).wait_recv()
        ad1(j).start()
    gather_first(0)
    received(norm_r.at[1], nr1)

    vectors = None
    for cc in range(COLS):
        shard = jnp.concatenate([nbuf[:, cc, 0, :], jnp.zeros((ROWS, D - LANES), F32)], axis=1)
        shard = pltpu.roll(shard, cc * WIDTH, 1) if cc else shard
        vectors = shard if vectors is None else vectors + shard
    gain_one, shift_one, gain_two, shift_two = [vectors[i : i + 1] for i in range(4)]

    ld_x.wait()

    def first_norm(m, _):
        normal, _inv = ln_stats(ig[m])
        n1[m] = (normal * gain_one + shift_one).astype(BF)
        return 0

    lax.fori_loop(0, MB, first_norm, 0)

    for j in range(Z_SIZE):
        ad0(j).wait_recv()
        ad1(j).wait_recv()
        sib(j).start()
    for j in range(Z_SIZE):
        sib(j).wait_recv()

    gather_second(0)

    def project(i, _):
        rows = dot_nt(n1[...].reshape(MB * LENGTH, D), wall[i]).astype(BF)
        for m in range(MB):
            qkv[m, i] = rows[m * LENGTH : (m + 1) * LENGTH]
        return 0

    lax.fori_loop(0, 3, project, 0)

    lane_head = lax.broadcasted_iota(jnp.int32, (1, LANES), 1) // HD
    head_mask = [jnp.where(lane_head == h, 1.0, 0.0).astype(BF) for h in range(HEADS_TILE)]
    scale = HD ** (-0.5)
    log2_scale = scale * math.log2(math.e)

    def at_step(it, i, fn):
        @pl.when(it == i)
        def _():
            fn()

    def slot_lanes(it, first, size):
        return pl.ds(pl.multiple_of((it % 2) * LENGTH + first, LANES), size)

    def slot_of(it):
        return gb.at[:, pl.ds(LENGTH, LENGTH), slot_lanes(it, 0, LENGTH)]

    def save_probs(it):
        return pltpu.make_async_copy(slot_of(it), probs_hbm.at[it], pb_sem.at[it % 2])

    def load_probs(it, where):
        return pltpu.make_async_copy(probs_hbm.at[where], slot_of(it), pb_sem.at[2 + it % 2])

    def second_norm(m):
        hidden = ig[m] + dot_nt(obuf[m], wall[3])
        yout[m] = hidden
        normal, _inv = ln_stats(hidden)
        tn2[owner(0, 0), pl.ds(m * LENGTH, LENGTH)] = (normal * gain_two + shift_two).astype(BF)
        tok_far(1, m).start()
        tok_sib(1, m).start()

    def forward_group(it, _):
        m, g = it // GROUPS, it % GROUPS
        at_step(it, 1, lambda: gather_diag(0))

        @pl.when(it == 8)
        def _():
            fz().wait_recv()
            gather_first(1)
            gather_second(1)


        @pl.when(it >= 2)
        def _():
            save_probs(it - 2).wait()

        lanes = pl.ds(pl.multiple_of(g * LANES, LANES), LANES)
        q = qkv[m, 0, :, lanes]
        kk = qkv[m, 1, :, lanes]
        v = qkv[m, 2, :, lanes]
        v_turned = v.T
        for h in range(HEADS_TILE):
            scores = dot_nt(kk, q * head_mask[h])
            for part in range(LENGTH // LANES):
                cols = slice(part * LANES, (part + 1) * LANES)
                shifted = scores[:, cols] * log2_scale + acc[1, m, 0:LENGTH, cols]
                expo = jnp.exp2(shifted - jnp.max(shifted, axis=0, keepdims=True))
                total = jnp.sum(expo, axis=0, keepdims=True)
                gb[h, LENGTH : 2 * LENGTH, slot_lanes(it, part * LANES, LANES)] = (expo * (1.0 / total)).astype(BF)
        mixed = [dot_nn(v_turned[h * HD : (h + 1) * HD], gb[h, LENGTH : 2 * LENGTH, slot_lanes(it, 0, LENGTH)]) for h in range(HEADS_TILE)]
        obuf[m, :, lanes] = jnp.concatenate(mixed, axis=0).T.astype(BF)
        save_probs(it).start()

        @pl.when(g == GROUPS - 1)
        def _():
            second_norm(m)

        return 0

    lax.fori_loop(0, MB * GROUPS, forward_group, 0)
    save_probs(MB * GROUPS - 2).wait()
    save_probs(MB * GROUPS - 1).wait()
    for m in range(MB):
        tok_far(0, m).wait_recv()
        tok_fwd(0, m).start()

    def scatter_ops(block, r1, r1_both, r2, s_one, s_two, rs):
        def one(u, p, b):
            dev = dev_y if p == 0 else dev_x
            rr = rd if b == 1 else (ry if p == 0 else rx)
            return remote(block(rr, u, p), r1(u, p, b), send.at[s_one], rs.at[p, u], dev)

        def two(u, p):
            dev = dev_x if p == 0 else dev_y
            rr = rx if p == 0 else ry
            return remote(block(rr, u, p), r2(u, p), send.at[s_two], rs.at[2 + p, u], dev)

        def start_one(u, parts=(0, 1)):
            for p in parts:
                for b in (1, 0):
                    one(u, p, b).start()

        def start_two(u):
            for p in range(2):
                received(rs.at[p, u], r1_both(u, p))
                mine = block(rx if p == 0 else ry, u, p)
                mine[...] = (mine[...].astype(F32) + r1(u, p, 1)[...].astype(F32)).astype(BF)
                two(u, p).start()

        def own_sum(u, p):
            two(u, p).wait_recv()
            return (
                block(r, u, p)[...].astype(F32)
                + r1(u, p, 0)[...].astype(F32)
                + r2(u, p)[...].astype(F32)
            )

        return start_one, start_two, own_sum

    def unit_lanes(u):
        return pl.ds(UNITS[u][0], UNITS[u][1])

    f_one, f_two, f_sum = scatter_ops(
        lambda rr, u, p: fw.at[p, rr, :, unit_lanes(u)],
        lambda u, p, b: fr1.at[p, b, :, unit_lanes(u)],
        lambda u, p: fr1.at[p, :, :, unit_lanes(u)],
        lambda u, p: fr2.at[p, :, unit_lanes(u)],
        S_F_ONE, S_F_TWO, frs_r,
    )

    def f_far(u, p):
        lanes = pl.ds(UNITS[u][0] - D, UNITS[u][1])
        return remote(fw.at[p, r, :, unit_lanes(u)], fr3.at[p, :, lanes], send.at[S_F_FAR], frs_r.at[4 + p, u], dev_z(2))

    def f_three(u):
        for p in range(2):
            fw[p, r, :, unit_lanes(u)] = f_sum(u, p).astype(BF)
            f_far(u, p).start()

    def g_rows(zz, p, parity):
        start = (zz * 2 + parity) * WIDTH
        if p is None:
            return rows16(start, WIDTH)
        return rows16(start + PART_ROWS[0] * p, PART_ROWS[p])

    def part_rows(p):
        return pl.ds(PART_ROWS[0] * p, PART_ROWS[p])

    a_one, a_two, a_sum = scatter_ops(
        lambda rr, zz, p: wgrad.at[rr, g_rows(zz, p, k)],
        lambda zz, p, b: ar1.at[zz, b, part_rows(p)],
        lambda zz, p: ar1.at[zz, :, part_rows(p)],
        lambda zz, p: ar2.at[zz, part_rows(p)],
        S_A_ONE, S_A_TWO, ars_r,
    )

    def a_near(zz):
        return remote(wgrad.at[r, g_rows(zz, None, k)], ar3.at[zz // 2], send.at[S_A_NEAR], ars_r.at[4, zz // 2], dev_z(1))

    def a_far(zz):
        return remote(wgrad.at[r, g_rows(zz, None, k)], ar3.at[2], send.at[S_A_FAR], ars_r.at[4, 2], dev_z(2))

    def held(i):
        return acc.at[0, owner(1, 0), pl.ds(FEATURES + i * WIDTH, WIDTH)]

    agrad = held(2)

    def a_three(zz):
        total = [a_sum(zz, p) for p in range(2)]

        @pl.when(z % 2 == zz % 2)
        def _():
            for p in range(2):
                held(zz // 2)[part_rows(p)] = total[p]

        @pl.when(z % 2 != zz % 2)
        def _():
            for p in range(2):
                wgrad[r, g_rows(zz, p, k)] = total[p].astype(BF)
            a_near(zz).start()

    def a_four(half):
        zz = half * 2 + z % 2
        a_near(2 * half).wait_recv()
        total = held(half)[...] + ar3[half].astype(F32)

        @pl.when(z == zz)
        def _():
            agrad[...] = total

        @pl.when(z != zz)
        def _():
            wgrad[r, g_rows(zz, None, k)] = total.astype(BF)
            a_far(zz).start()

    def cross(zz):
        return remote(wgrad.at[:, g_rows(zz, None, 1 - k)], rc.at[zz], send.at[S_CROSS], rc_r.at[zz], dev_sib)

    def a_start(zz):
        cross(zz).wait_recv()
        for rr in range(ROWS):
            mine = wgrad.at[rr, g_rows(zz, None, k)]
            mine[...] = (mine[...].astype(F32) + rc[zz, rr].astype(F32)).astype(BF)
        a_one(zz)

    def ffn_tile(i, t, rows=slice(None)):
        first, width = CHUNKS[i]
        up = fw[0, :, :, first : first + width].reshape(D, width)
        down = fw[1, :, :, first : first + width].reshape(D, width)
        act, slope = gelu_pair(dot_nn(tn2[t, rows], up))
        grad_act = dot_nn(tdy[t, rows], down)
        act = act.astype(BF)
        grad_up = (grad_act * slope).astype(BF)
        gb[t, rows, first : first + width] = act
        dub[t, rows, first : first + width] = grad_up
        dn_part = dot_nt(grad_up, up)
        y_part = dot_nt(act, down)
        if i == 0:
            acc[0, t, rows] = dn_part
            acc[1, t, rows] = y_part
        else:
            acc[0, t, rows] += dn_part
            acc[1, t, rows] += y_part

    def token_sums(lanes, left, right, first_owner, owners):
        first, width = lanes
        rows = owners * MB * LENGTH
        span = pl.ds(first_owner, owners)
        return dot_tn(left[span].reshape(rows, D), right[span, :, first : first + width].reshape(rows, width))

    pairs = ((tn2, dub), (tdy, gb))

    def near_grads(unit):
        for p, (left, right) in enumerate(pairs):
            grad = token_sums(UNITS[unit], left, right, (z % 2) * 2, 2)
            wgrad[p, :, 0 : UNITS[unit][1]] = grad.astype(BF)

    def unit_grads(unit, held_near=False):
        first, width = UNITS[unit]
        for p, (left, right) in enumerate(pairs):
            if held_near:
                grad = wgrad[p, :, 0:width].astype(F32) + token_sums(UNITS[unit], left, right, (1 - z % 2) * 2, 2)
            else:
                grad = token_sums(UNITS[unit], left, right, 0, 4)
            fw[p, :, :, first : first + width] = grad.astype(BF).reshape(ROWS, FEATURES, width)

    gathered(0)

    def near_tiles(s, _):
        def sib_tiles():
            for q in range(2):
                for m in range(MB):
                    tok_sib(q, m).wait_recv()

        at_step(s, 1, sib_tiles)
        ffn_tile(0, owner(0, s))
        return 0

    lax.fori_loop(0, 2, near_tiles, 0)

    def far_tiles(s, _):
        m = s // 2
        for m_ in range(MB):

            def arrived(m_=m_):
                tok_far(1, m_).wait_recv()
                tok_fwd(1, m_).start()

            def forwarded(m_=m_):
                for q in range(2):
                    tok_fwd(q, m_).wait_recv()

            if m_ == 1:
                at_step(s, 2, lambda: gather_diag(1))
                at_step(s, 2, lambda: near_grads(0))
            at_step(s, 2 * m_, arrived)
            at_step(s, 2 * m_ + 1, forwarded)
        ffn_tile(0, owner(1, s % 2), pl.ds(pl.multiple_of(m * LENGTH, LENGTH), LENGTH))
        return 0

    lax.fori_loop(0, 2 * MB, far_tiles, 0)
    fz().wait_send()
    gather_sent(0)
    gathered(1)

    def part_sib(q, n):
        return remote(acc.at[q, owner(n, 1)], near.at[q, n], send.at[S_PART], part_r.at[q, n], dev_sib)

    def stage_of(q, m):
        return stage.at[m] if q else wgrad.at[2, pl.ds(m * LENGTH, LENGTH)]

    def part_far(q, m):
        return remote(stage_of(q, m), far.at[q, m], send.at[(S_FAR_DN, S_FAR)[q]], part_r.at[q, 2 + m], dev_z(1))

    def to_far(q):
        part_sib(q, 1).wait_recv()
        for m in range(MB):
            rows = pl.ds(m * LENGTH, LENGTH)
            stage_of(q, m)[...] = (acc[q, owner(1, 0), rows] + near[q, 1, rows]).astype(BF)
            part_far(q, m).start()

    def second_block(s, _):
        ffn_tile(1, owner(1 - s // 2, 1 - s % 2))
        for n in range(2):

            def to_sib(n=n):
                part_sib(0, n).start()
                part_sib(1, n).start()

            at_step(s, 2 * (1 - n), to_sib)
        at_step(s, 1, lambda: to_far(0))

        @pl.when(s == 1)
        def _():
            unit_grads(0, held_near=True)
            f_one(0)

        at_step(s, 3, lambda: to_far(1))
        return 0

    lax.fori_loop(0, 4, second_block, 0)
    gather_sent(1)
    unit_grads(2)
    f_one(2)
    unit_grads(3)
    f_one(3)
    unit_grads(4)

    zero = jnp.zeros((1, D), F32)
    part_sib(0, 0).wait_recv()

    def whole(q, m):
        rows = pl.ds(m * LENGTH, LENGTH)
        return acc[q, owner(0, 0), rows] + near[q, 0, rows] + far[q, m].astype(F32)

    def second_backward(m):
        part_far(0, m).wait_recv()
        normal, inv = ln_stats(yout[m])
        grad = whole(0, m)
        grad_hidden = dyv[m] + ln_backward(normal, inv, gain_two, grad)
        dyv[m] = grad_hidden
        low = grad_hidden.astype(BF)
        dub[m, 0:LENGTH, D : 2 * D] = dot_nn(low, wall[3]).astype(BF)
        dub[2 + m, 0:LENGTH, D : 2 * D] = low
        nsum[pl.ds(2, 1)] += jnp.sum(grad * normal, axis=0, keepdims=True)
        nsum[pl.ds(3, 1)] += jnp.sum(grad, axis=0, keepdims=True)

    nsum[...] = jnp.zeros(nsum.shape, F32)
    load_probs(0, 0).start()
    second_backward(0)

    def first_backward(m):
        grad = dot_nn(qkv[m, 0], wall[0]) + dot_nn(qkv[m, 1], wall[1]) + dot_nn(qkv[m, 2], wall[2])
        normal, inv = ln_stats(ig[m])
        ig[m] = dyv[m] + ln_backward(normal, inv, gain_one, grad)
        nsum[pl.ds(0, 1)] += jnp.sum(grad * normal, axis=0, keepdims=True)
        nsum[pl.ds(1, 1)] += jnp.sum(grad, axis=0, keepdims=True)

    def backward_at(it):
        m = jnp.where(it < 6, it // 3, it % 2)
        g = jnp.where(it < 6, it % 3, it // 2)
        return m, g

    def group_grads(g):
        lanes = pl.ds(pl.multiple_of(g * LANES, LANES), LANES)
        for p in range(3):
            grad = dot_tn(qkv[0, p, :, lanes], n1[0]) + dot_tn(qkv[1, p, :, lanes], n1[1])
            wgrad[p, lanes] = grad.astype(BF)

    def backward_group(it, _):
        m, g = backward_at(it)

        at_step(it, 2, lambda: f_two(2))
        at_step(it, 2, lambda: f_one(4))

        @pl.when(it == 3)
        def _():
            second_backward(1)
            sent(S_FAR_DN, wgrad.at[2, pl.ds(0, MB * LENGTH)])
            rows = [dub[2 + i, 0:LENGTH, D : 2 * D] for i in range(MB)]
            wgrad[3] = (dot_tn(rows[0], obuf[0]) + dot_tn(rows[1], obuf[1])).astype(BF)

        at_step(it, 3, lambda: f_two(3))
        at_step(it, 4, lambda: f_three(2))
        at_step(it, 5, lambda: f_two(4))
        at_step(it, 5, lambda: f_three(3))
        at_step(it, 6, lambda: a_start(0))
        at_step(it, 7, lambda: f_three(4))
        at_step(it, 7, lambda: a_start(1))
        at_step(it, 9, lambda: a_start(2))
        at_step(it, 9, lambda: a_two(0))

        @pl.when(it + 1 < MB * GROUPS)
        def _():
            m_next, g_next = backward_at(it + 1)
            load_probs(it + 1, m_next * GROUPS + g_next).start()

        load_probs(it, m * GROUPS + g).wait()
        lanes = pl.ds(pl.multiple_of(g * LANES, LANES), LANES)
        q = qkv[m, 0, :, lanes]
        kk = qkv[m, 1, :, lanes]
        v = qkv[m, 2, :, lanes]
        do = dub[m, 0:LENGTH, pl.ds(pl.multiple_of(D + g * LANES, LANES), LANES)]
        k_turned = kk.T
        for h in range(HEADS_TILE):
            do_head = do * head_mask[h]
            for part in range(LENGTH // LANES):
                cols = slice(part * LANES, (part + 1) * LANES)
                wide = gb[h, LENGTH : 2 * LENGTH, slot_lanes(it, part * LANES, LANES)].astype(F32)
                product = dot_nt(v, do_head[cols]) * wide
                total = jnp.sum(product, axis=0, keepdims=True)
                gb[h, 0:LENGTH, cols] = (product - wide * total).astype(BF)
        grad_q, grad_k, grad_v = [], None, None
        for h in range(HEADS_TILE):
            v_part = dot_nn(gb[h, LENGTH : 2 * LENGTH, slot_lanes(it, 0, LENGTH)], do * head_mask[h])
            k_part = dot_nn(gb[h, 0:LENGTH, 0:LENGTH], q * head_mask[h])
            grad_v = v_part if grad_v is None else grad_v + v_part
            grad_k = k_part if grad_k is None else grad_k + k_part
            grad_q.append(dot_nn(k_turned[h * HD : (h + 1) * HD], gb[h, 0:LENGTH, 0:LENGTH]))
        qkv[m, 0, :, lanes] = (jnp.concatenate(grad_q, axis=0).T * scale).astype(BF)
        qkv[m, 1, :, lanes] = (grad_k * scale).astype(BF)
        qkv[m, 2, :, lanes] = grad_v.astype(BF)

        @pl.when(m == 1)
        def _():
            group_grads(g)

        at_step(it, 4, lambda: cross(0).start())
        at_step(it, 5, lambda: cross(1).start())
        at_step(it, 7, lambda: cross(2).start())
        at_step(it, 9, lambda: cross(3).start())
        return 0

    lax.fori_loop(0, MB * GROUPS, backward_group, 0)

    def put(i, src, dst):
        return pltpu.make_async_copy(src, dst, out_sem.at[i])

    def put_ffn(p):
        return put(4 + p, acc.at[p, owner(1, 0), pl.ds(0, FEATURES)], fgrad_hbm.at[p])

    first_backward(0)
    a_start(3)
    unit_grads(1)
    a_two(1)
    a_two(2)
    first_backward(1)
    for m in range(MB):
        put(m, ig.at[m], ig_hbm.at[m]).start()

    sums = nsum[...]
    lane_own = lax.broadcasted_iota(jnp.int32, (8, LANES), 1) < WIDTH
    for cc in range(COLS):
        shard = pltpu.roll(sums, D - cc * WIDTH, 1) if cc else sums
        shard = jnp.where(lane_own, shard[:, 0:LANES], 0.0)
        for rr in range(ROWS):
            ngrad[rr, cc] = shard[rr : rr + 1]

    def grad_rows(i):
        rr = (rx, ry, rd)[i]
        return remote(ngrad.at[rr], nr1.at[i], send.at[S_G_ONE], norm_r.at[2], (dev_x, dev_y, dev_d)[i])

    def grad_cols(j):
        col = zat(j // 2) * 2 + (k + j % 2) % 2
        return remote(ngrad.at[r, col], nr2.at[j - 1], send.at[S_G_TWO], norm_r.at[3], dev_row(j))

    for i in range(3):
        grad_rows(i).start()
    a_three(0)
    part_sib(1, 0).wait_recv()
    for m in range(MB):
        part_far(1, m).wait_recv()
        yout[m] = yout[m] + whole(1, m)
        put(2 + m, yout.at[m], yout_hbm.at[m]).start()
    a_two(3)
    f_one(1)
    f_two(0)
    a_three(1)
    a_three(2)
    a_three(3)
    received(norm_r.at[2], nr1)
    ngrad[r] = ngrad[r] + nr1[0] + nr1[1] + nr1[2]
    for j in range(1, COLS):
        grad_cols(j).start()
    a_four(0)
    f_two(1)
    a_four(1)
    for u in range(2):
        for p in range(2):
            acc[p, owner(1, 0), 0:FEATURES, unit_lanes(u)] = f_sum(u, p)

    sent(S_GATHER, wall.at[pl.ds(0, 3), pl.ds(0, 5 * WIDTH)])
    sent(S_SIB, wall.at[pl.ds(0, 2)])
    sent(S_TOK, tdy)
    sent(S_OWN, tn2.at[pl.ds(0, 2)])
    sent(S_PART, acc.at[0])
    sent(S_FAR, stage)
    sent(S_F_ONE, fw.at[0])
    sent(S_F_TWO, fr2)
    sent(S_A_ONE, wgrad.at[0])
    sent(S_A_TWO, ar2)
    sent(S_CROSS, rc)
    sent(S_N_ONE, nr2)
    sent(S_N_TWO, nr1)
    sent(S_G_ONE, nr1)

    for u in FAR_UNITS:
        lanes = pl.ds(UNITS[u][0] - D, UNITS[u][1])
        for p in range(2):
            f_far(u, p).wait_recv()
            acc[p, owner(1, 0), 0:FEATURES, lanes] += fr3[p, :, lanes].astype(F32)
    for p in range(2):
        put_ffn(p).start()
    received(norm_r.at[3], nr2)
    total = ngrad[r, c]
    for j in range(COLS - 1):
        total = total + nr2[j]
    nout[...] = total
    put(7, nout, nout_hbm).start()
    a_far(z).wait_recv()
    agrad[...] = agrad[...] + ar3[2].astype(F32)
    put(6, agrad, agrad_hbm).start()

    sent(S_G_TWO, nr2)
    sent(S_F_FAR, fr3)
    sent(S_A_NEAR, ar3.at[pl.ds(0, 2)])
    sent(S_A_FAR, ar3.at[2])
    for m in range(MB):
        put(m, ig.at[m], ig_hbm.at[m]).wait()
        put(2 + m, yout.at[m], yout_hbm.at[m]).wait()
    for p in range(2):
        put_ffn(p).wait()
    put(6, agrad, agrad_hbm).wait()
    put(7, nout, nout_hbm).wait()


def run_step(x, dy, ids, attn_w, norm_w, ffn_w):
    vm = pltpu.VMEM
    dma = pltpu.SemaphoreType.DMA
    any_spec = pl.BlockSpec(memory_space=pl.ANY)
    vspec = pl.BlockSpec(memory_space=pltpu.VMEM)
    tokens = MB * LENGTH
    return pl.pallas_call(
        step_kernel,
        out_shape=(
            jax.ShapeDtypeStruct((MB, LENGTH, D), F32),
            jax.ShapeDtypeStruct((MB, LENGTH, D), F32),
            jax.ShapeDtypeStruct((2, FEATURES, D), F32),
            jax.ShapeDtypeStruct((WIDTH, D), F32),
            jax.ShapeDtypeStruct((1, LANES), F32),
            jax.ShapeDtypeStruct((MB * GROUPS, HEADS_TILE, LENGTH, LENGTH), BF),
        ),
        in_specs=[any_spec] * 6,
        out_specs=(any_spec,) * 6,
        scratch_shapes=[
            vm((ROWS, D, D), BF),
            vm((ROWS, D, D), BF),
            vm((2, ROWS, FEATURES, 2 * D), BF),
            vm((MB, LENGTH, D), BF),
            vm((MB, 3, LENGTH, D), BF),
            vm((MB, LENGTH, D), BF),
            vm((4, tokens, D), BF),
            vm((4, tokens, D), BF),
            vm((4, tokens, 2 * D), BF),
            vm((4, tokens, 2 * D), BF),
            vm((2, 4, tokens, D), F32),
            vm((2, 2, tokens, D), F32),
            vm((MB, LENGTH, D), BF),
            vm((2, MB, LENGTH, D), BF),
            vm((MB, LENGTH, D), F32),
            vm((2, 2, FEATURES, 2 * D), BF),
            vm((2, FEATURES, 2 * D), BF),
            vm((2, FEATURES, D), BF),
            vm((Z_SIZE, ROWS, WIDTH, D), BF),
            vm((Z_SIZE, 2, WIDTH, D), BF),
            vm((Z_SIZE, WIDTH, D), BF),
            vm((Z_SIZE - 1, WIDTH, D), BF),
            vm((ROWS, COLS, 1, LANES), F32),
            vm((ROWS, COLS, 1, LANES), F32),
            vm((8, D), F32),
            vm((3, COLS, 1, LANES), F32),
            vm((COLS - 1, 1, LANES), F32),
            vm((MB, LENGTH, D), F32),
            vm((MB, LENGTH, D), F32),
            vm((MB, LENGTH), jnp.int32),
            vm((1, WIDTH), F32),
            vm((1, LANES), F32),
            dma((7,)), dma((4,)), dma((8,)),
            dma((19,)),
            dma((7, 2)),
            dma((5, Z_SIZE)),
            dma((7, 2)),
            dma((Z_SIZE,)),
            dma((2, 3, MB)),
            dma((2, 4)),
            dma((6, len(UNITS))),
            dma((5, Z_SIZE)),
            dma((Z_SIZE,)),
            dma((4,)),
        ],
        compiler_params=pltpu.CompilerParams(
            collective_id=0, has_side_effects=True, vmem_limit_bytes=64 * 1024 * 1024 - 4096
        ),
        name="encoder_step",
    )(x, dy, ffn_w, ids, attn_w, norm_w)


def update_kernel(rate, *refs):
    y_in, g_in, a_in, n_in, f_in = refs[0], refs[1], refs[2:6], refs[6:10], refs[10:14]
    y_out, g_out, a_out, n_out, f_out = refs[14], refs[15], refs[16:21], refs[21:26], refs[26:31]
    yb, gbuf, a_held, f_held, a_low, f_low, in_sem, out_sem = refs[31:]

    def load(i, src, dst):
        return pltpu.make_async_copy(src, dst, in_sem.at[i])

    def save(i, src, dst):
        return pltpu.make_async_copy(src, dst, out_sem.at[i])

    pieces = []
    for s in range(2):
        pieces.append(([v.at[s] for v in f_in], [v.at[s] for v in f_out], f_held.at[s], f_low.at[s]))
    pieces.append((list(a_in), list(a_out), a_held, a_low))
    loads = [
        [load(4 * n + i, src[i], held.at[i]) for i in range(4)]
        for n, (src, dst, held, low) in enumerate(pieces)
    ]
    through = [(load(12, y_in, yb), save(15, yb, y_out)), (load(13, g_in, gbuf), save(16, gbuf, g_out))]
    for copies in loads:
        for copy in copies:
            copy.start()
    for first, _second in through:
        first.start()

    def update(weights, moment, average, grad):
        moment_new = MOMENT_DECAY * moment + grad
        weights_new = weights - rate * (grad + MOMENT_DECAY * moment_new)
        average_new = AVERAGE_DECAY * average + (1.0 - AVERAGE_DECAY) * weights_new
        return moment_new, weights_new, average_new

    grad = n_in[3][:, 0:WIDTH]
    moment, weights, average = update(n_in[0][...], n_in[1][...], n_in[2][...], grad)
    for ref, value in zip(n_out, (grad, moment, weights, average, weights.astype(BF))):
        ref[...] = value

    saves = []
    for n, (src, dst, held, low) in enumerate(pieces):
        for copy in loads[n]:
            copy.wait()
        moment, weights, average = update(held[0], held[1], held[2], held[3])
        held[0] = weights
        held[1] = moment
        held[2] = average
        low[...] = weights.astype(BF)
        for i, value in enumerate((held.at[3], held.at[1], held.at[0], held.at[2], low)):
            saves.append(save(5 * n + i, value, dst[i]))
            saves[-1].start()
    for i, (first, second) in enumerate(through):
        first.wait()
        second.start()
    for copy in saves:
        copy.wait()
    for _first, second in through:
        second.wait()


def run_update(rate, carried, attn, norm, ffn):
    vm = pltpu.VMEM
    any_spec = pl.BlockSpec(memory_space=pltpu.HBM)
    vspec = pl.BlockSpec(memory_space=pltpu.VMEM)
    five = lambda like: [jax.ShapeDtypeStruct(like.shape, F32)] * 4 + [jax.ShapeDtypeStruct(like.shape, BF)]
    out = pl.pallas_call(
        functools.partial(update_kernel, rate),
        out_shape=[jax.ShapeDtypeStruct(v.shape, F32) for v in carried] + five(attn[0]) + five(norm[0]) + five(ffn[0]),
        in_specs=[any_spec] * 6 + [vspec] * 4 + [any_spec] * 4,
        out_specs=[any_spec] * 7 + [vspec] * 5 + [any_spec] * 5,
        scratch_shapes=[
            vm(carried[0].shape, F32),
            vm(carried[1].shape, F32),
            vm((4, *attn[0].shape), F32),
            vm((2, 4, *ffn[0].shape[1:]), F32),
            vm(attn[0].shape, BF),
            vm(ffn[0].shape, BF),
            pltpu.SemaphoreType.DMA((14,)),
            pltpu.SemaphoreType.DMA((17,)),
        ],
        compiler_params=pltpu.CompilerParams(vmem_limit_bytes=64 * 1024 * 1024 - 4096),
        name="update",
    )(*carried, *attn, *norm, *ffn)
    return out[0], out[1], out[2:7], out[7:12], out[12:17]


def local_slice(
    block_input, output_grad, sequence_ids,
    attn_weights, attn_momentum, attn_average,
    norm_params, norm_momentum, norm_average,
    ffn_weights, ffn_momentum, ffn_average,
):
    outputs, grads, ffn_grad, shard, norm_shard, _probs = run_step(
        block_input, output_grad, sequence_ids, attn_weights.T, norm_params[None], ffn_weights
    )
    total_tokens = MB * block_input.shape[1] * lax.axis_size("row") * lax.axis_size("col")
    step_rate = RATE_SCALE * total_tokens ** (-0.5)
    outputs, grads, attn, norm, ffn = run_update(
        step_rate,
        (outputs, grads),
        (attn_weights.T, attn_momentum.T, attn_average.T, shard),
        (norm_params[None], norm_momentum[None], norm_average[None], norm_shard),
        (ffn_weights, ffn_momentum, ffn_average, ffn_grad),
    )
    return (outputs, grads, *[v.T for v in attn], *[v[0] for v in norm], *ffn)


def local(*args):
    on_slice = (
        lax.axis_size("row") == ROWS
        and lax.axis_size("col") == COLS
        and args[0].shape[1] == LENGTH
        and args[3].shape == (D, WIDTH)
        and args[9].shape == (2, FEATURES, D)
    )
    return (local_slice if on_slice else local_general)(*args)


def solution(mesh):
    return jax.shard_map(
        local,
        mesh=mesh,
        in_specs=(
            P(None, ("row", "col"), None),
            P(None, ("row", "col"), None),
            P(None, ("row", "col")),
            P(None, ("row", "col")),
            P(None, ("row", "col")),
            P(None, ("row", "col")),
            P(("row", "col")),
            P(("row", "col")),
            P(("row", "col")),
            P(None, "row", "col"),
            P(None, "row", "col"),
            P(None, "row", "col"),
        ),
        out_specs=(
            P(None, ("row", "col"), None),
            P(None, ("row", "col"), None),
            P(None, ("row", "col")),
            P(None, ("row", "col")),
            P(None, ("row", "col")),
            P(None, ("row", "col")),
            P(None, ("row", "col")),
            P(("row", "col")),
            P(("row", "col")),
            P(("row", "col")),
            P(("row", "col")),
            P(("row", "col")),
            P(None, "row", "col"),
            P(None, "row", "col"),
            P(None, "row", "col"),
            P(None, "row", "col"),
            P(None, "row", "col"),
        ),
        check_vma=False,
    )
```

```python
import functools
import math

import jax
import jax.numpy as jnp
from jax import lax
from jax.experimental import pallas as pl
from jax.experimental.pallas import tpu as pltpu
from jax.sharding import PartitionSpec as P

D = 640
H = 20
HD = 32
MB = 2


EPSILON = 1e-05
MOMENT_DECAY = 0.9
AVERAGE_DECAY = 0.85
RATE_SCALE = 0.06
MASKED = -1e30


def layer_norm(values, gain, shift):
    center = values - jnp.mean(values, axis=-1, keepdims=True)
    spread = jnp.mean(center * center, axis=-1, keepdims=True)
    return center * lax.rsqrt(spread + EPSILON) * gain + shift


def gelu_exact(values):
    return jax.nn.gelu(values, approximate=False)


def matmul(left_side, right_side):
    return jnp.dot(left_side, right_side, preferred_element_type=jnp.float32)


def contract_rows(left_side, right_side):
    return lax.dot_general(
        left_side, right_side, (((0,), (0,)), ((), ())), preferred_element_type=jnp.float32
    )


def contract_cols(left_side, right_side):
    return lax.dot_general(
        left_side, right_side, (((1,), (1,)), ((), ())), preferred_element_type=jnp.float32
    )


def head_slices(qkv_low, first_col, head_group):
    length = qkv_low.shape[0]
    group_width = head_group * HD
    queries = lax.dynamic_slice_in_dim(qkv_low, first_col, group_width, 1).reshape(
        length, head_group, HD
    )
    keys_part = lax.dynamic_slice_in_dim(qkv_low, D + first_col, group_width, 1).reshape(
        length, head_group, HD
    )
    values = lax.dynamic_slice_in_dim(qkv_low, 2 * D + first_col, group_width, 1).reshape(
        length, head_group, HD
    )
    return (queries, keys_part, values)


def masked_scores(queries, keys_part, same_seq):
    scores = jnp.einsum(
        "qhe,khe->hqk", queries, keys_part, preferred_element_type=jnp.float32
    ) * HD ** (-0.5)
    return jnp.where(same_seq[None], scores, MASKED)


def attend_forward(qkv_low, same_seq):
    length = qkv_low.shape[0]
    head_group = math.gcd(H, 4)
    group_width = head_group * HD

    def one_group(group_index, state_all):
        mixed_all, maxima, totals = state_all
        first_col = group_index * group_width
        queries, keys_part, values = head_slices(qkv_low, first_col, head_group)
        scores = masked_scores(queries, keys_part, same_seq)
        row_max = jnp.max(scores, axis=-1, keepdims=True)
        exponent = jnp.exp(scores - row_max)
        row_total = jnp.sum(exponent, axis=-1, keepdims=True)
        attn_probs = (exponent / row_total).astype(jnp.bfloat16)
        mixed_rows = jnp.einsum(
            "hqk,khe->qhe", attn_probs, values, preferred_element_type=jnp.float32
        )
        mixed_all = lax.dynamic_update_slice_in_dim(
            mixed_all, mixed_rows.reshape(length, group_width), first_col, 1
        )
        maxima = lax.dynamic_update_slice_in_dim(
            maxima, row_max[:, :, 0], group_index * head_group, 0
        )
        totals = lax.dynamic_update_slice_in_dim(
            totals, row_total[:, :, 0], group_index * head_group, 0
        )
        return (mixed_all, maxima, totals)

    initial = (
        jnp.zeros((length, D), jnp.float32),
        jnp.zeros((H, length), jnp.float32),
        jnp.zeros((H, length), jnp.float32),
    )
    return lax.fori_loop(0, H // head_group, one_group, initial)


def attend_backward(qkv_low, same_seq, maxima, totals, grad_mixed):
    length = qkv_low.shape[0]
    head_group = math.gcd(H, 4)
    group_width = head_group * HD

    def one_group(group_index, grad_qkv):
        first_col = group_index * group_width
        queries, keys_part, values = head_slices(qkv_low, first_col, head_group)
        grad_part = lax.dynamic_slice_in_dim(grad_mixed, first_col, group_width, 1).reshape(
            length, head_group, HD
        )
        scores = masked_scores(queries, keys_part, same_seq)
        row_max = lax.dynamic_slice_in_dim(maxima, group_index * head_group, head_group, 0)[
            :, :, None
        ]
        row_total = lax.dynamic_slice_in_dim(totals, group_index * head_group, head_group, 0)[
            :, :, None
        ]
        attn_probs = jnp.exp(scores - row_max) / row_total
        grad_probs = jnp.einsum(
            "qhe,khe->hqk", grad_part, values, preferred_element_type=jnp.float32
        )
        grad_values = jnp.einsum(
            "hqk,qhe->khe",
            attn_probs.astype(jnp.bfloat16),
            grad_part,
            preferred_element_type=jnp.float32,
        )
        grad_scores = attn_probs * (
            grad_probs - jnp.sum(grad_probs * attn_probs, axis=-1, keepdims=True)
        )
        grad_scores = grad_scores.astype(jnp.bfloat16)
        grad_queries = jnp.einsum(
            "hqk,khe->qhe", grad_scores, keys_part, preferred_element_type=jnp.float32
        ) * HD ** (-0.5)
        grad_keys = jnp.einsum(
            "hqk,qhe->khe", grad_scores, queries, preferred_element_type=jnp.float32
        ) * HD ** (-0.5)
        for offset, grad_piece in ((0, grad_queries), (D, grad_keys), (2 * D, grad_values)):
            grad_qkv = lax.dynamic_update_slice_in_dim(
                grad_qkv, grad_piece.reshape(length, group_width), offset + first_col, 1
            )
        return grad_qkv

    return lax.fori_loop(0, H // head_group, one_group, jnp.zeros((length, 3 * D), jnp.float32))


def sgd_update(weights_old, moment, average, grad_sum, step_rate):
    moment_new = MOMENT_DECAY * moment + grad_sum
    weights_new = weights_old - step_rate * (grad_sum + MOMENT_DECAY * moment_new)
    average_new = AVERAGE_DECAY * average + (1.0 - AVERAGE_DECAY) * weights_new
    return (moment_new, weights_new, average_new, weights_new.astype(jnp.bfloat16))


def local_general(
    block_input,
    output_grad,
    sequence_ids,
    attn_weights,
    attn_momentum,
    attn_average,
    norm_params,
    norm_momentum,
    norm_average,
    ffn_weights,
    ffn_momentum,
    ffn_average,
):
    attn_full, norm_full = (
        lax.all_gather(attn_weights.astype(jnp.bfloat16), ("row", "col"), axis=1, tiled=True),
        lax.all_gather(norm_params.astype(jnp.bfloat16), ("row", "col"), axis=0, tiled=True),
    )
    norm_values = norm_full.astype(jnp.float32)
    gain_one = norm_values[:D]
    shift_one = norm_values[D : 2 * D]
    gain_two = norm_values[2 * D : 3 * D]
    shift_two = norm_values[3 * D :]
    qkv_weights = attn_full[:, : 3 * D]
    out_weights = attn_full[:, 3 * D :]
    ffn_rows = lax.all_gather(ffn_weights.astype(jnp.bfloat16), "row", axis=1, tiled=True)
    col_width = ffn_weights.shape[2]
    length = block_input.shape[1]
    attn_acc = jnp.zeros((D, 4 * D), jnp.float32)
    norm_acc = jnp.zeros((4 * D,), jnp.float32)
    ffn_acc = jnp.zeros((2, D, col_width), jnp.float32)
    outputs_all = []
    grads_all = []
    for micro_step in range(MB):
        inputs = block_input[micro_step]
        ids_row = sequence_ids[micro_step]
        same_seq = ids_row[:, None] == ids_row[None, :]
        normed, pull_one = jax.vjp(layer_norm, inputs, gain_one, shift_one)
        normed_low = normed.astype(jnp.bfloat16)
        qkv_low = matmul(normed_low, qkv_weights).astype(jnp.bfloat16)
        mixed_all, maxima, totals = attend_forward(qkv_low, same_seq)
        mixed_low = mixed_all.astype(jnp.bfloat16)
        hidden_in = inputs + matmul(mixed_low, out_weights)
        normed_two, pull_two = jax.vjp(layer_norm, hidden_in, gain_two, shift_two)
        normed_two_low = normed_two.astype(jnp.bfloat16)
        grad_out = output_grad[micro_step]
        grad_out_low = grad_out.astype(jnp.bfloat16)
        normed_all = lax.all_gather(normed_two_low, "col", axis=0, tiled=True)
        up_proj = matmul(normed_all, ffn_rows[0])
        activation, pull_gelu = jax.vjp(gelu_exact, up_proj)
        activ_low = activation.astype(jnp.bfloat16)
        ffn_out = lax.psum_scatter(
            contract_cols(activ_low, ffn_rows[1]).astype(jnp.bfloat16),
            "col",
            scatter_dimension=0,
            tiled=True,
        ).astype(jnp.float32)
        grad_all = lax.all_gather(grad_out_low, "col", axis=0, tiled=True)
        grad_act = matmul(grad_all, ffn_rows[1])
        grad_up = pull_gelu(grad_act)[0].astype(jnp.bfloat16)
        grad_normed_two = lax.psum_scatter(
            contract_cols(grad_up, ffn_rows[0]).astype(jnp.bfloat16),
            "col",
            scatter_dimension=0,
            tiled=True,
        ).astype(jnp.float32)
        ffn_acc = ffn_acc + jnp.stack(
            [contract_rows(normed_all, grad_up), contract_rows(grad_all, activ_low)]
        )
        outputs_all.append(hidden_in + ffn_out)
        grad_ln_two, gain_two_grad, shift_two_grad = pull_two(grad_normed_two)
        grad_hidden = grad_out + grad_ln_two
        grad_branch_low = grad_hidden.astype(jnp.bfloat16)
        out_proj_grad = contract_rows(mixed_low, grad_branch_low)
        grad_mixed_low = contract_cols(grad_branch_low, out_weights).astype(jnp.bfloat16)
        grad_qkv_low = attend_backward(qkv_low, same_seq, maxima, totals, grad_mixed_low).astype(
            jnp.bfloat16
        )
        qkv_grad = contract_rows(normed_low, grad_qkv_low)
        grad_normed = contract_cols(grad_qkv_low, qkv_weights)
        grad_ln_one, gain_one_grad, shift_one_grad = pull_one(grad_normed)
        grads_all.append(grad_hidden + grad_ln_one)
        attn_acc = attn_acc + jnp.concatenate([qkv_grad, out_proj_grad], axis=1)
        norm_acc = norm_acc + jnp.concatenate(
            [gain_one_grad, shift_one_grad, gain_two_grad, shift_two_grad]
        )
    ffn_grad = lax.psum_scatter(
        ffn_acc.astype(jnp.bfloat16), "row", scatter_dimension=1, tiled=True
    ).astype(jnp.float32)
    attn_grad, norm_grad = (
        lax.psum_scatter(attn_acc, ("row", "col"), scatter_dimension=1, tiled=True),
        lax.psum_scatter(norm_acc, ("row", "col"), scatter_dimension=0, tiled=True),
    )
    total_tokens = MB * length * lax.axis_size("row") * lax.axis_size("col")
    step_rate = RATE_SCALE * total_tokens ** (-0.5)
    attn_moment_new, attn_new, attn_avg_new, attn_copy = sgd_update(
        attn_weights, attn_momentum, attn_average, attn_grad, step_rate
    )
    norm_moment_new, norm_new, norm_avg_new, norm_copy = sgd_update(
        norm_params, norm_momentum, norm_average, norm_grad, step_rate
    )
    ffn_moment_new, ffn_new, ffn_avg_new, ffn_copy = sgd_update(
        ffn_weights, ffn_momentum, ffn_average, ffn_grad, step_rate
    )
    return (
        jnp.stack(outputs_all),
        jnp.stack(grads_all),
        attn_grad,
        attn_moment_new,
        attn_new,
        attn_avg_new,
        attn_copy,
        norm_grad,
        norm_moment_new,
        norm_new,
        norm_avg_new,
        norm_copy,
        ffn_grad,
        ffn_moment_new,
        ffn_new,
        ffn_avg_new,
        ffn_copy,
    )


MESH_ID = pl.DeviceIdType.MESH
BF = jnp.bfloat16
F32 = jnp.float32
LANES = 128
HEADS_TILE = LANES // HD
GROUPS = D // LANES
Z_SIZE = 4
COLS = 2 * Z_SIZE
ROWS = 4
WIDTH = D // COLS
LENGTH = 256
FEATURES = D // ROWS
PART_ROWS = (48, 32)
UNITS = ((0, 512), (512, 128), (640, 256), (896, 256), (1152, 128))
FAR_UNITS = (2, 3, 4)
CHUNKS = ((0, 512), (512, 768))


def dot_nn(a, b):
    return lax.dot_general(a, b, (((1,), (0,)), ((), ())), preferred_element_type=F32)


def dot_nt(a, b):
    return lax.dot_general(a, b, (((1,), (1,)), ((), ())), preferred_element_type=F32)


def dot_tn(a, b):
    return lax.dot_general(a, b, (((0,), (0,)), ((), ())), preferred_element_type=F32)


def ln_stats(values):
    center = values - jnp.mean(values, axis=-1, keepdims=True)
    spread = jnp.mean(center * center, axis=-1, keepdims=True)
    inv = lax.rsqrt(spread + EPSILON)
    return center * inv, inv


def ln_backward(normal, inv, gain, grad):
    scaled = grad * gain
    mean_one = jnp.mean(scaled, axis=-1, keepdims=True)
    mean_two = jnp.mean(scaled * normal, axis=-1, keepdims=True)
    return inv * (scaled - mean_one - normal * mean_two)


def gelu_pair(u):
    size = jnp.abs(u) * (2.0 ** -0.5)
    t = 1.0 / (1.0 + 0.3275911 * size)
    poly = 0.5 * 1.061405429
    for coef in (-1.453152027, 1.421413741, -0.284496736, 0.254829592):
        poly = poly * t + 0.5 * coef
    bell = jnp.exp2(u * u * (-0.5 * math.log2(math.e)))
    tail = poly * t * bell
    cap = jnp.where(u < 0.0, tail, 1.0 - tail)
    return u * cap, cap + u * (bell * (1.0 / math.sqrt(2.0 * math.pi)))


def step_kernel(
    x_hbm, dy_hbm, ffn_hbm, ids_hbm, attn_hbm, norm_hbm,
    yout_hbm, ig_hbm, fgrad_hbm, agrad_hbm, nout_hbm, probs_hbm,
    wall, wgrad, fw, n1, qkv, obuf, tn2, tdy, gb, dub, acc, near, stage, far, dyv,
    fr1, fr2, fr3, rc, ar1, ar2, ar3, nbuf, ngrad, nsum, nr1, nr2, yout, ig, ids, norm_w, nout,
    ld_sem, pb_sem, out_sem, send, fg_s, ag_r, fg_r, sib_r, tok_r, part_r, frs_r, ars_r, rc_r, norm_r,
):
    r = lax.axis_index("row")
    c = lax.axis_index("col")
    y, x, z, k = r // 2, r % 2, c // 2, c % 2
    rx, ry, rd = y * 2 + (1 - x), (1 - y) * 2 + x, (1 - y) * 2 + (1 - x)
    dev_x = (rx, c)
    dev_y = (ry, c)
    dev_d = (rd, c)
    dev_sib = (r, z * 2 + (1 - k))

    def exclusive(a, b):
        return ((a // 2 + b // 2) % 2) * 2 + (a % 2 + b % 2) % 2

    def zat(j):
        return exclusive(z, j)

    def dev_z(j):
        return (r, zat(j) * 2 + k)

    def dev_row(j):
        return (r, zat(j // 2) * 2 + (k + j % 2) % 2)

    def owner(z_rel, k_rel):
        return ((z + z_rel) % 2) * 2 + (k + k_rel) % 2

    def rows16(start, size):
        return pl.ds(pl.multiple_of(start, 16), size)

    (
        S_GATHER, S_SIB, S_TOK, S_OWN, S_PART, S_FAR, S_F_ONE, S_F_TWO, S_F_FAR,
        S_A_ONE, S_A_TWO, S_A_NEAR, S_A_FAR, S_CROSS, S_N_ONE, S_N_TWO, S_G_ONE, S_G_TWO, S_FAR_DN,
    ) = range(19)

    def sent(i, all_bytes):
        remote(all_bytes, all_bytes, send.at[i], send.at[i], dev_sib).wait_send()

    def received(sem, all_bytes):
        remote(all_bytes, all_bytes, sem, sem, dev_sib).wait_recv()

    def remote(src, dst, ss, rs, dev):
        return pltpu.make_async_remote_copy(
            src_ref=src, dst_ref=dst, send_sem=ss, recv_sem=rs, device_id=dev, device_id_type=MESH_ID
        )

    barrier = pltpu.get_barrier_semaphore()
    for dev in (dev_x, dev_y, dev_d, *[dev_row(j) for j in range(1, COLS)]):
        pl.semaphore_signal(barrier, inc=1, device_id=dev, device_id_type=MESH_ID)

    ld_f = [pltpu.make_async_copy(ffn_hbm.at[s], acc.at[0, s, pl.ds(0, FEATURES)], ld_sem.at[2 + s]) for s in range(2)]
    ld_x = pltpu.make_async_copy(x_hbm, ig, ld_sem.at[0])
    ld_y = pltpu.make_async_copy(dy_hbm, dyv, ld_sem.at[1])
    for s in range(2):
        ld_f[s].start()
    ld_w = pltpu.make_async_copy(attn_hbm, acc.at[1, 2, pl.ds(0, WIDTH)], ld_sem.at[4])
    ld_n = pltpu.make_async_copy(norm_hbm, norm_w, ld_sem.at[5])
    ld_i = pltpu.make_async_copy(ids_hbm, ids, ld_sem.at[6])
    ld_w.start()
    ld_n.start()
    ld_i.start()
    ld_y.start()
    ld_x.start()

    ld_w.wait()
    wall[r, rows16(c * WIDTH, WIDTH)] = acc[1, 2, 0:WIDTH].astype(BF)
    nbuf[r, c] = jnp.zeros((1, LANES), F32)
    ld_n.wait()
    nbuf[r, c, :, 0:WIDTH] = norm_w[...].astype(BF).astype(F32)
    pl.semaphore_wait(barrier, COLS + 2)

    def norm_one(j):
        return remote(nbuf.at[r, c], nbuf.at[r, c], send.at[S_N_ONE], norm_r.at[0], dev_row(j))

    def norm_two(i):
        return remote(nbuf.at[r], nbuf.at[r], send.at[S_N_TWO], norm_r.at[1], (dev_x, dev_y, dev_d)[i])

    def a_rows(j, p):
        start = (zat(j) * 2 + k) * WIDTH
        if p is None:
            return rows16(start, WIDTH)
        return rows16(start + PART_ROWS[0] * p, PART_ROWS[p])

    def gather_ops(piece, part, far_piece, far_dev, ss, rs):
        def cz(j):
            return remote(piece(r, 0), far_piece(j), ss(0, j), rs.at[0, j], far_dev(j))

        def cx(j):
            return remote(piece(r, j), piece(r, j), ss(1, j), rs.at[1, j], dev_x)

        def cy(j):
            return remote(piece(r, j), piece(r, j), ss(2, j), rs.at[2, j], dev_y)

        def cd0(j):
            return remote(part(rx, j, 0), part(rx, j, 0), ss(3, j), rs.at[3, j], dev_y)

        def cd1(j):
            return remote(part(ry, j, 1), part(ry, j, 1), ss(4, j), rs.at[4, j], dev_x)

        return cz, cx, cy, cd0, cd1

    az, ax, ay, ad0, ad1 = gather_ops(
        lambda rr, j: wall.at[rr, a_rows(j, None)],
        lambda rr, j, p: wall.at[rr, a_rows(j, p)],
        lambda j: wall.at[r, a_rows(0, None)],
        dev_z, lambda i, j: send.at[S_GATHER], ag_r,
    )
    def f_copy(src, dst, kind, j, dev):
        return remote(src, dst, fg_s.at[j if kind else 2], fg_r.at[kind, j], dev)

    def f_part(rr, i, p):
        return fw.at[p, rr, :, pl.ds(i * D, D)]

    def fz():
        return f_copy(fw.at[:, r, :, pl.ds(0, D)], fw.at[:, r, :, pl.ds(D, D)], 0, 0, dev_z(2))

    def fx(j, p):
        return f_copy(f_part(r, j, p), f_part(r, j, p), 1 + p, j, dev_x)

    def fy(j, p):
        return f_copy(f_part(r, j, p), f_part(r, j, p), 3 + p, j, dev_y)

    def fd(j, p):
        whose, dev = ((rx, dev_y), (ry, dev_x))[p]
        return f_copy(f_part(whose, j, p), f_part(whose, j, p), 5 + p, j, dev)

    def gather_first(j):
        fx(j, 0).start()
        fy(j, 1).start()

    def gather_second(j):
        fx(j, 1).start()
        fy(j, 0).start()

    def gather_diag(j):
        fx(j, 0).wait_recv()
        fd(j, 0).start()
        fy(j, 1).wait_recv()
        fd(j, 1).start()

    def gathered(j):
        fx(j, 1).wait_recv()
        fy(j, 0).wait_recv()
        fd(j, 0).wait_recv()
        fd(j, 1).wait_recv()

    def gather_sent(j):
        six = fw.at[:, pl.ds(0, 3), :, pl.ds(0, D)]
        remote(six, six, fg_s.at[j], fg_s.at[j], dev_sib).wait_send()

    def sib(j):
        ref = wall.at[:, a_rows(j, None)]
        return remote(ref, ref, send.at[S_SIB], sib_r.at[j], dev_sib)

    for j in range(1, COLS):
        norm_one(j).start()
    az(1).start()
    ax(0).start()
    ay(0).start()
    az(2).start()
    az(3).start()

    for s in range(2):
        ld_f[s].wait()
        fw[s, r, :, 0:D] = acc[0, s, 0:FEATURES].astype(BF)
    ld_i.wait()
    ld_y.wait()

    def make_bias(m, _):
        across = jnp.broadcast_to(ids[pl.ds(m, 1)].astype(F32), (LENGTH, LENGTH))
        acc[1, m, 0:LENGTH, 0:LENGTH] = jnp.where(across == across.T, 0.0, MASKED)
        tdy[owner(0, 0), pl.ds(m * LENGTH, LENGTH)] = dyv[m].astype(BF)
        return 0

    lax.fori_loop(0, MB, make_bias, 0)

    def tok_copy(q, n, m, dev, whose):
        ref = (tdy, tn2)[q].at[whose, pl.ds(m * LENGTH, LENGTH)]
        shared = S_OWN if q == 1 and n < 2 else S_TOK
        return remote(ref, ref, send.at[shared], tok_r.at[q, n, m], dev)

    def tok_sib(q, m):
        return tok_copy(q, 0, m, dev_sib, owner(0, 0))

    def tok_far(q, m):
        return tok_copy(q, 1, m, dev_z(1), owner(0, 0))

    def tok_fwd(q, m):
        return tok_copy(q, 2, m, dev_sib, owner(1, 0))

    for m in range(MB):
        tok_sib(0, m).start()

    ax(0).wait_recv()
    ad0(0).start()
    ay(0).wait_recv()
    ad1(0).start()
    az(1).wait_recv()
    ax(1).start()
    ay(1).start()
    for m in range(MB):
        tok_far(0, m).start()
    received(norm_r.at[0], nr2)
    for i in range(3):
        norm_two(i).start()
    for j in (2, 3):
        az(j).wait_recv()
        ax(j).start()
        ay(j).start()
    fz().start()
    for j in (1, 2, 3):
        ax(j).wait_recv()
        ad0(j).start()
        ay(j).wait_recv()
        ad1(j).start()
    gather_first(0)
    received(norm_r.at[1], nr1)

    vectors = None
    for cc in range(COLS):
        shard = jnp.concatenate([nbuf[:, cc, 0, :], jnp.zeros((ROWS, D - LANES), F32)], axis=1)
        shard = pltpu.roll(shard, cc * WIDTH, 1) if cc else shard
        vectors = shard if vectors is None else vectors + shard
    gain_one, shift_one, gain_two, shift_two = [vectors[i : i + 1] for i in range(4)]

    ld_x.wait()

    def first_norm(m, _):
        normal, _inv = ln_stats(ig[m])
        n1[m] = (normal * gain_one + shift_one).astype(BF)
        return 0

    lax.fori_loop(0, MB, first_norm, 0)

    for j in range(Z_SIZE):
        ad0(j).wait_recv()
        ad1(j).wait_recv()
        sib(j).start()
    for j in range(Z_SIZE):
        sib(j).wait_recv()

    gather_second(0)

    def project(i, _):
        rows = dot_nt(n1[...].reshape(MB * LENGTH, D), wall[i]).astype(BF)
        for m in range(MB):
            qkv[m, i] = rows[m * LENGTH : (m + 1) * LENGTH]
        return 0

    lax.fori_loop(0, 3, project, 0)

    lane_head = lax.broadcasted_iota(jnp.int32, (1, LANES), 1) // HD
    head_mask = [jnp.where(lane_head == h, 1.0, 0.0).astype(BF) for h in range(HEADS_TILE)]
    scale = HD ** (-0.5)
    log2_scale = scale * math.log2(math.e)

    def at_step(it, i, fn):
        @pl.when(it == i)
        def _():
            fn()

    def slot_lanes(it, first, size):
        return pl.ds(pl.multiple_of((it % 2) * LENGTH + first, LANES), size)

    def slot_of(it):
        return gb.at[:, pl.ds(LENGTH, LENGTH), slot_lanes(it, 0, LENGTH)]

    def save_probs(it):
        return pltpu.make_async_copy(slot_of(it), probs_hbm.at[it], pb_sem.at[it % 2])

    def load_probs(it, where):
        return pltpu.make_async_copy(probs_hbm.at[where], slot_of(it), pb_sem.at[2 + it % 2])

    def second_norm(m):
        hidden = ig[m] + dot_nt(obuf[m], wall[3])
        yout[m] = hidden
        normal, _inv = ln_stats(hidden)
        tn2[owner(0, 0), pl.ds(m * LENGTH, LENGTH)] = (normal * gain_two + shift_two).astype(BF)
        tok_far(1, m).start()
        tok_sib(1, m).start()

    def forward_group(it, _):
        m, g = it // GROUPS, it % GROUPS
        at_step(it, 1, lambda: gather_diag(0))

        @pl.when(it == 8)
        def _():
            fz().wait_recv()
            gather_first(1)
            gather_second(1)


        @pl.when(it >= 2)
        def _():
            save_probs(it - 2).wait()

        lanes = pl.ds(pl.multiple_of(g * LANES, LANES), LANES)
        q = qkv[m, 0, :, lanes]
        kk = qkv[m, 1, :, lanes]
        v = qkv[m, 2, :, lanes]
        v_turned = v.T
        for h in range(HEADS_TILE):
            scores = dot_nt(kk, q * head_mask[h])
            for part in range(LENGTH // LANES):
                cols = slice(part * LANES, (part + 1) * LANES)
                shifted = scores[:, cols] * log2_scale + acc[1, m, 0:LENGTH, cols]
                expo = jnp.exp2(shifted - jnp.max(shifted, axis=0, keepdims=True))
                total = jnp.sum(expo, axis=0, keepdims=True)
                gb[h, LENGTH : 2 * LENGTH, slot_lanes(it, part * LANES, LANES)] = (expo * (1.0 / total)).astype(BF)
        mixed = [dot_nn(v_turned[h * HD : (h + 1) * HD], gb[h, LENGTH : 2 * LENGTH, slot_lanes(it, 0, LENGTH)]) for h in range(HEADS_TILE)]
        obuf[m, :, lanes] = jnp.concatenate(mixed, axis=0).T.astype(BF)
        save_probs(it).start()

        @pl.when(g == GROUPS - 1)
        def _():
            second_norm(m)

        return 0

    lax.fori_loop(0, MB * GROUPS, forward_group, 0)
    save_probs(MB * GROUPS - 2).wait()
    save_probs(MB * GROUPS - 1).wait()
    for m in range(MB):
        tok_far(0, m).wait_recv()
        tok_fwd(0, m).start()

    def scatter_ops(block, r1, r1_both, r2, s_one, s_two, rs):
        def one(u, p, b):
            dev = dev_y if p == 0 else dev_x
            rr = rd if b == 1 else (ry if p == 0 else rx)
            return remote(block(rr, u, p), r1(u, p, b), send.at[s_one], rs.at[p, u], dev)

        def two(u, p):
            dev = dev_x if p == 0 else dev_y
            rr = rx if p == 0 else ry
            return remote(block(rr, u, p), r2(u, p), send.at[s_two], rs.at[2 + p, u], dev)

        def start_one(u, parts=(0, 1)):
            for p in parts:
                for b in (1, 0):
                    one(u, p, b).start()

        def start_two(u):
            for p in range(2):
                received(rs.at[p, u], r1_both(u, p))
                mine = block(rx if p == 0 else ry, u, p)
                mine[...] = (mine[...].astype(F32) + r1(u, p, 1)[...].astype(F32)).astype(BF)
                two(u, p).start()

        def own_sum(u, p):
            two(u, p).wait_recv()
            return (
                block(r, u, p)[...].astype(F32)
                + r1(u, p, 0)[...].astype(F32)
                + r2(u, p)[...].astype(F32)
            )

        return start_one, start_two, own_sum

    def unit_lanes(u):
        return pl.ds(UNITS[u][0], UNITS[u][1])

    f_one, f_two, f_sum = scatter_ops(
        lambda rr, u, p: fw.at[p, rr, :, unit_lanes(u)],
        lambda u, p, b: fr1.at[p, b, :, unit_lanes(u)],
        lambda u, p: fr1.at[p, :, :, unit_lanes(u)],
        lambda u, p: fr2.at[p, :, unit_lanes(u)],
        S_F_ONE, S_F_TWO, frs_r,
    )

    def f_far(u, p):
        lanes = pl.ds(UNITS[u][0] - D, UNITS[u][1])
        return remote(fw.at[p, r, :, unit_lanes(u)], fr3.at[p, :, lanes], send.at[S_F_FAR], frs_r.at[4 + p, u], dev_z(2))

    def f_three(u):
        for p in range(2):
            fw[p, r, :, unit_lanes(u)] = f_sum(u, p).astype(BF)
            f_far(u, p).start()

    def g_rows(zz, p, parity):
        start = (zz * 2 + parity) * WIDTH
        if p is None:
            return rows16(start, WIDTH)
        return rows16(start + PART_ROWS[0] * p, PART_ROWS[p])

    def part_rows(p):
        return pl.ds(PART_ROWS[0] * p, PART_ROWS[p])

    a_one, a_two, a_sum = scatter_ops(
        lambda rr, zz, p: wgrad.at[rr, g_rows(zz, p, k)],
        lambda zz, p, b: ar1.at[zz, b, part_rows(p)],
        lambda zz, p: ar1.at[zz, :, part_rows(p)],
        lambda zz, p: ar2.at[zz, part_rows(p)],
        S_A_ONE, S_A_TWO, ars_r,
    )

    def a_near(zz):
        return remote(wgrad.at[r, g_rows(zz, None, k)], ar3.at[zz // 2], send.at[S_A_NEAR], ars_r.at[4, zz // 2], dev_z(1))

    def a_far(zz):
        return remote(wgrad.at[r, g_rows(zz, None, k)], ar3.at[2], send.at[S_A_FAR], ars_r.at[4, 2], dev_z(2))

    def held(i):
        return acc.at[0, owner(1, 0), pl.ds(FEATURES + i * WIDTH, WIDTH)]

    agrad = held(2)

    def a_three(zz):
        total = [a_sum(zz, p) for p in range(2)]

        @pl.when(z % 2 == zz % 2)
        def _():
            for p in range(2):
                held(zz // 2)[part_rows(p)] = total[p]

        @pl.when(z % 2 != zz % 2)
        def _():
            for p in range(2):
                wgrad[r, g_rows(zz, p, k)] = total[p].astype(BF)
            a_near(zz).start()

    def a_four(half):
        zz = half * 2 + z % 2
        a_near(2 * half).wait_recv()
        total = held(half)[...] + ar3[half].astype(F32)

        @pl.when(z == zz)
        def _():
            agrad[...] = total

        @pl.when(z != zz)
        def _():
            wgrad[r, g_rows(zz, None, k)] = total.astype(BF)
            a_far(zz).start()

    def cross(zz):
        return remote(wgrad.at[:, g_rows(zz, None, 1 - k)], rc.at[zz], send.at[S_CROSS], rc_r.at[zz], dev_sib)

    def a_start(zz):
        cross(zz).wait_recv()
        for rr in range(ROWS):
            mine = wgrad.at[rr, g_rows(zz, None, k)]
            mine[...] = (mine[...].astype(F32) + rc[zz, rr].astype(F32)).astype(BF)
        a_one(zz)

    def ffn_tile(i, t, rows=slice(None)):
        first, width = CHUNKS[i]
        up = fw[0, :, :, first : first + width].reshape(D, width)
        down = fw[1, :, :, first : first + width].reshape(D, width)
        act, slope = gelu_pair(dot_nn(tn2[t, rows], up))
        grad_act = dot_nn(tdy[t, rows], down)
        act = act.astype(BF)
        grad_up = (grad_act * slope).astype(BF)
        gb[t, rows, first : first + width] = act
        dub[t, rows, first : first + width] = grad_up
        dn_part = dot_nt(grad_up, up)
        y_part = dot_nt(act, down)
        if i == 0:
            acc[0, t, rows] = dn_part
            acc[1, t, rows] = y_part
        else:
            acc[0, t, rows] += dn_part
            acc[1, t, rows] += y_part

    def token_sums(lanes, left, right, first_owner, owners):
        first, width = lanes
        rows = owners * MB * LENGTH
        span = pl.ds(first_owner, owners)
        return dot_tn(left[span].reshape(rows, D), right[span, :, first : first + width].reshape(rows, width))

    pairs = ((tn2, dub), (tdy, gb))

    def near_grads(unit):
        for p, (left, right) in enumerate(pairs):
            grad = token_sums(UNITS[unit], left, right, (z % 2) * 2, 2)
            wgrad[p, :, 0 : UNITS[unit][1]] = grad.astype(BF)

    def unit_grads(unit, held_near=False):
        first, width = UNITS[unit]
        for p, (left, right) in enumerate(pairs):
            if held_near:
                grad = wgrad[p, :, 0:width].astype(F32) + token_sums(UNITS[unit], left, right, (1 - z % 2) * 2, 2)
            else:
                grad = token_sums(UNITS[unit], left, right, 0, 4)
            fw[p, :, :, first : first + width] = grad.astype(BF).reshape(ROWS, FEATURES, width)

    gathered(0)

    def near_tiles(s, _):
        def sib_tiles():
            for q in range(2):
                for m in range(MB):
                    tok_sib(q, m).wait_recv()

        at_step(s, 1, sib_tiles)
        ffn_tile(0, owner(0, s))
        return 0

    lax.fori_loop(0, 2, near_tiles, 0)

    def far_tiles(s, _):
        m = s // 2
        for m_ in range(MB):

            def arrived(m_=m_):
                tok_far(1, m_).wait_recv()
                tok_fwd(1, m_).start()

            def forwarded(m_=m_):
                for q in range(2):
                    tok_fwd(q, m_).wait_recv()

            if m_ == 1:
                at_step(s, 2, lambda: gather_diag(1))
                at_step(s, 2, lambda: near_grads(0))
            at_step(s, 2 * m_, arrived)
            at_step(s, 2 * m_ + 1, forwarded)
        ffn_tile(0, owner(1, s % 2), pl.ds(pl.multiple_of(m * LENGTH, LENGTH), LENGTH))
        return 0

    lax.fori_loop(0, 2 * MB, far_tiles, 0)
    fz().wait_send()
    gather_sent(0)
    gathered(1)

    def part_sib(q, n):
        return remote(acc.at[q, owner(n, 1)], near.at[q, n], send.at[S_PART], part_r.at[q, n], dev_sib)

    def stage_of(q, m):
        return stage.at[m] if q else wgrad.at[2, pl.ds(m * LENGTH, LENGTH)]

    def part_far(q, m):
        return remote(stage_of(q, m), far.at[q, m], send.at[(S_FAR_DN, S_FAR)[q]], part_r.at[q, 2 + m], dev_z(1))

    def to_far(q):
        part_sib(q, 1).wait_recv()
        for m in range(MB):
            rows = pl.ds(m * LENGTH, LENGTH)
            stage_of(q, m)[...] = (acc[q, owner(1, 0), rows] + near[q, 1, rows]).astype(BF)
            part_far(q, m).start()

    def second_block(s, _):
        ffn_tile(1, owner(1 - s // 2, 1 - s % 2))
        for n in range(2):

            def to_sib(n=n):
                part_sib(0, n).start()
                part_sib(1, n).start()

            at_step(s, 2 * (1 - n), to_sib)
        at_step(s, 1, lambda: to_far(0))

        @pl.when(s == 1)
        def _():
            unit_grads(0, held_near=True)
            f_one(0)

        at_step(s, 3, lambda: to_far(1))
        return 0

    lax.fori_loop(0, 4, second_block, 0)
    gather_sent(1)
    unit_grads(2)
    f_one(2)
    unit_grads(3)
    f_one(3)
    unit_grads(4)

    zero = jnp.zeros((1, D), F32)
    part_sib(0, 0).wait_recv()

    def whole(q, m):
        rows = pl.ds(m * LENGTH, LENGTH)
        return acc[q, owner(0, 0), rows] + near[q, 0, rows] + far[q, m].astype(F32)

    def second_backward(m):
        part_far(0, m).wait_recv()
        normal, inv = ln_stats(yout[m])
        grad = whole(0, m)
        grad_hidden = dyv[m] + ln_backward(normal, inv, gain_two, grad)
        dyv[m] = grad_hidden
        low = grad_hidden.astype(BF)
        dub[m, 0:LENGTH, D : 2 * D] = dot_nn(low, wall[3]).astype(BF)
        dub[2 + m, 0:LENGTH, D : 2 * D] = low
        nsum[pl.ds(2, 1)] += jnp.sum(grad * normal, axis=0, keepdims=True)
        nsum[pl.ds(3, 1)] += jnp.sum(grad, axis=0, keepdims=True)

    nsum[...] = jnp.zeros(nsum.shape, F32)
    load_probs(0, 0).start()
    second_backward(0)

    def first_backward(m):
        grad = dot_nn(qkv[m, 0], wall[0]) + dot_nn(qkv[m, 1], wall[1]) + dot_nn(qkv[m, 2], wall[2])
        normal, inv = ln_stats(ig[m])
        ig[m] = dyv[m] + ln_backward(normal, inv, gain_one, grad)
        nsum[pl.ds(0, 1)] += jnp.sum(grad * normal, axis=0, keepdims=True)
        nsum[pl.ds(1, 1)] += jnp.sum(grad, axis=0, keepdims=True)

    def backward_at(it):
        m = jnp.where(it < 6, it // 3, it % 2)
        g = jnp.where(it < 6, it % 3, it // 2)
        return m, g

    def group_grads(g):
        lanes = pl.ds(pl.multiple_of(g * LANES, LANES), LANES)
        for p in range(3):
            grad = dot_tn(qkv[0, p, :, lanes], n1[0]) + dot_tn(qkv[1, p, :, lanes], n1[1])
            wgrad[p, lanes] = grad.astype(BF)

    def backward_group(it, _):
        m, g = backward_at(it)

        at_step(it, 2, lambda: f_two(2))
        at_step(it, 2, lambda: f_one(4))

        @pl.when(it == 3)
        def _():
            second_backward(1)
            sent(S_FAR_DN, wgrad.at[2, pl.ds(0, MB * LENGTH)])
            rows = [dub[2 + i, 0:LENGTH, D : 2 * D] for i in range(MB)]
            wgrad[3] = (dot_tn(rows[0], obuf[0]) + dot_tn(rows[1], obuf[1])).astype(BF)

        at_step(it, 3, lambda: f_two(3))
        at_step(it, 4, lambda: f_three(2))
        at_step(it, 5, lambda: f_two(4))
        at_step(it, 5, lambda: f_three(3))
        at_step(it, 6, lambda: a_start(0))
        at_step(it, 7, lambda: f_three(4))
        at_step(it, 7, lambda: a_start(1))
        at_step(it, 9, lambda: a_start(2))
        at_step(it, 9, lambda: a_two(0))

        @pl.when(it + 1 < MB * GROUPS)
        def _():
            m_next, g_next = backward_at(it + 1)
            load_probs(it + 1, m_next * GROUPS + g_next).start()

        load_probs(it, m * GROUPS + g).wait()
        lanes = pl.ds(pl.multiple_of(g * LANES, LANES), LANES)
        q = qkv[m, 0, :, lanes]
        kk = qkv[m, 1, :, lanes]
        v = qkv[m, 2, :, lanes]
        do = dub[m, 0:LENGTH, pl.ds(pl.multiple_of(D + g * LANES, LANES), LANES)]
        k_turned = kk.T
        for h in range(HEADS_TILE):
            do_head = do * head_mask[h]
            for part in range(LENGTH // LANES):
                cols = slice(part * LANES, (part + 1) * LANES)
                wide = gb[h, LENGTH : 2 * LENGTH, slot_lanes(it, part * LANES, LANES)].astype(F32)
                product = dot_nt(v, do_head[cols]) * wide
                total = jnp.sum(product, axis=0, keepdims=True)
                gb[h, 0:LENGTH, cols] = (product - wide * total).astype(BF)
        grad_q, grad_k, grad_v = [], None, None
        for h in range(HEADS_TILE):
            v_part = dot_nn(gb[h, LENGTH : 2 * LENGTH, slot_lanes(it, 0, LENGTH)], do * head_mask[h])
            k_part = dot_nn(gb[h, 0:LENGTH, 0:LENGTH], q * head_mask[h])
            grad_v = v_part if grad_v is None else grad_v + v_part
            grad_k = k_part if grad_k is None else grad_k + k_part
            grad_q.append(dot_nn(k_turned[h * HD : (h + 1) * HD], gb[h, 0:LENGTH, 0:LENGTH]))
        qkv[m, 0, :, lanes] = (jnp.concatenate(grad_q, axis=0).T * scale).astype(BF)
        qkv[m, 1, :, lanes] = (grad_k * scale).astype(BF)
        qkv[m, 2, :, lanes] = grad_v.astype(BF)

        @pl.when(m == 1)
        def _():
            group_grads(g)

        at_step(it, 4, lambda: cross(0).start())
        at_step(it, 5, lambda: cross(1).start())
        at_step(it, 7, lambda: cross(2).start())
        at_step(it, 9, lambda: cross(3).start())
        return 0

    lax.fori_loop(0, MB * GROUPS, backward_group, 0)

    def put(i, src, dst):
        return pltpu.make_async_copy(src, dst, out_sem.at[i])

    def put_ffn(p):
        return put(4 + p, acc.at[p, owner(1, 0), pl.ds(0, FEATURES)], fgrad_hbm.at[p])

    first_backward(0)
    a_start(3)
    unit_grads(1)
    a_two(1)
    a_two(2)
    first_backward(1)
    for m in range(MB):
        put(m, ig.at[m], ig_hbm.at[m]).start()

    sums = nsum[...]
    lane_own = lax.broadcasted_iota(jnp.int32, (8, LANES), 1) < WIDTH
    for cc in range(COLS):
        shard = pltpu.roll(sums, D - cc * WIDTH, 1) if cc else sums
        shard = jnp.where(lane_own, shard[:, 0:LANES], 0.0)
        for rr in range(ROWS):
            ngrad[rr, cc] = shard[rr : rr + 1]

    def grad_rows(i):
        rr = (rx, ry, rd)[i]
        return remote(ngrad.at[rr], nr1.at[i], send.at[S_G_ONE], norm_r.at[2], (dev_x, dev_y, dev_d)[i])

    def grad_cols(j):
        col = zat(j // 2) * 2 + (k + j % 2) % 2
        return remote(ngrad.at[r, col], nr2.at[j - 1], send.at[S_G_TWO], norm_r.at[3], dev_row(j))

    for i in range(3):
        grad_rows(i).start()
    a_three(0)
    part_sib(1, 0).wait_recv()
    for m in range(MB):
        part_far(1, m).wait_recv()
        yout[m] = yout[m] + whole(1, m)
        put(2 + m, yout.at[m], yout_hbm.at[m]).start()
    a_two(3)
    f_one(1)
    f_two(0)
    a_three(1)
    a_three(2)
    a_three(3)
    received(norm_r.at[2], nr1)
    ngrad[r] = ngrad[r] + nr1[0] + nr1[1] + nr1[2]
    for j in range(1, COLS):
        grad_cols(j).start()
    a_four(0)
    f_two(1)
    a_four(1)
    for u in range(2):
        for p in range(2):
            acc[p, owner(1, 0), 0:FEATURES, unit_lanes(u)] = f_sum(u, p)

    sent(S_GATHER, wall.at[pl.ds(0, 3), pl.ds(0, 5 * WIDTH)])
    sent(S_SIB, wall.at[pl.ds(0, 2)])
    sent(S_TOK, tdy)
    sent(S_OWN, tn2.at[pl.ds(0, 2)])
    sent(S_PART, acc.at[0])
    sent(S_FAR, stage)
    sent(S_F_ONE, fw.at[0])
    sent(S_F_TWO, fr2)
    sent(S_A_ONE, wgrad.at[0])
    sent(S_A_TWO, ar2)
    sent(S_CROSS, rc)
    sent(S_N_ONE, nr2)
    sent(S_N_TWO, nr1)
    sent(S_G_ONE, nr1)

    for u in FAR_UNITS:
        lanes = pl.ds(UNITS[u][0] - D, UNITS[u][1])
        for p in range(2):
            f_far(u, p).wait_recv()
            acc[p, owner(1, 0), 0:FEATURES, lanes] += fr3[p, :, lanes].astype(F32)
    for p in range(2):
        put_ffn(p).start()
    received(norm_r.at[3], nr2)
    total = ngrad[r, c]
    for j in range(COLS - 1):
        total = total + nr2[j]
    nout[...] = total
    put(7, nout, nout_hbm).start()
    a_far(z).wait_recv()
    agrad[...] = agrad[...] + ar3[2].astype(F32)
    put(6, agrad, agrad_hbm).start()

    sent(S_G_TWO, nr2)
    sent(S_F_FAR, fr3)
    sent(S_A_NEAR, ar3.at[pl.ds(0, 2)])
    sent(S_A_FAR, ar3.at[2])
    for m in range(MB):
        put(m, ig.at[m], ig_hbm.at[m]).wait()
        put(2 + m, yout.at[m], yout_hbm.at[m]).wait()
    for p in range(2):
        put_ffn(p).wait()
    put(6, agrad, agrad_hbm).wait()
    put(7, nout, nout_hbm).wait()


def run_step(x, dy, ids, attn_w, norm_w, ffn_w):
    vm = pltpu.VMEM
    dma = pltpu.SemaphoreType.DMA
    any_spec = pl.BlockSpec(memory_space=pl.ANY)
    vspec = pl.BlockSpec(memory_space=pltpu.VMEM)
    tokens = MB * LENGTH
    return pl.pallas_call(
        step_kernel,
        out_shape=(
            jax.ShapeDtypeStruct((MB, LENGTH, D), F32),
            jax.ShapeDtypeStruct((MB, LENGTH, D), F32),
            jax.ShapeDtypeStruct((2, FEATURES, D), F32),
            jax.ShapeDtypeStruct((WIDTH, D), F32),
            jax.ShapeDtypeStruct((1, LANES), F32),
            jax.ShapeDtypeStruct((MB * GROUPS, HEADS_TILE, LENGTH, LENGTH), BF),
        ),
        in_specs=[any_spec] * 6,
        out_specs=(any_spec,) * 6,
        scratch_shapes=[
            vm((ROWS, D, D), BF),
            vm((ROWS, D, D), BF),
            vm((2, ROWS, FEATURES, 2 * D), BF),
            vm((MB, LENGTH, D), BF),
            vm((MB, 3, LENGTH, D), BF),
            vm((MB, LENGTH, D), BF),
            vm((4, tokens, D), BF),
            vm((4, tokens, D), BF),
            vm((4, tokens, 2 * D), BF),
            vm((4, tokens, 2 * D), BF),
            vm((2, 4, tokens, D), F32),
            vm((2, 2, tokens, D), F32),
            vm((MB, LENGTH, D), BF),
            vm((2, MB, LENGTH, D), BF),
            vm((MB, LENGTH, D), F32),
            vm((2, 2, FEATURES, 2 * D), BF),
            vm((2, FEATURES, 2 * D), BF),
            vm((2, FEATURES, D), BF),
            vm((Z_SIZE, ROWS, WIDTH, D), BF),
            vm((Z_SIZE, 2, WIDTH, D), BF),
            vm((Z_SIZE, WIDTH, D), BF),
            vm((Z_SIZE - 1, WIDTH, D), BF),
            vm((ROWS, COLS, 1, LANES), F32),
            vm((ROWS, COLS, 1, LANES), F32),
            vm((8, D), F32),
            vm((3, COLS, 1, LANES), F32),
            vm((COLS - 1, 1, LANES), F32),
            vm((MB, LENGTH, D), F32),
            vm((MB, LENGTH, D), F32),
            vm((MB, LENGTH), jnp.int32),
            vm((1, WIDTH), F32),
            vm((1, LANES), F32),
            dma((7,)), dma((4,)), dma((8,)),
            dma((19,)),
            dma((3,)),
            dma((5, Z_SIZE)),
            dma((7, 2)),
            dma((Z_SIZE,)),
            dma((2, 3, MB)),
            dma((2, 4)),
            dma((6, len(UNITS))),
            dma((5, Z_SIZE)),
            dma((Z_SIZE,)),
            dma((4,)),
        ],
        compiler_params=pltpu.CompilerParams(
            collective_id=0, has_side_effects=True, vmem_limit_bytes=64 * 1024 * 1024 - 4096
        ),
        name="encoder_step",
    )(x, dy, ffn_w, ids, attn_w, norm_w)


def update_kernel(rate, *refs):
    y_in, g_in, a_in, n_in, f_in = refs[0], refs[1], refs[2:6], refs[6:10], refs[10:14]
    y_out, g_out, a_out, n_out, f_out = refs[14], refs[15], refs[16:21], refs[21:26], refs[26:31]
    yb, gbuf, a_held, f_held, a_low, f_low, in_sem, out_sem = refs[31:]

    def load(i, src, dst):
        return pltpu.make_async_copy(src, dst, in_sem.at[i])

    def save(i, src, dst):
        return pltpu.make_async_copy(src, dst, out_sem.at[i])

    pieces = []
    for s in range(2):
        pieces.append(([v.at[s] for v in f_in], [v.at[s] for v in f_out], f_held.at[s], f_low.at[s]))
    pieces.append((list(a_in), list(a_out), a_held, a_low))
    loads = [
        [load(4 * n + i, src[i], held.at[i]) for i in range(4)]
        for n, (src, dst, held, low) in enumerate(pieces)
    ]
    through = [(load(12, y_in, yb), save(15, yb, y_out)), (load(13, g_in, gbuf), save(16, gbuf, g_out))]
    for copies in loads:
        for copy in copies:
            copy.start()
    for first, _second in through:
        first.start()

    def update(weights, moment, average, grad):
        moment_new = MOMENT_DECAY * moment + grad
        weights_new = weights - rate * (grad + MOMENT_DECAY * moment_new)
        average_new = AVERAGE_DECAY * average + (1.0 - AVERAGE_DECAY) * weights_new
        return moment_new, weights_new, average_new

    grad = n_in[3][:, 0:WIDTH]
    moment, weights, average = update(n_in[0][...], n_in[1][...], n_in[2][...], grad)
    for ref, value in zip(n_out, (grad, moment, weights, average, weights.astype(BF))):
        ref[...] = value

    saves = []
    for n, (src, dst, held, low) in enumerate(pieces):
        for copy in loads[n]:
            copy.wait()
        moment, weights, average = update(held[0], held[1], held[2], held[3])
        held[0] = weights
        held[1] = moment
        held[2] = average
        low[...] = weights.astype(BF)
        for i, value in enumerate((held.at[3], held.at[1], held.at[0], held.at[2], low)):
            saves.append(save(5 * n + i, value, dst[i]))
            saves[-1].start()
    for i, (first, second) in enumerate(through):
        first.wait()
        second.start()
    for copy in saves:
        copy.wait()
    for _first, second in through:
        second.wait()


def run_update(rate, carried, attn, norm, ffn):
    vm = pltpu.VMEM
    any_spec = pl.BlockSpec(memory_space=pltpu.HBM)
    vspec = pl.BlockSpec(memory_space=pltpu.VMEM)
    five = lambda like: [jax.ShapeDtypeStruct(like.shape, F32)] * 4 + [jax.ShapeDtypeStruct(like.shape, BF)]
    out = pl.pallas_call(
        functools.partial(update_kernel, rate),
        out_shape=[jax.ShapeDtypeStruct(v.shape, F32) for v in carried] + five(attn[0]) + five(norm[0]) + five(ffn[0]),
        in_specs=[any_spec] * 6 + [vspec] * 4 + [any_spec] * 4,
        out_specs=[any_spec] * 7 + [vspec] * 5 + [any_spec] * 5,
        scratch_shapes=[
            vm(carried[0].shape, F32),
            vm(carried[1].shape, F32),
            vm((4, *attn[0].shape), F32),
            vm((2, 4, *ffn[0].shape[1:]), F32),
            vm(attn[0].shape, BF),
            vm(ffn[0].shape, BF),
            pltpu.SemaphoreType.DMA((14,)),
            pltpu.SemaphoreType.DMA((17,)),
        ],
        compiler_params=pltpu.CompilerParams(vmem_limit_bytes=64 * 1024 * 1024 - 4096),
        name="update",
    )(*carried, *attn, *norm, *ffn)
    return out[0], out[1], out[2:7], out[7:12], out[12:17]


def local_slice(
    block_input, output_grad, sequence_ids,
    attn_weights, attn_momentum, attn_average,
    norm_params, norm_momentum, norm_average,
    ffn_weights, ffn_momentum, ffn_average,
):
    outputs, grads, ffn_grad, shard, norm_shard, _probs = run_step(
        block_input, output_grad, sequence_ids, attn_weights.T, norm_params[None], ffn_weights
    )
    total_tokens = MB * block_input.shape[1] * lax.axis_size("row") * lax.axis_size("col")
    step_rate = RATE_SCALE * total_tokens ** (-0.5)
    outputs, grads, attn, norm, ffn = run_update(
        step_rate,
        (outputs, grads),
        (attn_weights.T, attn_momentum.T, attn_average.T, shard),
        (norm_params[None], norm_momentum[None], norm_average[None], norm_shard),
        (ffn_weights, ffn_momentum, ffn_average, ffn_grad),
    )
    return (outputs, grads, *[v.T for v in attn], *[v[0] for v in norm], *ffn)


def local(*args):
    on_slice = (
        lax.axis_size("row") == ROWS
        and lax.axis_size("col") == COLS
        and args[0].shape[1] == LENGTH
        and args[3].shape == (D, WIDTH)
        and args[9].shape == (2, FEATURES, D)
    )
    return (local_slice if on_slice else local_general)(*args)


def solution(mesh):
    return jax.shard_map(
        local,
        mesh=mesh,
        in_specs=(
            P(None, ("row", "col"), None),
            P(None, ("row", "col"), None),
            P(None, ("row", "col")),
            P(None, ("row", "col")),
            P(None, ("row", "col")),
            P(None, ("row", "col")),
            P(("row", "col")),
            P(("row", "col")),
            P(("row", "col")),
            P(None, "row", "col"),
            P(None, "row", "col"),
            P(None, "row", "col"),
        ),
        out_specs=(
            P(None, ("row", "col"), None),
            P(None, ("row", "col"), None),
            P(None, ("row", "col")),
            P(None, ("row", "col")),
            P(None, ("row", "col")),
            P(None, ("row", "col")),
            P(None, ("row", "col")),
            P(("row", "col")),
            P(("row", "col")),
            P(("row", "col")),
            P(("row", "col")),
            P(("row", "col")),
            P(None, "row", "col"),
            P(None, "row", "col"),
            P(None, "row", "col"),
            P(None, "row", "col"),
            P(None, "row", "col"),
        ),
        check_vma=False,
    )
```
